32 devices in a mesh: dp: 8 (over z, x), seq: 4 (over y, core).
Axes of the slice: x: 2, y: 2, z: 4, core: 2. Of those that a mesh axis runs over, the one named last changes fastest.
Arguments:
- latents: bfloat16 [8, 32, 32, 1152], P('dp', 'seq'), may hold values from -6 to 6
- text: bfloat16 [8, 300, 1152], P('dp'), may hold values from -6 to 6
- time_embed: float32 [8, 6912], P('dp'), may hold values from -2 to 2
- cotangent: bfloat16 [8, 32, 32, 1152], P('dp', 'seq'), may hold values from -6 to 6
- params: float32 [4, 5160960], P('seq', 'dp'), may hold values from -1.5 to 1.5, as said below
- moment_one: float32 [4, 5160960], P('seq', 'dp'), may hold values from -2 to 2
- moment_two: float32 [4, 5160960], P('seq', 'dp'), may hold values from 0.05 to 2
Outputs:
- output: bfloat16 [8, 32, 32, 1152], P('dp', 'seq')
- grad_input: float32 [8, 32, 32, 1152], P('dp', 'seq')
- gradient: float32 [4, 5160960], P('seq', 'dp')
- moment_one_new: float32 [4, 5160960], P('seq', 'dp')
- moment_two_new: float32 [4, 5160960], P('seq', 'dp')
- update: float32 [4, 5160960], P('seq', 'dp')
- bias_grads: float32 [4, 3744], P('seq')
The draws below stay inside these ranges and needn't reach their ends.
Inputs may be any that keep to these rules, and one draw needn't show every extreme that they name: `params`: the grid holds the block's parameters in the layout of the first step.
All inputs are finite; a program needn't handle non-finite values.
Results may differ from the reference program's by a relative error of at most 0.02.
Values may be sent and summed in bfloat16 or wider, within the bound.
A program may use at most 256 MiB of HBM per device.

```python
import math
import jax
import jax.numpy as jnp
from jax import lax

D = 1152
FF = 2880
CROSS_HEADS = 16
TXT = 300
HH = 32
WW = 32
LATENTS = 8
SEGMENTS = 4
NPARAM = 20643840


def draw_params(key, part):
    sections = [(6, D, 0.3), (D, 3 * D, D ** (-0.5)), (D, D, 2.0 * D ** (-0.5)), (1, D, 0.3), (D, D, D ** (-0.5)), (D, 2 * D, D ** (-0.5)), (D, D, 4.0 * D ** (-0.5)), (1, D, 0.3), (D, 2 * FF, D ** (-0.5)), (1, 2 * FF, 0.5), (9, 2 * FF, 1.0 / 3.0), (1, 2 * FF, 0.3), (FF, D, 3.0 * FF ** (-0.5)), (1, D, 0.3)]
    pieces = []
    for number, (rows_of, cols_of, spread) in enumerate(sections):
        sub_key = jax.random.fold_in(key, number + 11)
        sample = jax.random.truncated_normal(sub_key, -3.0, 3.0, (rows_of, cols_of), jnp.float32)
        block = (sample * spread).reshape(rows_of, SEGMENTS, cols_of // SEGMENTS).transpose(1, 0, 2)
        pieces.append(block.reshape(SEGMENTS, -1))
    return jnp.concatenate(pieces, axis=1)


def block_scale(own_key, extent, split, smallest, top_value):
    level, own = 1.0, jax.random.fold_in(own_key, 6)
    for position, blocks in split:
        heights = jnp.exp(jax.random.uniform(jax.random.fold_in(own, position), (blocks,), jnp.float32, smallest / len(split), top_value / len(split)))
        level = level * jnp.repeat(heights, extent[position] // blocks).reshape([-1 if axis == position else 1 for axis in range(len(extent))])
    return level


def normal_values(own_key, extent, deviation, reach, shards=(), kind=jnp.bfloat16):
    array = deviation * jax.random.normal(own_key, extent, jnp.float32)
    if shards:
        array = array * block_scale(own_key, extent, shards, -0.22, 0.18)
    return jnp.clip(array, -reach, reach).astype(kind)


def setup_inputs(seed: int = 0) -> dict:
    streams_of = jax.random.split(jax.random.key(seed), 8)
    latents = normal_values(streams_of[0], (LATENTS, HH, WW, D), 1.0, 6.0, ((0, 8), (1, 4)))
    text = normal_values(streams_of[1], (LATENTS, TXT, D), 1.0, 6.0, ((0, 8),))
    time_embed = normal_values(streams_of[2], (LATENTS, 6 * D), 0.3, 2.0, ((0, 8),), jnp.float32)
    cotangent = normal_values(streams_of[3], (LATENTS, HH, WW, D), 1.0, 6.0, ((0, 8), (1, 4)))
    params = draw_params(jax.random.fold_in(streams_of[7], 71), 0)
    moment_one = normal_values(streams_of[5], (SEGMENTS, NPARAM // SEGMENTS), 0.3, 2.0, ((0, 4), (1, 8)), jnp.float32)
    moment_two = jnp.clip(jnp.exp(math.log(2.0) - 3.6888794 * jax.random.uniform(streams_of[6], (SEGMENTS, NPARAM // SEGMENTS), jnp.float32) ** block_scale(streams_of[6], (SEGMENTS, NPARAM // SEGMENTS), ((0, 4), (1, 8)), -0.2, 0.2)), 0.05, 2.0)
    return dict(latents=latents, text=text, time_embed=time_embed, cotangent=cotangent, params=params, moment_one=moment_one, moment_two=moment_two)


@jax.custom_vjp
def low(v):
    return lax.optimization_barrier(v.astype(jnp.bfloat16)).astype(jnp.float32)

@jax.custom_vjp
def low_back(v):
    return v

def low_keep(v):
    return (low(v), None)

def low_pass(kept, grad):
    return (grad,)

def back_keep(v):
    return (v, None)

def back_low(kept, grad):
    return (low(grad),)
low.defvjp(low_keep, low_pass)
low_back.defvjp(back_keep, back_low)
precise = lax.Precision.HIGHEST
eps_norm = 1e-06
eps_linear = 1e-06
beta_first = 0.9
beta_second = 0.95
adam_eps = 1e-08
learn_rate = 0.0001
weight_decay = 0.01
adam_steps = 100.0

def piece_specs():
    return [(6, D, False), (D, 3 * D, False), (D, D, False), (1, D, True), (D, D, False), (D, 2 * D, False), (D, D, False), (1, D, True), (D, 2 * FF, False), (1, 2 * FF, True), (9, 2 * FF, False), (1, 2 * FF, True), (FF, D, False), (1, D, True)]

def unpack(grid):
    pieces = []
    offset = 0
    for rows_of, cols_of, vector in piece_specs():
        length = rows_of * cols_of // SEGMENTS
        block = grid[:, offset:offset + length].reshape(SEGMENTS, rows_of, cols_of // SEGMENTS)
        block = block.transpose(1, 0, 2).reshape(rows_of, cols_of)
        pieces.append(block.reshape(cols_of) if vector else block)
        offset = offset + length
    return pieces

def bias_columns(grid):
    blocks = []
    offset = 0
    for rows_of, cols_of, vector in piece_specs():
        length = rows_of * cols_of // SEGMENTS
        if vector:
            blocks.append(grid[:, offset:offset + length])
        offset = offset + length
    return jnp.concatenate(blocks, axis=1)

def layer_norm(values):
    centred = values - lax.optimization_barrier(jnp.mean(values, axis=-1, keepdims=True))
    variance = lax.optimization_barrier(jnp.mean(centred * centred, axis=-1, keepdims=True))
    return centred * lax.rsqrt(variance + eps_norm)

def rounded(values):
    return low(low_back(values))

def forward(picture, text_rows, time_rows, weights):
    mod_table, w_qkv, w_attn_out, b_attn_out, w_cross_q, w_cross_kv, w_cross_out, b_cross_out, w_in, b_in, w_depth, b_depth, w_point, b_point = unpack(weights)
    modulation = mod_table + time_rows.reshape(6, D)
    tokens = picture.reshape(HH * WW, D)
    heads_lin = D // 32
    hidden_one = low(layer_norm(tokens) * (1.0 + modulation[1]) + modulation[0])
    projected = low_back(jnp.dot(hidden_one, w_qkv, precision=precise))
    queries = low(jax.nn.relu(projected[:, :D])).reshape(-1, heads_lin, 32)
    keys_lin = low(jax.nn.relu(projected[:, D:2 * D])).reshape(-1, heads_lin, 32)
    values_lin = low(projected[:, 2 * D:]).reshape(-1, heads_lin, 32)
    kv_state = jnp.einsum('rhd,rhe->hde', keys_lin, values_lin, precision=precise)
    key_sum = lax.optimization_barrier(jnp.sum(keys_lin, axis=0))
    numerator = jnp.einsum('rhd,hde->rhe', queries, kv_state, precision=precise)
    denominator = jnp.einsum('rhd,hd->rh', queries, key_sum, precision=precise) + eps_linear
    attended = low((numerator / denominator[:, :, None]).reshape(-1, D))
    branch_one = low_back(jnp.dot(attended, w_attn_out, precision=precise) + b_attn_out)
    after_attn = tokens + modulation[2] * branch_one
    cross_dim = D // CROSS_HEADS
    score_scale = 1.0 / math.sqrt(cross_dim)
    query_c = rounded(jnp.dot(low(after_attn), w_cross_q, precision=precise)).reshape(-1, CROSS_HEADS, cross_dim)
    keyval = rounded(jnp.dot(text_rows, w_cross_kv, precision=precise))
    keys_c = keyval[:, :D].reshape(-1, CROSS_HEADS, cross_dim)
    values_c = keyval[:, D:].reshape(-1, CROSS_HEADS, cross_dim)
    scores = low_back(jnp.einsum('rhc,thc->hrt', query_c, keys_c, precision=precise) * score_scale)
    probs = low(jax.nn.softmax(scores, axis=-1))
    cross_mixed = rounded(jnp.einsum('hrt,thc->rhc', probs, values_c, precision=precise).reshape(-1, D))
    branch_cross = low_back(jnp.dot(cross_mixed, w_cross_out, precision=precise) + b_cross_out)
    after_cross = after_attn + branch_cross
    hidden_two = low(layer_norm(after_cross) * (1.0 + modulation[4]) + modulation[3])
    inner_pre = low_back(jnp.dot(hidden_two, w_in, precision=precise) + b_in)
    active = low(jax.nn.silu(inner_pre)).reshape(HH, WW, 2 * FF)
    padded = jnp.pad(active, ((1, 1), (1, 1), (0, 0)))
    conv_out = jnp.zeros((HH, WW, 2 * FF), jnp.float32) + b_depth
    for tap_row in range(3):
        for tap_col in range(3):
            conv_out = conv_out + w_depth[tap_row * 3 + tap_col] * padded[tap_row:tap_row + HH, tap_col:tap_col + WW]
    conv_out = low_back(conv_out).reshape(HH * WW, 2 * FF)
    gated_mix = low(conv_out[:, :FF] * jax.nn.silu(conv_out[:, FF:]))
    branch_two = low_back(jnp.dot(gated_mix, w_point, precision=precise) + b_point)
    result = after_cross + modulation[5] * branch_two
    return result.reshape(HH, WW, D)

def reference(latents, text, time_embed, cotangent, params, moment_one, moment_two):

    def one_latent(running, scanned):
        picture, text_rows, time_rows, cot_rows = scanned
        text_float = text_rows.astype(jnp.float32)

        def apply_block(image_in, grid_in):
            return forward(image_in, text_float, time_rows, low(grid_in))
        result, pullback = jax.vjp(apply_block, picture.astype(jnp.float32), params)
        grad_picture, grad_grid = pullback(cot_rows.astype(jnp.float32))
        return (running + grad_grid, (result.astype(jnp.bfloat16), grad_picture))
    summed, (output, grad_input) = lax.scan(one_latent, jnp.zeros(params.shape, jnp.float32), (latents, text, time_embed, cotangent))
    gradient = summed * lax.rsqrt(jnp.mean(summed * summed) + 1e-06)
    bias_grads = bias_columns(gradient)
    moment_one_new = beta_first * moment_one + (1.0 - beta_first) * gradient
    moment_two_new = beta_second * moment_two + (1.0 - beta_second) * gradient * gradient
    first_hat = moment_one_new / (1.0 - beta_first ** adam_steps)
    second_hat = moment_two_new / (1.0 - beta_second ** adam_steps)
    update = first_hat / (jnp.sqrt(second_hat) + adam_eps) + weight_decay * params
    return (output, grad_input, gradient, moment_one_new, moment_two_new, update, bias_grads)
```

```python
import math

import jax
import jax.numpy as jnp
from jax import lax
from jax.experimental import pallas as pl
from jax.experimental.pallas import tpu as pltpu
from jax.sharding import PartitionSpec as P

D = 1152
FF = 2880
CROSS_HEADS = 16


precise = lax.Precision.HIGHEST
eps_norm = 1e-06
eps_linear = 1e-06
beta_first = 0.9
beta_second = 0.95
adam_eps = 1e-08
weight_decay = 0.01
adam_steps = 100.0


def with_halo(block, sides, width):
    for axis, dim in sides:
        count = lax.axis_size(axis)
        forward = [(i, i + 1) for i in range(count - 1)]
        backward = [(target, source) for source, target in forward]
        low = lax.ppermute(
            lax.slice_in_dim(block, block.shape[dim] - width, None, axis=dim), axis, forward
        )
        high = lax.ppermute(lax.slice_in_dim(block, 0, width, axis=dim), axis, backward)
        block = jnp.concatenate([low, block, high], axis=dim)
    return block


def piece_specs():
    return [
        (6, D, False),
        (D, 3 * D, False),
        (D, D, False),
        (1, D, True),
        (D, D, False),
        (D, 2 * D, False),
        (D, D, False),
        (1, D, True),
        (D, 2 * FF, False),
        (1, 2 * FF, True),
        (9, 2 * FF, False),
        (1, 2 * FF, True),
        (FF, D, False),
        (1, D, True),
    ]


LANE = 128
UNIT = 32


def merge_units(values, lane_unit):
    out = values[0]
    last = values[0]
    for position in range(1, 4):
        if values[position] is not last:
            out = jnp.where(lane_unit >= position, values[position], out)
            last = values[position]
    return out


def rolled(value, units):
    units = units % 4
    return value if units == 0 else pltpu.roll(value, units * UNIT, 1)


def matrix_rows(count_rows):
    return 192 if count_rows % 192 == 0 else 64


def read_matrix(flat, offset, rows_of, cols_of, segs):
    total_rows = flat.shape[1]
    per_row = cols_of // segs // UNIT
    unit_at = offset // UNIT
    block = matrix_rows(rows_of)
    base = unit_at // 4 // 16 * 16
    shift = unit_at - 4 * base
    step = block * per_row // 4
    need = (shift + block * per_row - 1) // 4 + 1
    need = -(-need // 16) * 16
    assert base + (rows_of // block - 1) * step + need <= total_rows
    tiles = cols_of // LANE

    def kernel(in_ref, out_ref, wide, mixed):
        def widen(at, _):
            row = pl.multiple_of(at * 16, 16)
            for seg in range(segs):
                wide[pl.ds(pl.multiple_of(seg * need + row, 16), 16), :] = in_ref[
                    seg, pl.ds(row, 16), :
                ].astype(jnp.float32)
            return 0

        lax.fori_loop(0, need // 16, widen, 0)
        lane_unit = lax.broadcasted_iota(jnp.int32, (8, LANE), 1) // UNIT

        def group(at, _):
            for phase in range(4):
                loaded = {}
                turned = {}
                for tile in range(tiles):
                    parts = []
                    for slot in range(4):
                        col = 4 * tile + slot
                        seg, unit = col // per_row, col % per_row
                        source = shift + phase * per_row + unit
                        key = (seg, source // 4)
                        if key not in loaded:
                            loaded[key] = wide[
                                pl.ds(seg * need + key[1] + at * (8 * per_row), 8, stride=per_row),
                                :,
                            ]
                        turn = (slot - source) % 4
                        if (key, turn) not in turned:
                            turned[key, turn] = rolled(loaded[key], turn)
                        parts.append(turned[key, turn])
                    mixed[pl.ds(tile * block + phase + at * 32, 8, stride=4), :] = merge_units(
                        parts, lane_unit
                    )
            return 0

        lax.fori_loop(0, block // 32, group, 0)

        def narrow(at, _):
            row = pl.multiple_of(at * 16, 16)
            for tile in range(tiles):
                out_ref[pl.ds(row, 16), tile * LANE : (tile + 1) * LANE] = mixed[
                    pl.ds(pl.multiple_of(tile * block + row, 16), 16), :
                ].astype(jnp.bfloat16)
            return 0

        lax.fori_loop(0, block // 16, narrow, 0)

    return pl.pallas_call(
        kernel,
        grid=(rows_of // block,),
        in_specs=[
            pl.BlockSpec(
                (pl.Element(segs), pl.Element(need), pl.Element(LANE)),
                lambda at: (0, pl.multiple_of(base + at * step, 16), 0),
            )
        ],
        out_specs=pl.BlockSpec((block, cols_of), lambda at: (at, 0)),
        out_shape=jax.ShapeDtypeStruct((rows_of, cols_of), jnp.bfloat16),
        scratch_shapes=[
            pltpu.VMEM((segs * need, LANE), jnp.float32),
            pltpu.VMEM((tiles * block, LANE), jnp.float32),
        ],
        compiler_params=pltpu.CompilerParams(vmem_limit_bytes=48 << 20),
        cost_estimate=pl.CostEstimate(
            flops=0, bytes_accessed=4 * rows_of * cols_of, transcendentals=0
        ),
        name="read_matrix",
    )(flat)


def write_flat(segs, parts):
    specs = piece_specs()
    block_rows = 192
    total = sum(rows_of * cols_of // segs for rows_of, cols_of, _ in specs)
    flat_rows = total // LANE
    places = []
    offset = 0
    big, small = [], []
    for (rows_of, cols_of, _), value in zip(specs, parts):
        width = cols_of // segs
        length = rows_of * width
        if rows_of > 9:
            assert rows_of % block_rows == 0
            places.append((True, offset, rows_of, width, len(big)))
            big.append(value)
        else:
            lead = offset % LANE
            rest = -(lead + length) % LANE
            padded = jnp.pad(value.reshape(-1), (lead, rest)).reshape(-1, LANE)
            places.append((False, offset, length, None, len(small)))
            small.append(padded)
        offset += length
    widths = sorted({place[3] for place in places if place[0]})
    chunk = 1008

    def kernel(*refs):
        big_refs = refs[: len(big)]
        small_refs = refs[len(big) : len(big) + len(small)]
        out_ref = refs[len(big) + len(small)]
        flat = refs[len(big) + len(small) + 1]
        bufs = refs[len(big) + len(small) + 2 : len(big) + len(small) + 2 + len(widths)]
        out_buf, in_sem, out_sem = refs[-3:]
        lane_unit = lax.broadcasted_iota(jnp.int32, (8, LANE), 1) // UNIT
        row_unit = lax.broadcasted_iota(jnp.int32, (1, LANE), 1) // UNIT

        def place_small(ref, offset, length):
            first = offset // LANE
            last = (offset + length - 1) // LANE
            lead = offset % LANE // UNIT
            tail = (offset + length) % LANE // UNIT
            count = last - first + 1
            if count > 2:

                def copy_row(at, _):
                    flat[pl.ds(first + 1 + at, 1), :] = ref[pl.ds(1 + at, 1), :]
                    return 0

                lax.fori_loop(0, count - 2, copy_row, 0)
            keep = row_unit >= lead
            if count == 1 and tail:
                keep = keep & (row_unit < tail)
            flat[first : first + 1, :] = jnp.where(keep, ref[0:1, :], flat[first : first + 1, :])
            if count > 1:
                flat[last : last + 1, :] = (
                    jnp.where(
                        row_unit < tail, ref[count - 1 : count, :], flat[last : last + 1, :]
                    )
                    if tail
                    else ref[count - 1 : count, :]
                )

        def place_big(ref, buf, offset, rows_of, width):
            per_row = width // UNIT
            first = offset // LANE
            shift = offset % LANE // UNIT
            block = block_rows
            blocks = rows_of // block

            tiles = -(-width // LANE)

            def fetch(at, slot):
                row = pl.multiple_of(at * block, 64)
                return [
                    pltpu.make_async_copy(
                        ref.at[pl.ds(row, block), tile * LANE : (tile + 1) * LANE],
                        buf.at[slot, tile],
                        in_sem.at[slot, tile],
                    )
                    for tile in range(tiles)
                ]

            for copy in fetch(0, 0):
                copy.start()

            def one_block(at, _):
                slot = lax.rem(at, 2)

                @pl.when(at + 1 < blocks)
                def _():
                    for copy in fetch(at + 1, 1 - slot):
                        copy.start()

                for copy in fetch(at, slot):
                    copy.wait()

                def group(sub, _):
                    loaded = {}
                    turned = {}

                    def unit_value(phase, unit, lane):
                        key = (phase, unit // 4)
                        if key not in loaded:
                            loaded[key] = buf[
                                slot, key[1], pl.ds(phase + sub * 32, 8, stride=4), :
                            ]
                        turn = (lane - unit) % 4
                        if (key, turn) not in turned:
                            turned[key, turn] = rolled(loaded[key], turn)
                        return turned[key, turn]

                    start = first + (at * (block // 4) + sub * 8) * per_row
                    for row in range(per_row + (1 if shift else 0)):
                        where = pl.ds(start + row, 8, stride=per_row)
                        parts = []
                        kept = None
                        for lane in range(4):
                            unit = 4 * row + lane - shift
                            if unit < 0 or unit >= 4 * per_row:
                                if kept is None:
                                    kept = flat[where, :]
                                parts.append(kept)
                            else:
                                parts.append(unit_value(unit // per_row, unit % per_row, lane))
                        flat[where, :] = merge_units(parts, lane_unit)
                    return 0

                lax.fori_loop(0, block // 32, group, 0)
                return 0

            lax.fori_loop(0, blocks, one_block, 0)

        for is_big, offset, rows_of, width, index in places:
            if is_big:
                place_big(big_refs[index], bufs[widths.index(width)], offset, rows_of, width)
            else:
                place_small(small_refs[index], offset, rows_of)

        def emit(at, slot):
            return pltpu.make_async_copy(
                out_buf.at[slot],
                out_ref.at[pl.ds(pl.multiple_of(at * chunk, 16), chunk), :],
                out_sem.at[slot],
            )

        def one_chunk(at, _):
            slot = lax.rem(at, 2)

            @pl.when(at >= 2)
            def _():
                emit(at - 2, slot).wait()

            def narrow(sub, _):
                row = pl.multiple_of(sub * 16, 16)
                out_buf[slot, pl.ds(row, 16), :] = flat[
                    pl.ds(pl.multiple_of(at * chunk + row, 16), 16), :
                ].astype(jnp.bfloat16)
                return 0

            lax.fori_loop(0, chunk // 16, narrow, 0, unroll=3)
            emit(at, slot).start()
            return 0

        chunks = flat_rows // chunk
        lax.fori_loop(0, chunks, one_chunk, 0)
        emit(chunks - 2, (chunks - 2) % 2).wait()
        emit(chunks - 1, (chunks - 1) % 2).wait()

    return pl.pallas_call(
        kernel,
        in_specs=[pl.BlockSpec(memory_space=pl.ANY)] * len(big)
        + [pl.BlockSpec(memory_space=pltpu.VMEM)] * len(small),
        out_specs=pl.BlockSpec(memory_space=pl.ANY),
        out_shape=jax.ShapeDtypeStruct((flat_rows, LANE), jnp.bfloat16),
        scratch_shapes=[pltpu.VMEM((flat_rows, LANE), jnp.float32)]
        + [
            pltpu.VMEM((2, -(-width // LANE), block_rows, LANE), jnp.float32) for width in widths
        ]
        + [
            pltpu.VMEM((2, chunk, LANE), jnp.bfloat16),
            pltpu.SemaphoreType.DMA((2, -(-widths[-1] // LANE))),
            pltpu.SemaphoreType.DMA((2,)),
        ],
        compiler_params=pltpu.CompilerParams(vmem_limit_bytes=56 << 20),
        cost_estimate=pl.CostEstimate(flops=0, bytes_accessed=6 * total, transcendentals=0),
        name="write_flat",
    )(*big, *small)


def gather_weights(shard_low, segs):
    whole = lax.all_gather(shard_low.reshape(-1, LANE), ("seq", "dp"), axis=0, tiled=True)
    flat = whole.reshape(segs, -1, LANE)
    pieces = []
    offset = 0
    for rows_of, cols_of, vector in piece_specs():
        length = rows_of * cols_of // segs
        if rows_of > 9:
            pieces.append(read_matrix(flat, offset, rows_of, cols_of, segs))
        else:
            first, last = offset // LANE, -(-(offset + length) // LANE)
            lead = offset - first * LANE
            block = flat[:, first:last].reshape(segs, -1)[:, lead : lead + length]
            block = block.reshape(segs, rows_of, cols_of // segs).transpose(1, 0, 2)
            pieces.append(block.reshape(cols_of) if vector else block.reshape(rows_of, cols_of))
        offset = offset + length
    return pieces


def norm_parts(values):
    centred = values - jnp.mean(values, axis=-1, keepdims=True)
    inverse = lax.rsqrt(jnp.mean(centred * centred, axis=-1, keepdims=True) + eps_norm)
    return (centred * inverse, inverse)


def norm_back(grad_normed, normed, inverse):
    return inverse * (
        grad_normed
        - jnp.mean(grad_normed, axis=-1, keepdims=True)
        - normed * jnp.mean(grad_normed * normed, axis=-1, keepdims=True)
    )


def silu_slope(values):
    sigmoid_v = jax.nn.sigmoid(values)
    return sigmoid_v * (1.0 + values * (1.0 - sigmoid_v))


def to_low(values):
    return values.astype(jnp.bfloat16)


def matmul(left_op, right_op):
    return jnp.dot(left_op, right_op, preferred_element_type=jnp.float32)


def matmul_t(left_op, right_op):
    return lax.dot_general(
        left_op,
        right_op,
        (((left_op.ndim - 1,), (1,)), ((), ())),
        preferred_element_type=jnp.float32,
    )


def outer_sum(left_op, right_op):
    left_flat = left_op.reshape(-1, left_op.shape[-1])
    right_flat = right_op.reshape(-1, right_op.shape[-1])
    right_flat = jnp.pad(right_flat, ((0, 0), (0, -right_flat.shape[1] % LANE)))
    return lax.dot_general(
        left_flat, right_flat, (((0,), (0,)), ((), ())), preferred_element_type=jnp.float32
    )


def depth_conv(padded, kernel, row_dev, col_dev, flipped):
    kernel_f = kernel.astype(jnp.float32)
    summed = jnp.zeros(padded.shape[:1] + (row_dev, col_dev) + padded.shape[3:], jnp.float32)
    for tap_row in range(3):
        for tap_col in range(3):
            row_at = 2 - tap_row if flipped else tap_row
            col_at = 2 - tap_col if flipped else tap_col
            summed = (
                summed
                + kernel_f[tap_row * 3 + tap_col]
                * padded[:, row_at : row_at + row_dev, col_at : col_at + col_dev, :]
            )
    return summed


def shards(latents, text, time_embed, cotangent, params, moment_one, moment_two):
    lat_dev, row_dev, col_dev, width = latents.shape
    tokens_dev = row_dev * col_dev
    heads_lin = D // 32
    cross_dim = D // CROSS_HEADS
    score_scale = 1.0 / math.sqrt(cross_dim)
    text_len = text.shape[1]
    segs = lax.axis_size("seq")
    count_dp = lax.axis_size("dp")
    shard_low = params.astype(jnp.bfloat16)
    (
        mod_table,
        w_qkv,
        w_attn_out,
        b_attn_out,
        w_cross_q,
        w_cross_kv,
        w_cross_out,
        b_cross_out,
        w_in,
        b_in,
        w_depth,
        b_depth,
        w_point,
        b_point,
    ) = gather_weights(shard_low, segs)
    modulation = mod_table.astype(jnp.float32)[None] + time_embed.reshape(lat_dev, 6, D)
    shift_one = modulation[:, 0][:, None, :]
    scale_one = modulation[:, 1][:, None, :]
    gate_one = modulation[:, 2][:, None, :]
    shift_two = modulation[:, 3][:, None, :]
    scale_two = modulation[:, 4][:, None, :]
    gate_two = modulation[:, 5][:, None, :]
    tokens = latents.reshape(lat_dev, tokens_dev, D).astype(jnp.float32)
    normed_one, inverse_one = norm_parts(tokens)
    hidden_one = to_low(normed_one * (1.0 + scale_one) + shift_one)
    projected = matmul(hidden_one, w_qkv)
    query_pre = projected[..., :D]
    key_pre = projected[..., D : 2 * D]
    queries = to_low(jnp.maximum(query_pre, 0.0)).reshape(lat_dev, tokens_dev, heads_lin, 32)
    keys_lin = to_low(jnp.maximum(key_pre, 0.0)).reshape(lat_dev, tokens_dev, heads_lin, 32)
    values_lin = to_low(projected[..., 2 * D :]).reshape(lat_dev, tokens_dev, heads_lin, 32)
    state_part = jnp.einsum(
        "lrhd,lrhe->lhde", keys_lin, values_lin, preferred_element_type=jnp.float32
    )
    sum_part = jnp.sum(keys_lin, axis=1, dtype=jnp.float32)
    kv_state, key_sum = lax.psum((state_part, sum_part), "seq")
    query_f = queries.astype(jnp.float32)
    numerator = jnp.einsum("lrhd,lhde->lrhe", query_f, kv_state, precision=precise)
    denominator = jnp.einsum("lrhd,lhd->lrh", query_f, key_sum, precision=precise) + eps_linear
    attn_val = numerator / denominator[..., None]
    attended = to_low(attn_val.reshape(lat_dev, tokens_dev, D))
    branch_one = matmul(attended, w_attn_out) + b_attn_out.astype(jnp.float32)
    after_attn = tokens + gate_one * branch_one
    after_low = to_low(after_attn)
    query_c = to_low(matmul(after_low, w_cross_q)).reshape(
        lat_dev, tokens_dev, CROSS_HEADS, cross_dim
    )
    keyval = to_low(matmul(text, w_cross_kv))
    keys_c = keyval[..., :D].reshape(lat_dev, text_len, CROSS_HEADS, cross_dim)
    values_c = keyval[..., D:].reshape(lat_dev, text_len, CROSS_HEADS, cross_dim)
    scores = (
        jnp.einsum("lrhc,lthc->lhrt", query_c, keys_c, preferred_element_type=jnp.float32)
        * score_scale
    )
    row_peak = jnp.max(scores, axis=-1, keepdims=True)
    log_total = row_peak + jnp.log(jnp.sum(jnp.exp(scores - row_peak), axis=-1, keepdims=True))
    probs_low = to_low(jnp.exp(scores - log_total))
    cross_mixed = to_low(
        jnp.einsum(
            "lhrt,lthc->lrhc", probs_low, values_c, preferred_element_type=jnp.float32
        ).reshape(lat_dev, tokens_dev, D)
    )
    after_cross = after_attn + matmul(cross_mixed, w_cross_out) + b_cross_out.astype(jnp.float32)
    normed_two, inverse_two = norm_parts(after_cross)
    hidden_two = to_low(normed_two * (1.0 + scale_two) + shift_two)
    inner_pre = matmul(hidden_two, w_in) + b_in.astype(jnp.float32)
    active = to_low(jax.nn.silu(inner_pre)).reshape(lat_dev, row_dev, col_dev, 2 * FF)
    padded = jnp.pad(with_halo(active, (("seq", 1),), 1), ((0, 0), (0, 0), (1, 1), (0, 0)))
    conv_out = (
        depth_conv(padded, w_depth, row_dev, col_dev, False) + b_depth.astype(jnp.float32)
    ).reshape(lat_dev, tokens_dev, 2 * FF)
    up_part = conv_out[..., :FF]
    gate_part = conv_out[..., FF:]
    gated_mix = to_low(up_part * jax.nn.silu(gate_part))
    branch_two = matmul(gated_mix, w_point) + b_point.astype(jnp.float32)
    output = (after_cross + gate_two * branch_two).astype(jnp.bfloat16).reshape(latents.shape)
    grad_out = cotangent.reshape(lat_dev, tokens_dev, D).astype(jnp.float32)
    grad_gate_two = jnp.sum(grad_out * branch_two, axis=1)
    grad_branch_two = to_low(grad_out * gate_two)
    grad_gated = matmul_t(grad_branch_two, w_point)
    grad_up = grad_gated * jax.nn.silu(gate_part)
    grad_gate = grad_gated * up_part * silu_slope(gate_part)
    grad_conv = to_low(jnp.concatenate([grad_up, grad_gate], axis=-1)).reshape(
        lat_dev, row_dev, col_dev, 2 * FF
    )
    grad_b_depth = jnp.sum(grad_conv, axis=(0, 1, 2), dtype=jnp.float32)
    tap_grads = []
    for tap_row in range(3):
        for tap_col in range(3):
            tap_grads.append(
                jnp.einsum(
                    "lrcf,lrcf->f",
                    padded[:, tap_row : tap_row + row_dev, tap_col : tap_col + col_dev],
                    grad_conv,
                    preferred_element_type=jnp.float32,
                )
            )
    grad_w_depth = jnp.stack(tap_grads)
    grad_padded = jnp.pad(with_halo(grad_conv, (("seq", 1),), 1), ((0, 0), (0, 0), (1, 1), (0, 0)))
    grad_active = depth_conv(grad_padded, w_depth, row_dev, col_dev, True).reshape(
        lat_dev, tokens_dev, 2 * FF
    )
    grad_inner = to_low(grad_active * silu_slope(inner_pre))
    grad_hidden_two = matmul_t(grad_inner, w_in)
    grad_shift_two = jnp.sum(grad_hidden_two, axis=1)
    grad_scale_two = jnp.sum(grad_hidden_two * normed_two, axis=1)
    grad_second = grad_out + norm_back(grad_hidden_two * (1.0 + scale_two), normed_two, inverse_two)
    grad_cross_out = to_low(grad_second)
    grad_mixed = to_low(matmul_t(grad_cross_out, w_cross_out)).reshape(
        lat_dev, tokens_dev, CROSS_HEADS, cross_dim
    )
    scores_again = (
        jnp.einsum("lrhc,lthc->lhrt", query_c, keys_c, preferred_element_type=jnp.float32)
        * score_scale
    )
    probs = jnp.exp(scores_again - log_total)
    grad_probs = jnp.einsum(
        "lrhc,lthc->lhrt", grad_mixed, values_c, preferred_element_type=jnp.float32
    )
    grad_values_c = jnp.einsum(
        "lhrt,lrhc->lthc", to_low(probs), grad_mixed, preferred_element_type=jnp.float32
    )
    grad_scores = to_low(probs * (grad_probs - jnp.sum(probs * grad_probs, axis=-1, keepdims=True)))
    grad_query_c = to_low(
        jnp.einsum("lhrt,lthc->lrhc", grad_scores, keys_c, preferred_element_type=jnp.float32)
        * score_scale
    ).reshape(lat_dev, tokens_dev, D)
    grad_keys_c = (
        jnp.einsum("lhrt,lrhc->lthc", grad_scores, query_c, preferred_element_type=jnp.float32)
        * score_scale
    )
    grad_keyval_part = jnp.concatenate(
        [grad_keys_c.reshape(lat_dev, text_len, D), grad_values_c.reshape(lat_dev, text_len, D)],
        axis=-1,
    )
    grad_keyval_part = grad_keyval_part.reshape(lat_dev, text_len, segs, 2 * D // segs)
    grad_keyval = to_low(
        lax.psum_scatter(
            grad_keyval_part.astype(jnp.bfloat16), "seq", scatter_dimension=2, tiled=True
        ).astype(jnp.float32)
    ).reshape(lat_dev, text_len, 2 * D // segs)
    grad_w_cross_kv = outer_sum(text, grad_keyval)
    grad_first = grad_second + matmul_t(grad_query_c, w_cross_q)
    grad_gate_one = jnp.sum(grad_first * branch_one, axis=1)
    grad_branch_one = to_low(grad_first * gate_one)
    grad_attended = matmul_t(grad_branch_one, w_attn_out).reshape(
        lat_dev, tokens_dev, heads_lin, 32
    )
    grad_numer = grad_attended / denominator[..., None]
    grad_denom = -jnp.sum(grad_attended * attn_val, axis=-1) / denominator
    grad_query = (
        jnp.einsum("lrhe,lhde->lrhd", grad_numer, kv_state, precision=precise)
        + grad_denom[..., None] * key_sum[:, None]
    )
    state_grad_part = jnp.einsum("lrhd,lrhe->lhde", query_f, grad_numer, precision=precise)
    sum_grad_part = jnp.einsum("lrhd,lrh->lhd", query_f, grad_denom, precision=precise)
    state_grad, sum_grad = (
        lax.psum(state_grad_part.astype(jnp.bfloat16), "seq").astype(jnp.float32),
        lax.psum(sum_grad_part.astype(jnp.bfloat16), "seq").astype(jnp.float32),
    )
    keys_f = keys_lin.astype(jnp.float32)
    values_f = values_lin.astype(jnp.float32)
    grad_keys = (
        jnp.einsum("lrhe,lhde->lrhd", values_f, state_grad, precision=precise) + sum_grad[:, None]
    )
    grad_values = jnp.einsum("lrhd,lhde->lrhe", keys_f, state_grad, precision=precise)
    grad_projected = to_low(
        jnp.concatenate(
            [
                grad_query.reshape(lat_dev, tokens_dev, D) * (query_pre > 0.0),
                grad_keys.reshape(lat_dev, tokens_dev, D) * (key_pre > 0.0),
                grad_values.reshape(lat_dev, tokens_dev, D),
            ],
            axis=-1,
        )
    )
    grad_hidden_one = matmul_t(grad_projected, w_qkv)
    grad_input = grad_first + norm_back(
        grad_hidden_one * (1.0 + scale_one), normed_one, inverse_one
    )
    grad_table = jnp.sum(
        jnp.stack(
            [
                jnp.sum(grad_hidden_one, axis=1),
                jnp.sum(grad_hidden_one * normed_one, axis=1),
                grad_gate_one,
                grad_shift_two,
                grad_scale_two,
                grad_gate_two,
            ],
            axis=1,
        ),
        axis=0,
    )
    table_q, depth_q, depth_bias_q = (
        lax.psum_scatter(
            grad_table.reshape(6, segs, D // segs).astype(jnp.bfloat16),
            "seq",
            scatter_dimension=1,
            tiled=True,
        ).astype(jnp.float32),
        lax.psum_scatter(
            grad_w_depth.reshape(9, segs, 2 * FF // segs).astype(jnp.bfloat16),
            "seq",
            scatter_dimension=1,
            tiled=True,
        ).astype(jnp.float32),
        lax.psum_scatter(
            grad_b_depth.reshape(1, segs, 2 * FF // segs).astype(jnp.bfloat16),
            "seq",
            scatter_dimension=1,
            tiled=True,
        ).astype(jnp.float32),
    )
    inputs_cat = jnp.concatenate(
        [hidden_one, attended, after_low, cross_mixed, hidden_two, gated_mix], axis=-1
    )
    inputs_all = lax.all_gather(inputs_cat, "seq", axis=1, tiled=True)

    def quarters(values):
        return values.reshape(lat_dev, tokens_dev, segs, values.shape[-1] // segs)

    outputs_cat = jnp.concatenate(
        [
            quarters(grad_projected),
            quarters(grad_branch_one),
            quarters(grad_query_c),
            quarters(grad_cross_out),
            quarters(grad_inner),
            quarters(grad_branch_two),
        ],
        axis=-1,
    )
    outputs_mine = lax.all_to_all(outputs_cat, "seq", split_axis=2, concat_axis=1, tiled=True)
    outputs_mine = outputs_mine.reshape(lat_dev, outputs_mine.shape[1], outputs_mine.shape[3])
    col_d = D // segs
    col_ff = 2 * FF // segs
    y_qkv = outputs_mine[..., 0 : 3 * col_d]
    y_attn = outputs_mine[..., 3 * col_d : 4 * col_d]
    y_cross_q = outputs_mine[..., 4 * col_d : 5 * col_d]
    y_cross_out = outputs_mine[..., 5 * col_d : 6 * col_d]
    y_inner = outputs_mine[..., 6 * col_d : 6 * col_d + col_ff]
    y_point = outputs_mine[..., 6 * col_d + col_ff : 7 * col_d + col_ff]
    grad_w_qkv = outer_sum(inputs_all[..., 0:D], y_qkv)
    grad_w_attn_out = outer_sum(inputs_all[..., D : 2 * D], y_attn)
    grad_w_cross_q = outer_sum(inputs_all[..., 2 * D : 3 * D], y_cross_q)
    grad_w_cross_out = outer_sum(inputs_all[..., 3 * D : 4 * D], y_cross_out)
    grad_w_in = outer_sum(inputs_all[..., 4 * D : 5 * D], y_inner)
    grad_w_point = outer_sum(inputs_all[..., 5 * D : 5 * D + FF], y_point)
    grad_b_attn_out = jnp.sum(y_attn, axis=(0, 1), dtype=jnp.float32)
    grad_b_cross_out = jnp.sum(y_cross_out, axis=(0, 1), dtype=jnp.float32)
    grad_b_in = jnp.sum(y_inner, axis=(0, 1), dtype=jnp.float32)
    grad_b_point = jnp.sum(y_point, axis=(0, 1), dtype=jnp.float32)
    bias_part = jnp.concatenate(
        [grad_b_attn_out, grad_b_cross_out, grad_b_in, depth_bias_q.ravel(), grad_b_point]
    )
    bias_total = lax.psum(bias_part, "dp")
    quarter_grad = write_flat(
        segs,
        [
            table_q,
            grad_w_qkv,
            grad_w_attn_out,
            grad_b_attn_out,
            grad_w_cross_q,
            grad_w_cross_kv,
            grad_w_cross_out,
            grad_b_cross_out,
            grad_w_in,
            grad_b_in,
            depth_q,
            depth_bias_q,
            grad_w_point,
            grad_b_point,
        ],
    )
    grad_shard = (
        lax.psum_scatter(
            quarter_grad.reshape(count_dp, -1, LANE), "dp", scatter_dimension=0, tiled=True
        )
        .astype(jnp.float32)
        .reshape(1, -1)
    )
    square_total = lax.psum(jnp.sum(grad_shard * grad_shard), ("dp", "seq"))
    entries_all = grad_shard.size * lax.axis_size(("dp", "seq"))
    factor = lax.rsqrt(square_total / entries_all + 1e-06)
    gradient = grad_shard * factor
    bias_grads = (bias_total * factor).reshape(1, -1)
    moment_one_new = beta_first * moment_one + (1.0 - beta_first) * gradient
    moment_two_new = beta_second * moment_two + (1.0 - beta_second) * gradient * gradient
    first_hat = moment_one_new / (1.0 - beta_first**adam_steps)
    second_hat = moment_two_new / (1.0 - beta_second**adam_steps)
    update = first_hat / (jnp.sqrt(second_hat) + adam_eps) + weight_decay * params
    return (
        output,
        grad_input.reshape(latents.shape),
        gradient,
        moment_one_new,
        moment_two_new,
        update,
        bias_grads,
    )


def solution(mesh):
    return jax.shard_map(
        shards,
        mesh=mesh,
        in_specs=(
            P("dp", "seq", None, None),
            P("dp", None, None),
            P("dp", None),
            P("dp", "seq", None, None),
            P("seq", "dp"),
            P("seq", "dp"),
            P("seq", "dp"),
        ),
        out_specs=(
            P("dp", "seq", None, None),
            P("dp", "seq", None, None),
            P("seq", "dp"),
            P("seq", "dp"),
            P("seq", "dp"),
            P("seq", "dp"),
            P("seq", None),
        ),
        check_vma=False,
    )
```

```python
import math

import jax
import jax.numpy as jnp
from jax import lax
from jax.experimental import pallas as pl
from jax.experimental.pallas import tpu as pltpu
from jax.sharding import PartitionSpec as P

D = 1152
FF = 2880
CROSS_HEADS = 16


precise = lax.Precision.HIGHEST
eps_norm = 1e-06
eps_linear = 1e-06
beta_first = 0.9
beta_second = 0.95
adam_eps = 1e-08
weight_decay = 0.01
adam_steps = 100.0


def with_halo(block, sides, width):
    for axis, dim in sides:
        count = lax.axis_size(axis)
        forward = [(i, i + 1) for i in range(count - 1)]
        backward = [(target, source) for source, target in forward]
        low = lax.ppermute(
            lax.slice_in_dim(block, block.shape[dim] - width, None, axis=dim), axis, forward
        )
        high = lax.ppermute(lax.slice_in_dim(block, 0, width, axis=dim), axis, backward)
        block = jnp.concatenate([low, block, high], axis=dim)
    return block


def piece_specs():
    return [
        (6, D, False),
        (D, 3 * D, False),
        (D, D, False),
        (1, D, True),
        (D, D, False),
        (D, 2 * D, False),
        (D, D, False),
        (1, D, True),
        (D, 2 * FF, False),
        (1, 2 * FF, True),
        (9, 2 * FF, False),
        (1, 2 * FF, True),
        (FF, D, False),
        (1, D, True),
    ]


LANE = 128
UNIT = 32


def merge_units(values, lane_unit):
    out = values[0]
    last = values[0]
    for position in range(1, 4):
        if values[position] is not last:
            out = jnp.where(lane_unit >= position, values[position], out)
            last = values[position]
    return out


def rolled(value, units):
    units = units % 4
    return value if units == 0 else pltpu.roll(value, units * UNIT, 1)


def matrix_rows(count_rows):
    return 192 if count_rows % 192 == 0 else 64


def read_matrix(flat, offset, rows_of, cols_of, segs):
    total_rows = flat.shape[1]
    per_row = cols_of // segs // UNIT
    unit_at = offset // UNIT
    block = matrix_rows(rows_of)
    base = unit_at // 4 // 16 * 16
    shift = unit_at - 4 * base
    step = block * per_row // 4
    need = (shift + block * per_row - 1) // 4 + 1
    need = -(-need // 16) * 16
    assert base + (rows_of // block - 1) * step + need <= total_rows
    tiles = cols_of // LANE

    def kernel(in_ref, out_ref, wide, mixed):
        def widen(at, _):
            row = pl.multiple_of(at * 16, 16)
            for seg in range(segs):
                wide[pl.ds(pl.multiple_of(seg * need + row, 16), 16), :] = in_ref[
                    seg, pl.ds(row, 16), :
                ].astype(jnp.float32)
            return 0

        lax.fori_loop(0, need // 16, widen, 0)
        lane_unit = lax.broadcasted_iota(jnp.int32, (8, LANE), 1) // UNIT

        def group(at, _):
            for phase in range(4):
                loaded = {}
                turned = {}
                for tile in range(tiles):
                    parts = []
                    for slot in range(4):
                        col = 4 * tile + slot
                        seg, unit = col // per_row, col % per_row
                        source = shift + phase * per_row + unit
                        key = (seg, source // 4)
                        if key not in loaded:
                            loaded[key] = wide[
                                pl.ds(seg * need + key[1] + at * (8 * per_row), 8, stride=per_row),
                                :,
                            ]
                        turn = (slot - source) % 4
                        if (key, turn) not in turned:
                            turned[key, turn] = rolled(loaded[key], turn)
                        parts.append(turned[key, turn])
                    mixed[pl.ds(tile * block + phase + at * 32, 8, stride=4), :] = merge_units(
                        parts, lane_unit
                    )
            return 0

        lax.fori_loop(0, block // 32, group, 0)

        def narrow(at, _):
            row = pl.multiple_of(at * 16, 16)
            for tile in range(tiles):
                out_ref[pl.ds(row, 16), tile * LANE : (tile + 1) * LANE] = mixed[
                    pl.ds(pl.multiple_of(tile * block + row, 16), 16), :
                ].astype(jnp.bfloat16)
            return 0

        lax.fori_loop(0, block // 16, narrow, 0)

    return pl.pallas_call(
        kernel,
        grid=(rows_of // block,),
        in_specs=[
            pl.BlockSpec(
                (pl.Element(segs), pl.Element(need), pl.Element(LANE)),
                lambda at: (0, pl.multiple_of(base + at * step, 16), 0),
            )
        ],
        out_specs=pl.BlockSpec((block, cols_of), lambda at: (at, 0)),
        out_shape=jax.ShapeDtypeStruct((rows_of, cols_of), jnp.bfloat16),
        scratch_shapes=[
            pltpu.VMEM((segs * need, LANE), jnp.float32),
            pltpu.VMEM((tiles * block, LANE), jnp.float32),
        ],
        compiler_params=pltpu.CompilerParams(vmem_limit_bytes=48 << 20),
        cost_estimate=pl.CostEstimate(
            flops=0, bytes_accessed=4 * rows_of * cols_of, transcendentals=0
        ),
        name="read_matrix",
    )(flat)


def write_flat(segs, parts):
    specs = piece_specs()
    block_rows = 192
    total = sum(rows_of * cols_of // segs for rows_of, cols_of, _ in specs)
    flat_rows = total // LANE
    places = []
    offset = 0
    big, small = [], []
    for (rows_of, cols_of, _), value in zip(specs, parts):
        width = cols_of // segs
        length = rows_of * width
        if rows_of > 9:
            assert rows_of % block_rows == 0
            places.append((True, offset, rows_of, width, len(big)))
            big.append(value)
        else:
            lead = offset % LANE
            rest = -(lead + length) % LANE
            padded = jnp.pad(value.reshape(-1), (lead, rest)).reshape(-1, LANE)
            places.append((False, offset, length, None, len(small)))
            small.append(padded)
        offset += length
    widths = sorted({place[3] for place in places if place[0]})
    chunk = 1008

    def kernel(*refs):
        big_refs = refs[: len(big)]
        small_refs = refs[len(big) : len(big) + len(small)]
        out_ref = refs[len(big) + len(small)]
        flat = refs[len(big) + len(small) + 1]
        bufs = refs[len(big) + len(small) + 2 : len(big) + len(small) + 2 + len(widths)]
        out_buf, in_sem, out_sem = refs[-3:]
        lane_unit = lax.broadcasted_iota(jnp.int32, (8, LANE), 1) // UNIT
        row_unit = lax.broadcasted_iota(jnp.int32, (1, LANE), 1) // UNIT

        def place_small(ref, offset, length):
            first = offset // LANE
            last = (offset + length - 1) // LANE
            lead = offset % LANE // UNIT
            tail = (offset + length) % LANE // UNIT
            count = last - first + 1
            if count > 2:

                def copy_row(at, _):
                    flat[pl.ds(first + 1 + at, 1), :] = ref[pl.ds(1 + at, 1), :]
                    return 0

                lax.fori_loop(0, count - 2, copy_row, 0)
            keep = row_unit >= lead
            if count == 1 and tail:
                keep = keep & (row_unit < tail)
            flat[first : first + 1, :] = jnp.where(keep, ref[0:1, :], flat[first : first + 1, :])
            if count > 1:
                flat[last : last + 1, :] = (
                    jnp.where(
                        row_unit < tail, ref[count - 1 : count, :], flat[last : last + 1, :]
                    )
                    if tail
                    else ref[count - 1 : count, :]
                )

        def place_big(ref, buf, offset, rows_of, width):
            per_row = width // UNIT
            first = offset // LANE
            shift = offset % LANE // UNIT
            block = block_rows
            blocks = rows_of // block

            tiles = -(-width // LANE)

            def fetch(at, slot):
                row = pl.multiple_of(at * block, 64)
                return [
                    pltpu.make_async_copy(
                        ref.at[pl.ds(row, block), tile * LANE : (tile + 1) * LANE],
                        buf.at[slot, tile],
                        in_sem.at[slot, tile],
                    )
                    for tile in range(tiles)
                ]

            for copy in fetch(0, 0):
                copy.start()

            def one_block(at, _):
                slot = lax.rem(at, 2)

                @pl.when(at + 1 < blocks)
                def _():
                    for copy in fetch(at + 1, 1 - slot):
                        copy.start()

                for copy in fetch(at, slot):
                    copy.wait()

                def group(sub, _):
                    loaded = {}
                    turned = {}

                    def unit_value(phase, unit, lane):
                        key = (phase, unit // 4)
                        if key not in loaded:
                            loaded[key] = buf[
                                slot, key[1], pl.ds(phase + sub * 32, 8, stride=4), :
                            ]
                        turn = (lane - unit) % 4
                        if (key, turn) not in turned:
                            turned[key, turn] = rolled(loaded[key], turn)
                        return turned[key, turn]

                    start = first + (at * (block // 4) + sub * 8) * per_row
                    for row in range(per_row + (1 if shift else 0)):
                        where = pl.ds(start + row, 8, stride=per_row)
                        parts = []
                        kept = None
                        for lane in range(4):
                            unit = 4 * row + lane - shift
                            if unit < 0 or unit >= 4 * per_row:
                                if kept is None:
                                    kept = flat[where, :]
                                parts.append(kept)
                            else:
                                parts.append(unit_value(unit // per_row, unit % per_row, lane))
                        flat[where, :] = merge_units(parts, lane_unit)
                    return 0

                lax.fori_loop(0, block // 32, group, 0)
                return 0

            lax.fori_loop(0, blocks, one_block, 0)

        for is_big, offset, rows_of, width, index in places:
            if is_big:
                place_big(big_refs[index], bufs[widths.index(width)], offset, rows_of, width)
            else:
                place_small(small_refs[index], offset, rows_of)

        def emit(at, slot):
            return pltpu.make_async_copy(
                out_buf.at[slot],
                out_ref.at[pl.ds(pl.multiple_of(at * chunk, 16), chunk), :],
                out_sem.at[slot],
            )

        def one_chunk(at, _):
            slot = lax.rem(at, 2)

            @pl.when(at >= 2)
            def _():
                emit(at - 2, slot).wait()

            def narrow(sub, _):
                row = pl.multiple_of(sub * 16, 16)
                out_buf[slot, pl.ds(row, 16), :] = flat[
                    pl.ds(pl.multiple_of(at * chunk + row, 16), 16), :
                ].astype(jnp.bfloat16)
                return 0

            lax.fori_loop(0, chunk // 16, narrow, 0, unroll=3)
            emit(at, slot).start()
            return 0

        chunks = flat_rows // chunk
        lax.fori_loop(0, chunks, one_chunk, 0)
        emit(chunks - 2, (chunks - 2) % 2).wait()
        emit(chunks - 1, (chunks - 1) % 2).wait()

    return pl.pallas_call(
        kernel,
        in_specs=[pl.BlockSpec(memory_space=pl.ANY)] * len(big)
        + [pl.BlockSpec(memory_space=pltpu.VMEM)] * len(small),
        out_specs=pl.BlockSpec(memory_space=pl.ANY),
        out_shape=jax.ShapeDtypeStruct((flat_rows, LANE), jnp.bfloat16),
        scratch_shapes=[pltpu.VMEM((flat_rows, LANE), jnp.float32)]
        + [
            pltpu.VMEM((2, -(-width // LANE), block_rows, LANE), jnp.float32) for width in widths
        ]
        + [
            pltpu.VMEM((2, chunk, LANE), jnp.bfloat16),
            pltpu.SemaphoreType.DMA((2, -(-widths[-1] // LANE))),
            pltpu.SemaphoreType.DMA((2,)),
        ],
        compiler_params=pltpu.CompilerParams(vmem_limit_bytes=56 << 20),
        cost_estimate=pl.CostEstimate(flops=0, bytes_accessed=6 * total, transcendentals=0),
        name="write_flat",
    )(*big, *small)


def round_rows(values):
    def kernel(in_ref, out_ref):
        out_ref[...] = in_ref[...].astype(jnp.bfloat16)

    return pl.pallas_call(
        kernel,
        in_specs=[pl.BlockSpec(memory_space=pltpu.VMEM)],
        out_specs=pl.BlockSpec(memory_space=pltpu.VMEM),
        out_shape=jax.ShapeDtypeStruct(values.shape, jnp.bfloat16),
        name="round_rows",
    )(values)


def gather_weights(shard_low, segs):
    whole = lax.all_gather(shard_low, ("seq", "dp"), axis=0, tiled=True)
    flat = whole.reshape(segs, -1, LANE)
    pieces = []
    offset = 0
    for rows_of, cols_of, vector in piece_specs():
        length = rows_of * cols_of // segs
        if rows_of > 9:
            pieces.append(read_matrix(flat, offset, rows_of, cols_of, segs))
        else:
            first, last = offset // LANE, -(-(offset + length) // LANE)
            lead = offset - first * LANE
            block = flat[:, first:last].reshape(segs, -1)[:, lead : lead + length]
            block = block.reshape(segs, rows_of, cols_of // segs).transpose(1, 0, 2)
            pieces.append(block.reshape(cols_of) if vector else block.reshape(rows_of, cols_of))
        offset = offset + length
    return pieces


MESH = pl.DeviceIdType.MESH


def peer_barrier(groups):
    barrier = pltpu.get_barrier_semaphore()
    total = 0
    for axis, count in groups:
        me = lax.axis_index(axis)
        for step in range(1, count):
            pl.semaphore_signal(
                barrier, inc=1, device_id={axis: lax.rem(me + step, count)}, device_id_type=MESH
            )
        total += count - 1
    pl.semaphore_wait(barrier, total)


def exchange(axis, count, source, slots, send_sem, recv_sem):
    me = lax.axis_index(axis)
    for step in range(1, count):
        pltpu.make_async_remote_copy(
            src_ref=source,
            dst_ref=slots.at[me],
            send_sem=send_sem.at[step - 1],
            recv_sem=recv_sem.at[me],
            device_id={axis: lax.rem(me + step, count)},
            device_id_type=MESH,
        ).start()


def exchange_wait(axis, count, source, slots, send_sem, recv_sem):
    me = lax.axis_index(axis)
    for step in range(1, count):
        peer = lax.rem(me + step, count)
        copy = pltpu.make_async_remote_copy(
            src_ref=source,
            dst_ref=slots.at[peer],
            send_sem=send_sem.at[step - 1],
            recv_sem=recv_sem.at[peer],
            device_id={axis: peer},
            device_id_type=MESH,
        )
        copy.wait_send()
        copy.wait_recv()


def in_order(axis, count, own, slots):
    me = lax.axis_index(axis)
    total = None
    for index in range(count):
        term = jnp.where(me == index, own, slots[index].astype(jnp.float32))
        total = term if total is None else total + term
    return total


def seq_sum(block, collective_id):
    count = lax.axis_size("seq")

    def kernel(in_ref, out_ref, slots, send_sem, recv_sem):
        peer_barrier([("seq", count)])
        exchange("seq", count, in_ref, slots, send_sem, recv_sem)
        exchange_wait("seq", count, in_ref, slots, send_sem, recv_sem)
        out_ref[...] = in_order("seq", count, in_ref[...].astype(jnp.float32), slots)

    return pl.pallas_call(
        kernel,
        in_specs=[pl.BlockSpec(memory_space=pltpu.VMEM)],
        out_specs=pl.BlockSpec(memory_space=pltpu.VMEM),
        out_shape=jax.ShapeDtypeStruct(block.shape, jnp.float32),
        scratch_shapes=[
            pltpu.VMEM((count,) + block.shape, block.dtype),
            pltpu.SemaphoreType.DMA((count - 1,)),
            pltpu.SemaphoreType.DMA((count,)),
        ],
        compiler_params=pltpu.CompilerParams(collective_id=collective_id, has_side_effects=True),
        name="seq_sum",
    )(block)


def state_sum(state, sums, kind, collective_id):
    heads = state.shape[1]
    flat = jnp.concatenate(
        [state.reshape(-1, LANE), jnp.pad(sums.reshape(-1), (0, -sums.size % LANE)).reshape(-1, LANE)]
    ).astype(kind)
    rows = flat.shape[0]
    flat = jnp.pad(flat, ((0, -rows % 16), (0, 0)))
    total = seq_sum(flat, collective_id)
    split = state.size // LANE
    return (
        total[:split].reshape(state.shape),
        total[split:].reshape(-1)[: sums.size].reshape(1, heads, -1),
    )


def finish(grad_shard, bias_part, params, moment_one, moment_two):
    rows = grad_shard.shape[0]
    count_dp = lax.axis_size("dp")
    count_seq = lax.axis_size("seq")
    entries = rows * LANE * count_dp * count_seq
    chunk = 48 if rows % 48 == 0 else rows
    bias_rows = bias_part.shape[0]

    def kernel(
        grad_ref,
        bias_ref,
        param_ref,
        one_ref,
        two_ref,
        gradient_ref,
        one_out,
        two_out,
        update_ref,
        bias_out,
        square,
        square_dp,
        square_seq,
        partial,
        bias_slots,
        send_bias,
        recv_bias,
        send_dp,
        recv_dp,
        send_seq,
        recv_seq,
    ):
        peer_barrier([("dp", count_dp), ("seq", count_seq)])
        exchange("dp", count_dp, bias_ref, bias_slots, send_bias, recv_bias)

        def squares(at, total):
            part = grad_ref[pl.ds(at * chunk, chunk), :].astype(jnp.float32)
            return total + jnp.sum(part * part, axis=0, keepdims=True)

        total = lax.fori_loop(0, rows // chunk, squares, jnp.zeros((1, LANE), jnp.float32))
        square[...] = jnp.broadcast_to(total, (8, LANE))
        exchange("dp", count_dp, square, square_dp, send_dp, recv_dp)
        exchange_wait("dp", count_dp, square, square_dp, send_dp, recv_dp)
        partial[...] = in_order("dp", count_dp, square[...], square_dp)
        exchange("seq", count_seq, partial, square_seq, send_seq, recv_seq)
        exchange_wait("seq", count_seq, partial, square_seq, send_seq, recv_seq)
        whole = jnp.sum(
            in_order("seq", count_seq, partial[...], square_seq)[0:1], axis=1, keepdims=True
        )
        factor = lax.rsqrt(whole / entries + 1e-06)
        exchange_wait("dp", count_dp, bias_ref, bias_slots, send_bias, recv_bias)
        bias_out[...] = in_order("dp", count_dp, bias_ref[...], bias_slots) * factor

        def step(at, _):
            where = pl.ds(at * chunk, chunk)
            gradient = grad_ref[where, :].astype(jnp.float32) * factor
            first = beta_first * one_ref[where, :] + (1.0 - beta_first) * gradient
            second = beta_second * two_ref[where, :] + (1.0 - beta_second) * gradient * gradient
            gradient_ref[where, :] = gradient
            one_out[where, :] = first
            two_out[where, :] = second
            first_hat = first / (1.0 - beta_first**adam_steps)
            second_hat = second / (1.0 - beta_second**adam_steps)
            update_ref[where, :] = (
                first_hat / (jnp.sqrt(second_hat) + adam_eps) + weight_decay * param_ref[where, :]
            )
            return 0

        lax.fori_loop(0, rows // chunk, step, 0)

    flat = jax.ShapeDtypeStruct((rows, LANE), jnp.float32)
    tile = (8, LANE)
    return pl.pallas_call(
        kernel,
        in_specs=[pl.BlockSpec(memory_space=pltpu.VMEM)] * 5,
        out_specs=[pl.BlockSpec(memory_space=pltpu.VMEM)] * 5,
        out_shape=[flat] * 4 + [jax.ShapeDtypeStruct((bias_rows, LANE), jnp.float32)],
        scratch_shapes=[
            pltpu.VMEM(tile, jnp.float32),
            pltpu.VMEM((count_dp,) + tile, jnp.float32),
            pltpu.VMEM((count_seq,) + tile, jnp.float32),
            pltpu.VMEM(tile, jnp.float32),
            pltpu.VMEM((count_dp, bias_rows, LANE), jnp.float32),
            pltpu.SemaphoreType.DMA((count_dp - 1,)),
            pltpu.SemaphoreType.DMA((count_dp,)),
            pltpu.SemaphoreType.DMA((count_dp - 1,)),
            pltpu.SemaphoreType.DMA((count_dp,)),
            pltpu.SemaphoreType.DMA((count_seq - 1,)),
            pltpu.SemaphoreType.DMA((count_seq,)),
        ],
        compiler_params=pltpu.CompilerParams(
            collective_id=1, has_side_effects=True, vmem_limit_bytes=48 << 20
        ),
        name="finish",
    )(grad_shard, bias_part, params, moment_one, moment_two)


def norm_parts(values):
    centred = values - jnp.mean(values, axis=-1, keepdims=True)
    inverse = lax.rsqrt(jnp.mean(centred * centred, axis=-1, keepdims=True) + eps_norm)
    return (centred * inverse, inverse)


def norm_back(grad_normed, normed, inverse):
    return inverse * (
        grad_normed
        - jnp.mean(grad_normed, axis=-1, keepdims=True)
        - normed * jnp.mean(grad_normed * normed, axis=-1, keepdims=True)
    )


def silu_slope(values):
    sigmoid_v = jax.nn.sigmoid(values)
    return sigmoid_v * (1.0 + values * (1.0 - sigmoid_v))


def to_low(values):
    return values.astype(jnp.bfloat16)


def matmul(left_op, right_op):
    return jnp.dot(left_op, right_op, preferred_element_type=jnp.float32)


def matmul_t(left_op, right_op):
    return lax.dot_general(
        left_op,
        right_op,
        (((left_op.ndim - 1,), (1,)), ((), ())),
        preferred_element_type=jnp.float32,
    )


def outer_sum(left_op, right_op):
    left_flat = left_op.reshape(-1, left_op.shape[-1])
    right_flat = right_op.reshape(-1, right_op.shape[-1])
    right_flat = jnp.pad(right_flat, ((0, 0), (0, -right_flat.shape[1] % LANE)))
    return lax.dot_general(
        left_flat, right_flat, (((0,), (0,)), ((), ())), preferred_element_type=jnp.float32
    )


def depth_conv(padded, kernel, row_dev, col_dev, flipped):
    kernel_f = kernel.astype(jnp.float32)
    summed = jnp.zeros(padded.shape[:1] + (row_dev, col_dev) + padded.shape[3:], jnp.float32)
    for tap_row in range(3):
        for tap_col in range(3):
            row_at = 2 - tap_row if flipped else tap_row
            col_at = 2 - tap_col if flipped else tap_col
            summed = (
                summed
                + kernel_f[tap_row * 3 + tap_col]
                * padded[:, row_at : row_at + row_dev, col_at : col_at + col_dev, :]
            )
    return summed


def shards(latents, text, time_embed, cotangent, params, moment_one, moment_two):
    lat_dev, row_dev, col_dev, width = latents.shape
    tokens_dev = row_dev * col_dev
    heads_lin = D // 32
    cross_dim = D // CROSS_HEADS
    score_scale = 1.0 / math.sqrt(cross_dim)
    text_len = text.shape[1]
    segs = lax.axis_size("seq")
    count_dp = lax.axis_size("dp")
    def spread(values):
        joined = jnp.concatenate(values, axis=-1).reshape(-1, sum(v.shape[-1] for v in values))
        whole = lax.all_gather(joined, "seq", axis=0, tiled=True)
        parts = []
        at = 0
        for value in values:
            parts.append(whole[:, at : at + value.shape[-1]])
            at += value.shape[-1]
        return parts

    def collect(values):
        blocks = jnp.stack(
            [
                jnp.concatenate(
                    [
                        value.reshape(-1, value.shape[-1])[
                            :, seg * (value.shape[-1] // segs) : (seg + 1) * (value.shape[-1] // segs)
                        ]
                        for value in values
                    ],
                    axis=1,
                )
                for seg in range(segs)
            ]
        )
        mine = lax.all_to_all(blocks, "seq", split_axis=0, concat_axis=0, tiled=True)
        mine = mine.reshape(-1, mine.shape[-1])
        parts = []
        at = 0
        for value in values:
            width = value.shape[-1] // segs
            parts.append(mine[:, at : at + width])
            at += width
        return parts

    params_rows = params.reshape(-1, LANE)
    shard_low = round_rows(params_rows)
    (
        mod_table,
        w_qkv,
        w_attn_out,
        b_attn_out,
        w_cross_q,
        w_cross_kv,
        w_cross_out,
        b_cross_out,
        w_in,
        b_in,
        w_depth,
        b_depth,
        w_point,
        b_point,
    ) = gather_weights(shard_low, segs)
    modulation = mod_table.astype(jnp.float32)[None] + time_embed.reshape(lat_dev, 6, D)
    shift_one = modulation[:, 0][:, None, :]
    scale_one = modulation[:, 1][:, None, :]
    gate_one = modulation[:, 2][:, None, :]
    shift_two = modulation[:, 3][:, None, :]
    scale_two = modulation[:, 4][:, None, :]
    gate_two = modulation[:, 5][:, None, :]
    tokens = latents.reshape(lat_dev, tokens_dev, D).astype(jnp.float32)
    normed_one, inverse_one = norm_parts(tokens)
    hidden_one = to_low(normed_one * (1.0 + scale_one) + shift_one)
    projected = matmul(hidden_one, w_qkv)
    query_pre = projected[..., :D]
    key_pre = projected[..., D : 2 * D]
    queries = to_low(jnp.maximum(query_pre, 0.0)).reshape(lat_dev, tokens_dev, heads_lin, 32)
    keys_lin = to_low(jnp.maximum(key_pre, 0.0)).reshape(lat_dev, tokens_dev, heads_lin, 32)
    values_lin = to_low(projected[..., 2 * D :]).reshape(lat_dev, tokens_dev, heads_lin, 32)
    state_part = jnp.einsum(
        "lrhd,lrhe->lhde", keys_lin, values_lin, preferred_element_type=jnp.float32
    )
    sum_part = jnp.sum(keys_lin, axis=1, dtype=jnp.float32)
    kv_state, key_sum = state_sum(state_part, sum_part, jnp.float32, 2)
    query_f = queries.astype(jnp.float32)
    numerator = jnp.einsum("lrhd,lhde->lrhe", query_f, kv_state, precision=precise)
    denominator = jnp.einsum("lrhd,lhd->lrh", query_f, key_sum, precision=precise) + eps_linear
    attn_val = numerator / denominator[..., None]
    attended = to_low(attn_val.reshape(lat_dev, tokens_dev, D))
    branch_one = matmul(attended, w_attn_out) + b_attn_out.astype(jnp.float32)
    after_attn = tokens + gate_one * branch_one
    after_low = to_low(after_attn)
    query_c = to_low(matmul(after_low, w_cross_q)).reshape(
        lat_dev, tokens_dev, CROSS_HEADS, cross_dim
    )
    keyval = to_low(matmul(text, w_cross_kv))
    keys_c = keyval[..., :D].reshape(lat_dev, text_len, CROSS_HEADS, cross_dim)
    values_c = keyval[..., D:].reshape(lat_dev, text_len, CROSS_HEADS, cross_dim)
    scores = (
        jnp.einsum("lrhc,lthc->lhrt", query_c, keys_c, preferred_element_type=jnp.float32)
        * score_scale
    )
    row_peak = jnp.max(scores, axis=-1, keepdims=True)
    log_total = row_peak + jnp.log(jnp.sum(jnp.exp(scores - row_peak), axis=-1, keepdims=True))
    probs_low = to_low(jnp.exp(scores - log_total))
    cross_mixed = to_low(
        jnp.einsum(
            "lhrt,lthc->lrhc", probs_low, values_c, preferred_element_type=jnp.float32
        ).reshape(lat_dev, tokens_dev, D)
    )
    after_cross = after_attn + matmul(cross_mixed, w_cross_out) + b_cross_out.astype(jnp.float32)
    normed_two, inverse_two = norm_parts(after_cross)
    hidden_two = to_low(normed_two * (1.0 + scale_two) + shift_two)
    inner_pre = matmul(hidden_two, w_in) + b_in.astype(jnp.float32)
    active = to_low(jax.nn.silu(inner_pre)).reshape(lat_dev, row_dev, col_dev, 2 * FF)
    padded = jnp.pad(with_halo(active, (("seq", 1),), 1), ((0, 0), (0, 0), (1, 1), (0, 0)))
    conv_out = (
        depth_conv(padded, w_depth, row_dev, col_dev, False) + b_depth.astype(jnp.float32)
    ).reshape(lat_dev, tokens_dev, 2 * FF)
    up_part = conv_out[..., :FF]
    gate_part = conv_out[..., FF:]
    gated_mix = to_low(up_part * jax.nn.silu(gate_part))
    branch_two = lax.optimization_barrier(
        matmul(gated_mix, w_point) + b_point.astype(jnp.float32)
    )
    output = (after_cross + gate_two * branch_two).astype(jnp.bfloat16).reshape(latents.shape)
    grad_out = cotangent.reshape(lat_dev, tokens_dev, D).astype(jnp.float32)
    grad_gate_two = jnp.sum(grad_out * branch_two, axis=1)
    grad_branch_two = to_low(grad_out * gate_two)
    grad_branch_two, x_qkv, x_attn, x_cross_q, x_cross_out, x_inner = lax.optimization_barrier(
        (
            grad_branch_two,
            *spread([hidden_one, attended, after_low]),
            *spread([cross_mixed, hidden_two]),
        )
    )
    grad_gated = matmul_t(grad_branch_two, w_point)
    grad_up = grad_gated * jax.nn.silu(gate_part)
    grad_gate = grad_gated * up_part * silu_slope(gate_part)
    grad_conv = to_low(jnp.concatenate([grad_up, grad_gate], axis=-1)).reshape(
        lat_dev, row_dev, col_dev, 2 * FF
    )
    grad_b_depth = jnp.sum(grad_conv, axis=(0, 1, 2), dtype=jnp.float32)
    tap_grads = []
    for tap_row in range(3):
        for tap_col in range(3):
            tap_grads.append(
                jnp.einsum(
                    "lrcf,lrcf->f",
                    padded[:, tap_row : tap_row + row_dev, tap_col : tap_col + col_dev],
                    grad_conv,
                    preferred_element_type=jnp.float32,
                )
            )
    grad_w_depth = jnp.stack(tap_grads)
    grad_padded = jnp.pad(with_halo(grad_conv, (("seq", 1),), 1), ((0, 0), (0, 0), (1, 1), (0, 0)))
    grad_active = depth_conv(grad_padded, w_depth, row_dev, col_dev, True).reshape(
        lat_dev, tokens_dev, 2 * FF
    )
    grad_inner = to_low(grad_active * silu_slope(inner_pre))
    grad_inner, x_point = lax.optimization_barrier((grad_inner, *spread([gated_mix])))
    grad_hidden_two = matmul_t(grad_inner, w_in)
    grad_shift_two = jnp.sum(grad_hidden_two, axis=1)
    grad_scale_two = jnp.sum(grad_hidden_two * normed_two, axis=1)
    grad_second = grad_out + norm_back(grad_hidden_two * (1.0 + scale_two), normed_two, inverse_two)
    grad_cross_out = to_low(grad_second)
    grad_mixed = to_low(matmul_t(grad_cross_out, w_cross_out)).reshape(
        lat_dev, tokens_dev, CROSS_HEADS, cross_dim
    )
    scores_again = (
        jnp.einsum("lrhc,lthc->lhrt", query_c, keys_c, preferred_element_type=jnp.float32)
        * score_scale
    )
    probs = jnp.exp(scores_again - log_total)
    grad_probs = jnp.einsum(
        "lrhc,lthc->lhrt", grad_mixed, values_c, preferred_element_type=jnp.float32
    )
    grad_values_c = jnp.einsum(
        "lhrt,lrhc->lthc", to_low(probs), grad_mixed, preferred_element_type=jnp.float32
    )
    grad_scores = to_low(probs * (grad_probs - jnp.sum(probs * grad_probs, axis=-1, keepdims=True)))
    grad_query_c = to_low(
        jnp.einsum("lhrt,lthc->lrhc", grad_scores, keys_c, preferred_element_type=jnp.float32)
        * score_scale
    ).reshape(lat_dev, tokens_dev, D)
    grad_keys_c = (
        jnp.einsum("lhrt,lrhc->lthc", grad_scores, query_c, preferred_element_type=jnp.float32)
        * score_scale
    )
    grad_keyval_part = jnp.concatenate(
        [grad_keys_c.reshape(lat_dev, text_len, D), grad_values_c.reshape(lat_dev, text_len, D)],
        axis=-1,
    )
    grad_keyval_part = grad_keyval_part.reshape(lat_dev, text_len, segs, 2 * D // segs)
    grad_keyval = to_low(
        lax.psum_scatter(
            grad_keyval_part.astype(jnp.bfloat16), "seq", scatter_dimension=2, tiled=True
        ).astype(jnp.float32)
    ).reshape(lat_dev, text_len, 2 * D // segs)
    grad_w_cross_kv = outer_sum(text, grad_keyval)
    grad_first = grad_second + matmul_t(grad_query_c, w_cross_q)
    grad_gate_one = jnp.sum(grad_first * branch_one, axis=1)
    grad_branch_one = to_low(grad_first * gate_one)
    grad_branch_one, y_point, y_inner = lax.optimization_barrier(
        (grad_branch_one, *collect([grad_branch_two, grad_inner]))
    )
    grad_attended = matmul_t(grad_branch_one, w_attn_out).reshape(
        lat_dev, tokens_dev, heads_lin, 32
    )
    grad_numer = grad_attended / denominator[..., None]
    grad_denom = -jnp.sum(grad_attended * attn_val, axis=-1) / denominator
    grad_query = (
        jnp.einsum("lrhe,lhde->lrhd", grad_numer, kv_state, precision=precise)
        + grad_denom[..., None] * key_sum[:, None]
    )
    state_grad_part = jnp.einsum("lrhd,lrhe->lhde", query_f, grad_numer, precision=precise)
    sum_grad_part = jnp.einsum("lrhd,lrh->lhd", query_f, grad_denom, precision=precise)
    state_grad, sum_grad = state_sum(state_grad_part, sum_grad_part, jnp.bfloat16, 3)
    keys_f = keys_lin.astype(jnp.float32)
    values_f = values_lin.astype(jnp.float32)
    grad_keys = (
        jnp.einsum("lrhe,lhde->lrhd", values_f, state_grad, precision=precise) + sum_grad[:, None]
    )
    grad_values = jnp.einsum("lrhd,lhde->lrhe", keys_f, state_grad, precision=precise)
    grad_projected = to_low(
        jnp.concatenate(
            [
                grad_query.reshape(lat_dev, tokens_dev, D) * (query_pre > 0.0),
                grad_keys.reshape(lat_dev, tokens_dev, D) * (key_pre > 0.0),
                grad_values.reshape(lat_dev, tokens_dev, D),
            ],
            axis=-1,
        )
    )
    grad_projected, y_cross_out, y_cross_q, y_attn = lax.optimization_barrier(
        (grad_projected, *collect([grad_cross_out, grad_query_c, grad_branch_one]))
    )
    grad_hidden_one = matmul_t(grad_projected, w_qkv)
    grad_input = grad_first + norm_back(
        grad_hidden_one * (1.0 + scale_one), normed_one, inverse_one
    )
    grad_table = jnp.sum(
        jnp.stack(
            [
                jnp.sum(grad_hidden_one, axis=1),
                jnp.sum(grad_hidden_one * normed_one, axis=1),
                grad_gate_one,
                grad_shift_two,
                grad_scale_two,
                grad_gate_two,
            ],
            axis=1,
        ),
        axis=0,
    )
    grad_table = lax.optimization_barrier(grad_table)
    col_d = D // segs
    col_ff = 2 * FF // segs
    small_parts = jnp.concatenate(
        [
            grad_table.reshape(6, segs, col_d).transpose(1, 0, 2).reshape(segs, -1),
            grad_w_depth.reshape(9, segs, col_ff).transpose(1, 0, 2).reshape(segs, -1),
            grad_b_depth.reshape(segs, col_ff),
        ],
        axis=1,
    ).astype(jnp.bfloat16)
    small_parts = small_parts.reshape(segs, -1, LANE)
    small_mine = (
        lax.psum_scatter(small_parts, "seq", scatter_dimension=0, tiled=True)
        .astype(jnp.float32)
        .reshape(-1)
    )
    table_q = small_mine[: 6 * col_d].reshape(6, col_d)
    depth_q = small_mine[6 * col_d : 6 * col_d + 9 * col_ff].reshape(9, col_ff)
    depth_bias_q = small_mine[6 * col_d + 9 * col_ff :].reshape(1, col_ff)

    (y_qkv,) = collect([grad_projected])
    grad_w_qkv = outer_sum(x_qkv, y_qkv)
    grad_w_attn_out = outer_sum(x_attn, y_attn)
    grad_w_cross_q = outer_sum(x_cross_q, y_cross_q)
    grad_w_cross_out = outer_sum(x_cross_out, y_cross_out)
    grad_w_in = outer_sum(x_inner, y_inner)
    grad_w_point = outer_sum(x_point, y_point)
    grad_b_attn_out = jnp.sum(y_attn, axis=0, dtype=jnp.float32)
    grad_b_cross_out = jnp.sum(y_cross_out, axis=0, dtype=jnp.float32)
    grad_b_in = jnp.sum(y_inner, axis=0, dtype=jnp.float32)
    grad_b_point = jnp.sum(y_point, axis=0, dtype=jnp.float32)
    bias_part = jnp.concatenate(
        [grad_b_attn_out, grad_b_cross_out, grad_b_in, depth_bias_q.ravel(), grad_b_point]
    )
    len_bias = bias_part.size
    bias_rows = -(-bias_part.size // (8 * LANE)) * 8
    bias_part = jnp.pad(bias_part, (0, bias_rows * LANE - bias_part.size)).reshape(-1, LANE)
    quarter_grad = write_flat(
        segs,
        [
            table_q,
            grad_w_qkv,
            grad_w_attn_out,
            grad_b_attn_out,
            grad_w_cross_q,
            grad_w_cross_kv,
            grad_w_cross_out,
            grad_b_cross_out,
            grad_w_in,
            grad_b_in,
            depth_q,
            depth_bias_q,
            grad_w_point,
            grad_b_point,
        ],
    )
    grad_shard = lax.psum_scatter(
        quarter_grad.reshape(count_dp, -1, LANE), "dp", scatter_dimension=0, tiled=True
    ).reshape(-1, LANE)
    *flat_outs, bias_grads = finish(
        grad_shard,
        bias_part,
        params_rows,
        moment_one.reshape(-1, LANE),
        moment_two.reshape(-1, LANE),
    )
    gradient, moment_one_new, moment_two_new, update = [
        value.reshape(params.shape) for value in flat_outs
    ]
    return (
        output,
        grad_input.reshape(latents.shape),
        gradient,
        moment_one_new,
        moment_two_new,
        update,
        bias_grads.reshape(1, -1)[:, :len_bias],
    )


def solution(mesh):
    return jax.shard_map(
        shards,
        mesh=mesh,
        in_specs=(
            P("dp", "seq", None, None),
            P("dp", None, None),
            P("dp", None),
            P("dp", "seq", None, None),
            P("seq", "dp"),
            P("seq", "dp"),
            P("seq", "dp"),
        ),
        out_specs=(
            P("dp", "seq", None, None),
            P("dp", "seq", None, None),
            P("seq", "dp"),
            P("seq", "dp"),
            P("seq", "dp"),
            P("seq", "dp"),
            P("seq", None),
        ),
        check_vma=False,
    )
```

```python
import math

import jax
import jax.numpy as jnp
from jax import lax
from jax.experimental import pallas as pl
from jax.experimental.pallas import tpu as pltpu
from jax.sharding import PartitionSpec as P

D = 1152
FF = 2880
CROSS_HEADS = 16


precise = lax.Precision.HIGHEST
eps_norm = 1e-06
eps_linear = 1e-06
beta_first = 0.9
beta_second = 0.95
adam_eps = 1e-08
weight_decay = 0.01
adam_steps = 100.0


def with_halo(block, sides, width):
    for axis, dim in sides:
        count = lax.axis_size(axis)
        forward = [(i, i + 1) for i in range(count - 1)]
        backward = [(target, source) for source, target in forward]
        low = lax.ppermute(
            lax.slice_in_dim(block, block.shape[dim] - width, None, axis=dim), axis, forward
        )
        high = lax.ppermute(lax.slice_in_dim(block, 0, width, axis=dim), axis, backward)
        block = jnp.concatenate([low, block, high], axis=dim)
    return block


def piece_specs():
    return [
        (6, D, False),
        (D, 3 * D, False),
        (D, D, False),
        (1, D, True),
        (D, D, False),
        (D, 2 * D, False),
        (D, D, False),
        (1, D, True),
        (D, 2 * FF, False),
        (1, 2 * FF, True),
        (9, 2 * FF, False),
        (1, 2 * FF, True),
        (FF, D, False),
        (1, D, True),
    ]


LANE = 128
UNIT = 32


def merge_units(values, lane_unit):
    out = values[0]
    last = values[0]
    for position in range(1, 4):
        if values[position] is not last:
            out = jnp.where(lane_unit >= position, values[position], out)
            last = values[position]
    return out


def rolled(value, units):
    units = units % 4
    return value if units == 0 else pltpu.roll(value, units * UNIT, 1)


def matrix_rows(count_rows):
    return 192 if count_rows % 192 == 0 else 64


def read_matrix(flat, offset, rows_of, cols_of, segs):
    total_rows = flat.shape[1]
    per_row = cols_of // segs // UNIT
    unit_at = offset // UNIT
    block = matrix_rows(rows_of)
    base = unit_at // 4 // 16 * 16
    shift = unit_at - 4 * base
    step = block * per_row // 4
    need = (shift + block * per_row - 1) // 4 + 1
    need = -(-need // 16) * 16
    assert base + (rows_of // block - 1) * step + need <= total_rows
    tiles = cols_of // LANE

    def kernel(in_ref, out_ref, wide, mixed):
        def widen(at, _):
            row = pl.multiple_of(at * 16, 16)
            for seg in range(segs):
                wide[pl.ds(pl.multiple_of(seg * need + row, 16), 16), :] = in_ref[
                    seg, pl.ds(row, 16), :
                ].astype(jnp.float32)
            return 0

        lax.fori_loop(0, need // 16, widen, 0, unroll=8)
        lane_unit = lax.broadcasted_iota(jnp.int32, (8, LANE), 1) // UNIT

        def group(at, _):
            for phase in range(4):
                loaded = {}
                turned = {}
                for tile in range(tiles):
                    parts = []
                    for slot in range(4):
                        col = 4 * tile + slot
                        seg, unit = col // per_row, col % per_row
                        source = shift + phase * per_row + unit
                        key = (seg, source // 4)
                        if key not in loaded:
                            loaded[key] = wide[
                                pl.ds(seg * need + key[1] + at * (8 * per_row), 8, stride=per_row),
                                :,
                            ]
                        turn = (slot - source) % 4
                        if (key, turn) not in turned:
                            turned[key, turn] = rolled(loaded[key], turn)
                        parts.append(turned[key, turn])
                    mixed[pl.ds(tile * block + phase + at * 32, 8, stride=4), :] = merge_units(
                        parts, lane_unit
                    )
            return 0

        lax.fori_loop(0, block // 32, group, 0, unroll=2)

        def narrow(at, _):
            row = pl.multiple_of(at * 16, 16)
            for tile in range(tiles):
                out_ref[pl.ds(row, 16), tile * LANE : (tile + 1) * LANE] = mixed[
                    pl.ds(pl.multiple_of(tile * block + row, 16), 16), :
                ].astype(jnp.bfloat16)
            return 0

        lax.fori_loop(0, block // 16, narrow, 0, unroll=2)

    return pl.pallas_call(
        kernel,
        grid=(rows_of // block,),
        in_specs=[
            pl.BlockSpec(
                (pl.Element(segs), pl.Element(need), pl.Element(LANE)),
                lambda at: (0, pl.multiple_of(base + at * step, 16), 0),
            )
        ],
        out_specs=pl.BlockSpec((block, cols_of), lambda at: (at, 0)),
        out_shape=jax.ShapeDtypeStruct((rows_of, cols_of), jnp.bfloat16),
        scratch_shapes=[
            pltpu.VMEM((segs * need, LANE), jnp.float32),
            pltpu.VMEM((tiles * block, LANE), jnp.float32),
        ],
        compiler_params=pltpu.CompilerParams(vmem_limit_bytes=48 << 20),
        cost_estimate=pl.CostEstimate(
            flops=0, bytes_accessed=4 * rows_of * cols_of, transcendentals=0
        ),
        name="read_matrix",
    )(flat)


def write_flat(segs, parts):
    specs = piece_specs()
    block_rows = 192
    total = sum(rows_of * cols_of // segs for rows_of, cols_of, _ in specs)
    flat_rows = total // LANE
    places = []
    offset = 0
    big, small = [], []
    for (rows_of, cols_of, _), value in zip(specs, parts):
        width = cols_of // segs
        length = rows_of * width
        if rows_of > 9:
            assert rows_of % block_rows == 0
            places.append((True, offset, rows_of, width, len(big)))
            big.append(value)
        else:
            lead = offset % LANE
            rest = -(lead + length) % LANE
            padded = jnp.pad(value.reshape(-1), (lead, rest)).reshape(-1, LANE)
            places.append((False, offset, length, None, len(small)))
            small.append(padded)
        offset += length
    widths = sorted({place[3] for place in places if place[0]})
    chunk = 144

    def kernel(*refs):
        big_refs = refs[: len(big)]
        small_refs = refs[len(big) : len(big) + len(small)]
        out_ref = refs[len(big) + len(small)]
        flat = refs[len(big) + len(small) + 1]
        bufs = refs[len(big) + len(small) + 2 : len(big) + len(small) + 2 + len(widths)]
        in_sem = refs[-1]
        lane_unit = lax.broadcasted_iota(jnp.int32, (8, LANE), 1) // UNIT
        row_unit = lax.broadcasted_iota(jnp.int32, (1, LANE), 1) // UNIT

        def place_small(ref, offset, length):
            first = offset // LANE
            last = (offset + length - 1) // LANE
            lead = offset % LANE // UNIT
            tail = (offset + length) % LANE // UNIT
            count = last - first + 1
            if count > 2:

                def copy_row(at, _):
                    flat[pl.ds(first + 1 + at, 1), :] = ref[pl.ds(1 + at, 1), :]
                    return 0

                lax.fori_loop(0, count - 2, copy_row, 0)
            keep = row_unit >= lead
            if count == 1 and tail:
                keep = keep & (row_unit < tail)
            flat[first : first + 1, :] = jnp.where(keep, ref[0:1, :], flat[first : first + 1, :])
            if count > 1:
                flat[last : last + 1, :] = (
                    jnp.where(
                        row_unit < tail, ref[count - 1 : count, :], flat[last : last + 1, :]
                    )
                    if tail
                    else ref[count - 1 : count, :]
                )

        def fetch_block(ref, buf, width, at, slot):
            row = pl.multiple_of(at * block_rows, 64)
            return [
                pltpu.make_async_copy(
                    ref.at[pl.ds(row, block_rows), tile * LANE : (tile + 1) * LANE],
                    buf.at[slot, tile],
                    in_sem.at[widths.index(width), slot, tile],
                )
                for tile in range(-(-width // LANE))
            ]

        def place_big(ref, buf, offset, rows_of, width):
            per_row = width // UNIT
            first = offset // LANE
            shift = offset % LANE // UNIT
            block = block_rows
            blocks = rows_of // block

            def fetch(at, slot):
                return fetch_block(ref, buf, width, at, slot)

            def one_block(at, _):
                slot = lax.rem(at, 2)

                @pl.when(at + 1 < blocks)
                def _():
                    for copy in fetch(at + 1, 1 - slot):
                        copy.start()

                for copy in fetch(at, slot):
                    copy.wait()

                def group(sub, _):
                    loaded = {}
                    turned = {}

                    def unit_value(phase, unit, lane):
                        key = (phase, unit // 4)
                        if key not in loaded:
                            loaded[key] = buf[
                                slot, key[1], pl.ds(phase + sub * 32, 8, stride=4), :
                            ]
                        turn = (lane - unit) % 4
                        if (key, turn) not in turned:
                            turned[key, turn] = rolled(loaded[key], turn)
                        return turned[key, turn]

                    start = first + (at * (block // 4) + sub * 8) * per_row
                    for row in range(per_row + (1 if shift else 0)):
                        where = pl.ds(start + row, 8, stride=per_row)
                        parts = []
                        kept = None
                        for lane in range(4):
                            unit = 4 * row + lane - shift
                            if unit < 0 or unit >= 4 * per_row:
                                if kept is None:
                                    kept = flat[where, :]
                                parts.append(kept)
                            else:
                                parts.append(unit_value(unit // per_row, unit % per_row, lane))
                        flat[where, :] = merge_units(parts, lane_unit)
                    return 0

                lax.fori_loop(0, block // 32, group, 0, unroll=3)
                return 0

            lax.fori_loop(0, blocks, one_block, 0)

        def first_fetch(width, after):
            for is_big, _, _, other, index in places:
                if is_big and other == width and index > after:
                    buf = bufs[widths.index(width)]
                    for copy in fetch_block(big_refs[index], buf, width, 0, 0):
                        copy.start()
                    return

        for width in widths:
            first_fetch(width, -1)
        for is_big, offset, rows_of, width, index in places:
            if is_big:
                place_big(big_refs[index], bufs[widths.index(width)], offset, rows_of, width)
                first_fetch(width, index)
            else:
                place_small(small_refs[index], offset, rows_of)

        def narrow(at, _):
            where = pl.ds(pl.multiple_of(at * chunk, 16), chunk)
            out_ref[where, :] = flat[where, :].astype(jnp.bfloat16)
            return 0

        lax.fori_loop(0, flat_rows // chunk, narrow, 0)

    return pl.pallas_call(
        kernel,
        in_specs=[pl.BlockSpec(memory_space=pl.ANY)] * len(big)
        + [pl.BlockSpec(memory_space=pltpu.VMEM)] * len(small),
        out_specs=pl.BlockSpec(memory_space=pltpu.VMEM),
        out_shape=jax.ShapeDtypeStruct((flat_rows, LANE), jnp.bfloat16),
        scratch_shapes=[pltpu.VMEM((flat_rows, LANE), jnp.float32)]
        + [
            pltpu.VMEM((2, -(-width // LANE), block_rows, LANE), jnp.float32) for width in widths
        ]
        + [
            pltpu.SemaphoreType.DMA((len(widths), 2, -(-widths[-1] // LANE))),
        ],
        compiler_params=pltpu.CompilerParams(vmem_limit_bytes=56 << 20),
        cost_estimate=pl.CostEstimate(flops=0, bytes_accessed=6 * total, transcendentals=0),
        name="write_flat",
    )(*big, *small)


def round_rows(values):
    def kernel(in_ref, out_ref):
        out_ref[...] = in_ref[...].astype(jnp.bfloat16)

    return pl.pallas_call(
        kernel,
        in_specs=[pl.BlockSpec(memory_space=pltpu.VMEM)],
        out_specs=pl.BlockSpec(memory_space=pltpu.VMEM),
        out_shape=jax.ShapeDtypeStruct(values.shape, jnp.bfloat16),
        name="round_rows",
    )(values)


def gather_weights(shard_low, segs):
    whole = lax.all_gather(shard_low, ("seq", "dp"), axis=0, tiled=True)
    flat = whole.reshape(segs, -1, LANE)
    pieces = []
    offset = 0
    for rows_of, cols_of, vector in piece_specs():
        length = rows_of * cols_of // segs
        if rows_of > 9:
            pieces.append(read_matrix(flat, offset, rows_of, cols_of, segs))
        else:
            first, last = offset // LANE, -(-(offset + length) // LANE)
            lead = offset - first * LANE
            block = flat[:, first:last].reshape(segs, -1)[:, lead : lead + length]
            block = block.reshape(segs, rows_of, cols_of // segs).transpose(1, 0, 2)
            pieces.append(block.reshape(cols_of) if vector else block.reshape(rows_of, cols_of))
        offset = offset + length
    return pieces


MESH = pl.DeviceIdType.MESH


def peer_barrier(groups):
    barrier = pltpu.get_barrier_semaphore()
    total = 0
    for axis, count in groups:
        me = lax.axis_index(axis)
        for step in range(1, count):
            pl.semaphore_signal(
                barrier, inc=1, device_id={axis: lax.rem(me + step, count)}, device_id_type=MESH
            )
        total += count - 1
    pl.semaphore_wait(barrier, total)


def exchange(axis, count, source, slots, send_sem, recv_sem):
    me = lax.axis_index(axis)
    for step in range(1, count):
        pltpu.make_async_remote_copy(
            src_ref=source,
            dst_ref=slots.at[me],
            send_sem=send_sem.at[step - 1],
            recv_sem=recv_sem.at[me],
            device_id={axis: lax.rem(me + step, count)},
            device_id_type=MESH,
        ).start()


def exchange_wait(axis, count, source, slots, send_sem, recv_sem):
    me = lax.axis_index(axis)
    for step in range(1, count):
        peer = lax.rem(me + step, count)
        copy = pltpu.make_async_remote_copy(
            src_ref=source,
            dst_ref=slots.at[peer],
            send_sem=send_sem.at[step - 1],
            recv_sem=recv_sem.at[peer],
            device_id={axis: peer},
            device_id_type=MESH,
        )
        copy.wait_send()
        copy.wait_recv()


def in_order(axis, count, own, slots):
    me = lax.axis_index(axis)
    total = None
    for index in range(count):
        term = jnp.where(me == index, own, slots[index].astype(jnp.float32))
        total = term if total is None else total + term
    return total


def seq_sum(block, collective_id):
    count = lax.axis_size("seq")

    def kernel(in_ref, out_ref, slots, send_sem, recv_sem):
        peer_barrier([("seq", count)])
        exchange("seq", count, in_ref, slots, send_sem, recv_sem)
        exchange_wait("seq", count, in_ref, slots, send_sem, recv_sem)
        out_ref[...] = in_order("seq", count, in_ref[...].astype(jnp.float32), slots)

    return pl.pallas_call(
        kernel,
        in_specs=[pl.BlockSpec(memory_space=pltpu.VMEM)],
        out_specs=pl.BlockSpec(memory_space=pltpu.VMEM),
        out_shape=jax.ShapeDtypeStruct(block.shape, jnp.float32),
        scratch_shapes=[
            pltpu.VMEM((count,) + block.shape, block.dtype),
            pltpu.SemaphoreType.DMA((count - 1,)),
            pltpu.SemaphoreType.DMA((count,)),
        ],
        compiler_params=pltpu.CompilerParams(collective_id=collective_id, has_side_effects=True),
        name="seq_sum",
    )(block)


def state_sum(state, sums, kind, collective_id):
    heads = state.shape[1]
    flat = jnp.concatenate(
        [state.reshape(-1, LANE), jnp.pad(sums.reshape(-1), (0, -sums.size % LANE)).reshape(-1, LANE)]
    ).astype(kind)
    rows = flat.shape[0]
    flat = jnp.pad(flat, ((0, -rows % 16), (0, 0)))
    total = seq_sum(flat, collective_id)
    split = state.size // LANE
    return (
        total[:split].reshape(state.shape),
        total[split:].reshape(-1)[: sums.size].reshape(1, heads, -1),
    )


def reduce_shard(flat):
    rows = flat.shape[0] // 8
    pieces = 3
    part = rows // pieces
    step = 80

    def kernel(in_ref, out_ref, recv_x, send_z, recv_z, x_send, x_recv, z_send, z_recv):
        me = lax.axis_index("dp")
        near = lax.rem(me, 2)
        far = lax.div(me, 2)
        partner = me + 1 - 2 * near

        def far_of(shift):
            return lax.rem(far + shift, 4)

        barrier = pltpu.get_barrier_semaphore()
        pl.semaphore_signal(barrier, inc=1, device_id={"dp": partner}, device_id_type=MESH)
        for shift in range(1, 4):
            pl.semaphore_signal(
                barrier,
                inc=1,
                device_id={"dp": 2 * far_of(shift) + near},
                device_id_type=MESH,
            )
        pl.semaphore_wait(barrier, 4)

        def window(shard, piece):
            return pl.ds(pl.multiple_of(shard * rows + piece * part, 16), part)

        def x_copy(shift, piece):
            return pltpu.make_async_remote_copy(
                src_ref=in_ref.at[window(2 * far_of(shift) + 1 - near, piece), :],
                dst_ref=recv_x.at[shift, pl.ds(piece * part, part), :],
                send_sem=x_send.at[shift, piece],
                recv_sem=x_recv.at[shift, piece],
                device_id={"dp": partner},
                device_id_type=MESH,
            )

        def z_copy(shift, piece):
            return pltpu.make_async_remote_copy(
                src_ref=send_z.at[shift - 1, pl.ds(piece * part, part), :],
                dst_ref=recv_z.at[shift - 1, pl.ds(piece * part, part), :],
                send_sem=z_send.at[shift - 1, piece],
                recv_sem=z_recv.at[shift - 1, piece],
                device_id={"dp": 2 * far_of(shift) + near},
                device_id_type=MESH,
            )

        order = (1, 2, 3, 0)
        for shift in order:
            for piece in range(pieces):
                x_copy(shift, piece).start()

        def own_sum(shift, row, at):
            start = (2 * far_of(shift) + near) * rows + row + at * step
            own = in_ref[pl.ds(pl.multiple_of(start, 16), step), :]
            other = recv_x[shift, pl.ds(pl.multiple_of(row + at * step, 16), step), :]
            return own.astype(jnp.float32) + other.astype(jnp.float32)

        for shift in order:
            for piece in range(pieces):
                x_copy(shift, piece).wait_recv()
                row = piece * part

                def add(at, _, shift=shift, row=row):
                    where = pl.ds(pl.multiple_of(row + at * step, 16), step)
                    total = own_sum(shift, row, at)
                    if shift:
                        send_z[shift - 1, where, :] = total.astype(jnp.bfloat16)
                    else:
                        out_ref[where, :] = total
                    return 0

                lax.fori_loop(0, part // step, add, 0)
                if shift:
                    z_copy(shift, piece).start()
        for shift in range(1, 4):
            for piece in range(pieces):
                z_copy(shift, piece).wait_recv()
                row = piece * part

                def gather(at, _, shift=shift, row=row):
                    where = pl.ds(pl.multiple_of(row + at * step, 16), step)
                    out_ref[where, :] = out_ref[where, :] + recv_z[shift - 1, where, :].astype(
                        jnp.float32
                    )
                    return 0

                lax.fori_loop(0, part // step, gather, 0)
        for shift in range(4):
            for piece in range(pieces):
                x_copy(shift, piece).wait_send()
                if shift:
                    z_copy(shift, piece).wait_send()

    block = (rows, LANE)
    return pl.pallas_call(
        kernel,
        in_specs=[pl.BlockSpec(memory_space=pltpu.VMEM)],
        out_specs=pl.BlockSpec(memory_space=pltpu.VMEM),
        out_shape=jax.ShapeDtypeStruct(block, jnp.float32),
        scratch_shapes=[
            pltpu.VMEM((4,) + block, jnp.bfloat16),
            pltpu.VMEM((3,) + block, jnp.bfloat16),
            pltpu.VMEM((3,) + block, jnp.bfloat16),
            pltpu.SemaphoreType.DMA((4, pieces)),
            pltpu.SemaphoreType.DMA((4, pieces)),
            pltpu.SemaphoreType.DMA((3, pieces)),
            pltpu.SemaphoreType.DMA((3, pieces)),
        ],
        compiler_params=pltpu.CompilerParams(
            collective_id=4, has_side_effects=True, vmem_limit_bytes=40 << 20
        ),
        name="reduce_shard",
    )(flat)


def finish(grad_shard, bias_part, params, moment_one, moment_two):
    rows = grad_shard.shape[0]
    count_dp = lax.axis_size("dp")
    count_seq = lax.axis_size("seq")
    entries = rows * LANE * count_dp * count_seq
    chunk = 48 if rows % 48 == 0 else rows
    bias_rows = bias_part.shape[0]

    def kernel(
        grad_ref,
        bias_ref,
        param_ref,
        one_ref,
        two_ref,
        gradient_ref,
        one_out,
        two_out,
        update_ref,
        bias_out,
        square,
        square_dp,
        square_seq,
        partial,
        bias_slots,
        send_bias,
        recv_bias,
        send_dp,
        recv_dp,
        send_seq,
        recv_seq,
    ):
        peer_barrier([("dp", count_dp), ("seq", count_seq)])
        exchange("dp", count_dp, bias_ref, bias_slots, send_bias, recv_bias)

        def squares(at, total):
            part = grad_ref[pl.ds(at * chunk, chunk), :].astype(jnp.float32)
            return total + jnp.sum(part * part, axis=0, keepdims=True)

        total = lax.fori_loop(0, rows // chunk, squares, jnp.zeros((1, LANE), jnp.float32))
        square[...] = jnp.broadcast_to(total, (8, LANE))
        exchange("dp", count_dp, square, square_dp, send_dp, recv_dp)
        exchange_wait("dp", count_dp, square, square_dp, send_dp, recv_dp)
        partial[...] = in_order("dp", count_dp, square[...], square_dp)
        exchange("seq", count_seq, partial, square_seq, send_seq, recv_seq)
        exchange_wait("seq", count_seq, partial, square_seq, send_seq, recv_seq)
        whole = jnp.sum(
            in_order("seq", count_seq, partial[...], square_seq)[0:1], axis=1, keepdims=True
        )
        factor = lax.rsqrt(whole / entries + 1e-06)
        exchange_wait("dp", count_dp, bias_ref, bias_slots, send_bias, recv_bias)
        bias_out[...] = in_order("dp", count_dp, bias_ref[...], bias_slots) * factor

        def step(at, _):
            where = pl.ds(at * chunk, chunk)
            gradient = grad_ref[where, :].astype(jnp.float32) * factor
            first = beta_first * one_ref[where, :] + (1.0 - beta_first) * gradient
            second = beta_second * two_ref[where, :] + (1.0 - beta_second) * gradient * gradient
            gradient_ref[where, :] = gradient
            one_out[where, :] = first
            two_out[where, :] = second
            first_hat = first / (1.0 - beta_first**adam_steps)
            second_hat = second / (1.0 - beta_second**adam_steps)
            update_ref[where, :] = (
                first_hat / (jnp.sqrt(second_hat) + adam_eps) + weight_decay * param_ref[where, :]
            )
            return 0

        lax.fori_loop(0, rows // chunk, step, 0)

    flat = jax.ShapeDtypeStruct((rows, LANE), jnp.float32)
    tile = (8, LANE)
    return pl.pallas_call(
        kernel,
        in_specs=[pl.BlockSpec(memory_space=pltpu.VMEM)] * 5,
        out_specs=[pl.BlockSpec(memory_space=pltpu.VMEM)] * 5,
        out_shape=[flat] * 4 + [jax.ShapeDtypeStruct((bias_rows, LANE), jnp.float32)],
        scratch_shapes=[
            pltpu.VMEM(tile, jnp.float32),
            pltpu.VMEM((count_dp,) + tile, jnp.float32),
            pltpu.VMEM((count_seq,) + tile, jnp.float32),
            pltpu.VMEM(tile, jnp.float32),
            pltpu.VMEM((count_dp, bias_rows, LANE), jnp.float32),
            pltpu.SemaphoreType.DMA((count_dp - 1,)),
            pltpu.SemaphoreType.DMA((count_dp,)),
            pltpu.SemaphoreType.DMA((count_dp - 1,)),
            pltpu.SemaphoreType.DMA((count_dp,)),
            pltpu.SemaphoreType.DMA((count_seq - 1,)),
            pltpu.SemaphoreType.DMA((count_seq,)),
        ],
        compiler_params=pltpu.CompilerParams(
            collective_id=1, has_side_effects=True, vmem_limit_bytes=48 << 20
        ),
        name="finish",
    )(grad_shard, bias_part, params, moment_one, moment_two)


def norm_parts(values):
    centred = values - jnp.mean(values, axis=-1, keepdims=True)
    inverse = lax.rsqrt(jnp.mean(centred * centred, axis=-1, keepdims=True) + eps_norm)
    return (centred * inverse, inverse)


def norm_back(grad_normed, normed, inverse):
    return inverse * (
        grad_normed
        - jnp.mean(grad_normed, axis=-1, keepdims=True)
        - normed * jnp.mean(grad_normed * normed, axis=-1, keepdims=True)
    )


def silu_slope(values):
    sigmoid_v = jax.nn.sigmoid(values)
    return sigmoid_v * (1.0 + values * (1.0 - sigmoid_v))


def to_low(values):
    return values.astype(jnp.bfloat16)


def matmul(left_op, right_op):
    return jnp.dot(left_op, right_op, preferred_element_type=jnp.float32)


def matmul_t(left_op, right_op):
    return lax.dot_general(
        left_op,
        right_op,
        (((left_op.ndim - 1,), (1,)), ((), ())),
        preferred_element_type=jnp.float32,
    )


def outer_sum(left_op, right_op):
    left_flat = left_op.reshape(-1, left_op.shape[-1])
    right_flat = right_op.reshape(-1, right_op.shape[-1])
    right_flat = jnp.pad(right_flat, ((0, 0), (0, -right_flat.shape[1] % LANE)))
    return lax.dot_general(
        left_flat, right_flat, (((0,), (0,)), ((), ())), preferred_element_type=jnp.float32
    )


def depth_conv(padded, kernel, row_dev, col_dev, flipped):
    kernel_f = kernel.astype(jnp.float32)
    summed = jnp.zeros(padded.shape[:1] + (row_dev, col_dev) + padded.shape[3:], jnp.float32)
    for tap_row in range(3):
        for tap_col in range(3):
            row_at = 2 - tap_row if flipped else tap_row
            col_at = 2 - tap_col if flipped else tap_col
            summed = (
                summed
                + kernel_f[tap_row * 3 + tap_col]
                * padded[:, row_at : row_at + row_dev, col_at : col_at + col_dev, :]
            )
    return summed


def shards(latents, text, time_embed, cotangent, params, moment_one, moment_two):
    lat_dev, row_dev, col_dev, width = latents.shape
    tokens_dev = row_dev * col_dev
    heads_lin = D // 32
    cross_dim = D // CROSS_HEADS
    score_scale = 1.0 / math.sqrt(cross_dim)
    text_len = text.shape[1]
    segs = lax.axis_size("seq")
    count_dp = lax.axis_size("dp")
    def spread(values):
        joined = jnp.concatenate(values, axis=-1).reshape(-1, sum(v.shape[-1] for v in values))
        whole = lax.all_gather(joined, "seq", axis=0, tiled=True)
        parts = []
        at = 0
        for value in values:
            parts.append(whole[:, at : at + value.shape[-1]])
            at += value.shape[-1]
        return parts

    def collect(values):
        blocks = jnp.stack(
            [
                jnp.concatenate(
                    [
                        value.reshape(-1, value.shape[-1])[
                            :, seg * (value.shape[-1] // segs) : (seg + 1) * (value.shape[-1] // segs)
                        ]
                        for value in values
                    ],
                    axis=1,
                )
                for seg in range(segs)
            ]
        )
        mine = lax.all_to_all(blocks, "seq", split_axis=0, concat_axis=0, tiled=True)
        mine = mine.reshape(-1, mine.shape[-1])
        parts = []
        at = 0
        for value in values:
            width = value.shape[-1] // segs
            parts.append(mine[:, at : at + width])
            at += width
        return parts

    params_rows = params.reshape(-1, LANE)
    shard_low = round_rows(params_rows)
    (
        mod_table,
        w_qkv,
        w_attn_out,
        b_attn_out,
        w_cross_q,
        w_cross_kv,
        w_cross_out,
        b_cross_out,
        w_in,
        b_in,
        w_depth,
        b_depth,
        w_point,
        b_point,
    ) = gather_weights(shard_low, segs)
    modulation = mod_table.astype(jnp.float32)[None] + time_embed.reshape(lat_dev, 6, D)
    shift_one = modulation[:, 0][:, None, :]
    scale_one = modulation[:, 1][:, None, :]
    gate_one = modulation[:, 2][:, None, :]
    shift_two = modulation[:, 3][:, None, :]
    scale_two = modulation[:, 4][:, None, :]
    gate_two = modulation[:, 5][:, None, :]
    tokens = latents.reshape(lat_dev, tokens_dev, D).astype(jnp.float32)
    normed_one, inverse_one = norm_parts(tokens)
    hidden_one = to_low(normed_one * (1.0 + scale_one) + shift_one)
    projected = matmul(hidden_one, w_qkv)
    query_pre = projected[..., :D]
    key_pre = projected[..., D : 2 * D]
    queries = to_low(jnp.maximum(query_pre, 0.0)).reshape(lat_dev, tokens_dev, heads_lin, 32)
    keys_lin = to_low(jnp.maximum(key_pre, 0.0)).reshape(lat_dev, tokens_dev, heads_lin, 32)
    values_lin = to_low(projected[..., 2 * D :]).reshape(lat_dev, tokens_dev, heads_lin, 32)
    state_part = jnp.einsum(
        "lrhd,lrhe->lhde", keys_lin, values_lin, preferred_element_type=jnp.float32
    )
    sum_part = jnp.sum(keys_lin, axis=1, dtype=jnp.float32)
    kv_state, key_sum = state_sum(state_part, sum_part, jnp.float32, 2)
    query_f = queries.astype(jnp.float32)
    numerator = jnp.einsum("lrhd,lhde->lrhe", query_f, kv_state, precision=precise)
    denominator = jnp.einsum("lrhd,lhd->lrh", query_f, key_sum, precision=precise) + eps_linear
    attn_val = numerator / denominator[..., None]
    attended = to_low(attn_val.reshape(lat_dev, tokens_dev, D))
    branch_one = matmul(attended, w_attn_out) + b_attn_out.astype(jnp.float32)
    after_attn = tokens + gate_one * branch_one
    after_low = to_low(after_attn)
    query_c = to_low(matmul(after_low, w_cross_q)).reshape(
        lat_dev, tokens_dev, CROSS_HEADS, cross_dim
    )
    keyval = to_low(matmul(text, w_cross_kv))
    keys_c = keyval[..., :D].reshape(lat_dev, text_len, CROSS_HEADS, cross_dim)
    values_c = keyval[..., D:].reshape(lat_dev, text_len, CROSS_HEADS, cross_dim)
    scores = (
        jnp.einsum("lrhc,lthc->lhrt", query_c, keys_c, preferred_element_type=jnp.float32)
        * score_scale
    )
    row_peak = jnp.max(scores, axis=-1, keepdims=True)
    log_total = row_peak + jnp.log(jnp.sum(jnp.exp(scores - row_peak), axis=-1, keepdims=True))
    probs_low = to_low(jnp.exp(scores - log_total))
    cross_mixed = to_low(
        jnp.einsum(
            "lhrt,lthc->lrhc", probs_low, values_c, preferred_element_type=jnp.float32
        ).reshape(lat_dev, tokens_dev, D)
    )
    after_cross = after_attn + matmul(cross_mixed, w_cross_out) + b_cross_out.astype(jnp.float32)
    normed_two, inverse_two = norm_parts(after_cross)
    hidden_two = to_low(normed_two * (1.0 + scale_two) + shift_two)
    inner_pre = matmul(hidden_two, w_in) + b_in.astype(jnp.float32)
    active = to_low(jax.nn.silu(inner_pre)).reshape(lat_dev, row_dev, col_dev, 2 * FF)
    padded = jnp.pad(with_halo(active, (("seq", 1),), 1), ((0, 0), (0, 0), (1, 1), (0, 0)))
    conv_out = (
        depth_conv(padded, w_depth, row_dev, col_dev, False) + b_depth.astype(jnp.float32)
    ).reshape(lat_dev, tokens_dev, 2 * FF)
    up_part = conv_out[..., :FF]
    gate_part = conv_out[..., FF:]
    gated_mix = to_low(up_part * jax.nn.silu(gate_part))
    branch_two = lax.optimization_barrier(
        matmul(gated_mix, w_point) + b_point.astype(jnp.float32)
    )
    output = (after_cross + gate_two * branch_two).astype(jnp.bfloat16).reshape(latents.shape)
    grad_out = cotangent.reshape(lat_dev, tokens_dev, D).astype(jnp.float32)
    grad_gate_two = jnp.sum(grad_out * branch_two, axis=1)
    grad_branch_two = to_low(grad_out * gate_two)
    grad_branch_two, x_qkv, x_attn, x_cross_q, x_cross_out, x_inner = lax.optimization_barrier(
        (
            grad_branch_two,
            *spread([hidden_one, attended, after_low]),
            *spread([cross_mixed, hidden_two]),
        )
    )
    grad_gated = matmul_t(grad_branch_two, w_point)
    grad_up = grad_gated * jax.nn.silu(gate_part)
    grad_gate = grad_gated * up_part * silu_slope(gate_part)
    grad_conv = to_low(jnp.concatenate([grad_up, grad_gate], axis=-1)).reshape(
        lat_dev, row_dev, col_dev, 2 * FF
    )
    grad_b_depth = jnp.sum(grad_conv, axis=(0, 1, 2), dtype=jnp.float32)
    tap_grads = []
    for tap_row in range(3):
        for tap_col in range(3):
            tap_grads.append(
                jnp.einsum(
                    "lrcf,lrcf->f",
                    padded[:, tap_row : tap_row + row_dev, tap_col : tap_col + col_dev],
                    grad_conv,
                    preferred_element_type=jnp.float32,
                )
            )
    grad_w_depth = jnp.stack(tap_grads)
    grad_padded = jnp.pad(with_halo(grad_conv, (("seq", 1),), 1), ((0, 0), (0, 0), (1, 1), (0, 0)))
    grad_active = depth_conv(grad_padded, w_depth, row_dev, col_dev, True).reshape(
        lat_dev, tokens_dev, 2 * FF
    )
    grad_inner = to_low(grad_active * silu_slope(inner_pre))
    grad_inner, x_point = lax.optimization_barrier((grad_inner, *spread([gated_mix])))
    grad_hidden_two = matmul_t(grad_inner, w_in)
    grad_shift_two = jnp.sum(grad_hidden_two, axis=1)
    grad_scale_two = jnp.sum(grad_hidden_two * normed_two, axis=1)
    grad_second = grad_out + norm_back(grad_hidden_two * (1.0 + scale_two), normed_two, inverse_two)
    grad_cross_out = to_low(grad_second)
    grad_mixed = to_low(matmul_t(grad_cross_out, w_cross_out)).reshape(
        lat_dev, tokens_dev, CROSS_HEADS, cross_dim
    )
    scores_again = (
        jnp.einsum("lrhc,lthc->lhrt", query_c, keys_c, preferred_element_type=jnp.float32)
        * score_scale
    )
    probs = jnp.exp(scores_again - log_total)
    grad_probs = jnp.einsum(
        "lrhc,lthc->lhrt", grad_mixed, values_c, preferred_element_type=jnp.float32
    )
    grad_values_c = jnp.einsum(
        "lhrt,lrhc->lthc", to_low(probs), grad_mixed, preferred_element_type=jnp.float32
    )
    grad_scores = to_low(probs * (grad_probs - jnp.sum(probs * grad_probs, axis=-1, keepdims=True)))
    grad_query_c = to_low(
        jnp.einsum("lhrt,lthc->lrhc", grad_scores, keys_c, preferred_element_type=jnp.float32)
        * score_scale
    ).reshape(lat_dev, tokens_dev, D)
    grad_keys_c = (
        jnp.einsum("lhrt,lrhc->lthc", grad_scores, query_c, preferred_element_type=jnp.float32)
        * score_scale
    )
    grad_keyval_part = jnp.concatenate(
        [grad_keys_c.reshape(lat_dev, text_len, D), grad_values_c.reshape(lat_dev, text_len, D)],
        axis=-1,
    )
    grad_keyval_part = grad_keyval_part.reshape(lat_dev, text_len, segs, 2 * D // segs)
    grad_keyval = to_low(
        lax.psum_scatter(
            grad_keyval_part.astype(jnp.bfloat16), "seq", scatter_dimension=2, tiled=True
        ).astype(jnp.float32)
    ).reshape(lat_dev, text_len, 2 * D // segs)
    grad_w_cross_kv = outer_sum(text, grad_keyval)
    grad_first = grad_second + matmul_t(grad_query_c, w_cross_q)
    grad_gate_one = jnp.sum(grad_first * branch_one, axis=1)
    grad_branch_one = to_low(grad_first * gate_one)
    grad_branch_one, y_point, y_inner = lax.optimization_barrier(
        (grad_branch_one, *collect([grad_branch_two, grad_inner]))
    )
    grad_attended = matmul_t(grad_branch_one, w_attn_out).reshape(
        lat_dev, tokens_dev, heads_lin, 32
    )
    grad_numer = grad_attended / denominator[..., None]
    grad_denom = -jnp.sum(grad_attended * attn_val, axis=-1) / denominator
    grad_query = (
        jnp.einsum("lrhe,lhde->lrhd", grad_numer, kv_state, precision=precise)
        + grad_denom[..., None] * key_sum[:, None]
    )
    state_grad_part = jnp.einsum("lrhd,lrhe->lhde", query_f, grad_numer, precision=precise)
    sum_grad_part = jnp.einsum("lrhd,lrh->lhd", query_f, grad_denom, precision=precise)
    state_grad, sum_grad = state_sum(state_grad_part, sum_grad_part, jnp.bfloat16, 3)
    keys_f = keys_lin.astype(jnp.float32)
    values_f = values_lin.astype(jnp.float32)
    grad_keys = (
        jnp.einsum("lrhe,lhde->lrhd", values_f, state_grad, precision=precise) + sum_grad[:, None]
    )
    grad_values = jnp.einsum("lrhd,lhde->lrhe", keys_f, state_grad, precision=precise)
    grad_projected = to_low(
        jnp.concatenate(
            [
                grad_query.reshape(lat_dev, tokens_dev, D) * (query_pre > 0.0),
                grad_keys.reshape(lat_dev, tokens_dev, D) * (key_pre > 0.0),
                grad_values.reshape(lat_dev, tokens_dev, D),
            ],
            axis=-1,
        )
    )
    grad_projected, y_cross_out, y_cross_q, y_attn = lax.optimization_barrier(
        (grad_projected, *collect([grad_cross_out, grad_query_c, grad_branch_one]))
    )
    grad_hidden_one = matmul_t(grad_projected, w_qkv)
    grad_input = grad_first + norm_back(
        grad_hidden_one * (1.0 + scale_one), normed_one, inverse_one
    )
    grad_table = jnp.sum(
        jnp.stack(
            [
                jnp.sum(grad_hidden_one, axis=1),
                jnp.sum(grad_hidden_one * normed_one, axis=1),
                grad_gate_one,
                grad_shift_two,
                grad_scale_two,
                grad_gate_two,
            ],
            axis=1,
        ),
        axis=0,
    )
    grad_table = lax.optimization_barrier(grad_table)
    col_d = D // segs
    col_ff = 2 * FF // segs
    small_parts = jnp.concatenate(
        [
            grad_table.reshape(6, segs, col_d).transpose(1, 0, 2).reshape(segs, -1),
            grad_w_depth.reshape(9, segs, col_ff).transpose(1, 0, 2).reshape(segs, -1),
            grad_b_depth.reshape(segs, col_ff),
        ],
        axis=1,
    ).astype(jnp.bfloat16)
    small_parts = small_parts.reshape(segs, -1, LANE)
    small_mine = (
        lax.psum_scatter(small_parts, "seq", scatter_dimension=0, tiled=True)
        .astype(jnp.float32)
        .reshape(-1)
    )
    table_q = small_mine[: 6 * col_d].reshape(6, col_d)
    depth_q = small_mine[6 * col_d : 6 * col_d + 9 * col_ff].reshape(9, col_ff)
    depth_bias_q = small_mine[6 * col_d + 9 * col_ff :].reshape(1, col_ff)

    (y_qkv,) = collect([grad_projected])
    grad_w_qkv = outer_sum(x_qkv, y_qkv)
    grad_w_attn_out = outer_sum(x_attn, y_attn)
    grad_w_cross_q = outer_sum(x_cross_q, y_cross_q)
    grad_w_cross_out = outer_sum(x_cross_out, y_cross_out)
    grad_w_in = outer_sum(x_inner, y_inner)
    grad_w_point = outer_sum(x_point, y_point)
    grad_b_attn_out = jnp.sum(y_attn, axis=0, dtype=jnp.float32)
    grad_b_cross_out = jnp.sum(y_cross_out, axis=0, dtype=jnp.float32)
    grad_b_in = jnp.sum(y_inner, axis=0, dtype=jnp.float32)
    grad_b_point = jnp.sum(y_point, axis=0, dtype=jnp.float32)
    bias_part = jnp.concatenate(
        [grad_b_attn_out, grad_b_cross_out, grad_b_in, depth_bias_q.ravel(), grad_b_point]
    )
    len_bias = bias_part.size
    bias_rows = -(-bias_part.size // (8 * LANE)) * 8
    bias_part = jnp.pad(bias_part, (0, bias_rows * LANE - bias_part.size)).reshape(-1, LANE)
    quarter_grad = write_flat(
        segs,
        [
            table_q,
            grad_w_qkv,
            grad_w_attn_out,
            grad_b_attn_out,
            grad_w_cross_q,
            grad_w_cross_kv,
            grad_w_cross_out,
            grad_b_cross_out,
            grad_w_in,
            grad_b_in,
            depth_q,
            depth_bias_q,
            grad_w_point,
            grad_b_point,
        ],
    )
    if count_dp == 8 and quarter_grad.shape[0] % (8 * 240) == 0:
        grad_shard = reduce_shard(quarter_grad)
    else:
        grad_shard = lax.psum_scatter(
            quarter_grad.reshape(count_dp, -1, LANE), "dp", scatter_dimension=0, tiled=True
        ).reshape(-1, LANE)
    *flat_outs, bias_grads = finish(
        grad_shard,
        bias_part,
        params_rows,
        moment_one.reshape(-1, LANE),
        moment_two.reshape(-1, LANE),
    )
    gradient, moment_one_new, moment_two_new, update = [
        value.reshape(params.shape) for value in flat_outs
    ]
    return (
        output,
        grad_input.reshape(latents.shape),
        gradient,
        moment_one_new,
        moment_two_new,
        update,
        bias_grads.reshape(1, -1)[:, :len_bias],
    )


def solution(mesh):
    return jax.shard_map(
        shards,
        mesh=mesh,
        in_specs=(
            P("dp", "seq", None, None),
            P("dp", None, None),
            P("dp", None),
            P("dp", "seq", None, None),
            P("seq", "dp"),
            P("seq", "dp"),
            P("seq", "dp"),
        ),
        out_specs=(
            P("dp", "seq", None, None),
            P("dp", "seq", None, None),
            P("seq", "dp"),
            P("seq", "dp"),
            P("seq", "dp"),
            P("seq", "dp"),
            P("seq", None),
        ),
        check_vma=False,
    )
```

```python
import math

import jax
import jax.numpy as jnp
from jax import lax
from jax.experimental import pallas as pl
from jax.experimental.pallas import tpu as pltpu
from jax.sharding import PartitionSpec as P

D = 1152
FF = 2880
CROSS_HEADS = 16


precise = lax.Precision.HIGHEST
eps_norm = 1e-06
eps_linear = 1e-06
beta_first = 0.9
beta_second = 0.95
adam_eps = 1e-08
weight_decay = 0.01
adam_steps = 100.0


def with_halo(block, sides, width):
    for axis, dim in sides:
        count = lax.axis_size(axis)
        forward = [(i, i + 1) for i in range(count - 1)]
        backward = [(target, source) for source, target in forward]
        low = lax.ppermute(
            lax.slice_in_dim(block, block.shape[dim] - width, None, axis=dim), axis, forward
        )
        high = lax.ppermute(lax.slice_in_dim(block, 0, width, axis=dim), axis, backward)
        block = jnp.concatenate([low, block, high], axis=dim)
    return block


def piece_specs():
    return [
        (6, D, False),
        (D, 3 * D, False),
        (D, D, False),
        (1, D, True),
        (D, D, False),
        (D, 2 * D, False),
        (D, D, False),
        (1, D, True),
        (D, 2 * FF, False),
        (1, 2 * FF, True),
        (9, 2 * FF, False),
        (1, 2 * FF, True),
        (FF, D, False),
        (1, D, True),
    ]


LANE = 128
UNIT = 32
MESH = pl.DeviceIdType.MESH


def merge_units(values, lane_unit):
    out = values[0]
    last = values[0]
    for position in range(1, 4):
        if values[position] is not last:
            out = jnp.where(lane_unit >= position, values[position], out)
            last = values[position]
    return out


def rolled(value, units):
    units = units % 4
    return value if units == 0 else pltpu.roll(value, units * UNIT, 1)


def matrix_rows(count_rows):
    return 192 if count_rows % 192 == 0 else 64


def read_matrix(flat, offset, rows_of, cols_of, segs):
    total_rows = flat.shape[1]
    per_row = cols_of // segs // UNIT
    unit_at = offset // UNIT
    block = matrix_rows(rows_of)
    base = unit_at // 4 // 16 * 16
    shift = unit_at - 4 * base
    step = block * per_row // 4
    need = (shift + block * per_row - 1) // 4 + 1
    need = -(-need // 16) * 16
    assert base + (rows_of // block - 1) * step + need <= total_rows
    tiles = cols_of // LANE

    def kernel(in_ref, out_ref, wide, mixed):
        def widen(at, _):
            row = pl.multiple_of(at * 16, 16)
            for seg in range(segs):
                wide[pl.ds(pl.multiple_of(seg * need + row, 16), 16), :] = in_ref[
                    seg, pl.ds(row, 16), :
                ].astype(jnp.float32)
            return 0

        lax.fori_loop(0, need // 16, widen, 0, unroll=8)
        lane_unit = lax.broadcasted_iota(jnp.int32, (8, LANE), 1) // UNIT

        def group(at, _):
            for phase in range(4):
                loaded = {}
                turned = {}
                for tile in range(tiles):
                    parts = []
                    for slot in range(4):
                        col = 4 * tile + slot
                        seg, unit = col // per_row, col % per_row
                        source = shift + phase * per_row + unit
                        key = (seg, source // 4)
                        if key not in loaded:
                            loaded[key] = wide[
                                pl.ds(seg * need + key[1] + at * (8 * per_row), 8, stride=per_row),
                                :,
                            ]
                        turn = (slot - source) % 4
                        if (key, turn) not in turned:
                            turned[key, turn] = rolled(loaded[key], turn)
                        parts.append(turned[key, turn])
                    mixed[pl.ds(tile * block + phase + at * 32, 8, stride=4), :] = merge_units(
                        parts, lane_unit
                    )
            return 0

        lax.fori_loop(0, block // 32, group, 0, unroll=2)

        def narrow(at, _):
            row = pl.multiple_of(at * 16, 16)
            for tile in range(tiles):
                out_ref[pl.ds(row, 16), tile * LANE : (tile + 1) * LANE] = mixed[
                    pl.ds(pl.multiple_of(tile * block + row, 16), 16), :
                ].astype(jnp.bfloat16)
            return 0

        lax.fori_loop(0, block // 16, narrow, 0, unroll=2)

    return pl.pallas_call(
        kernel,
        grid=(rows_of // block,),
        in_specs=[
            pl.BlockSpec(
                (pl.Element(segs), pl.Element(need), pl.Element(LANE)),
                lambda at: (0, pl.multiple_of(base + at * step, 16), 0),
            )
        ],
        out_specs=pl.BlockSpec((block, cols_of), lambda at: (at, 0)),
        out_shape=jax.ShapeDtypeStruct((rows_of, cols_of), jnp.bfloat16),
        scratch_shapes=[
            pltpu.VMEM((segs * need, LANE), jnp.float32),
            pltpu.VMEM((tiles * block, LANE), jnp.float32),
        ],
        compiler_params=pltpu.CompilerParams(vmem_limit_bytes=48 << 20),
        cost_estimate=pl.CostEstimate(
            flops=0, bytes_accessed=4 * rows_of * cols_of, transcendentals=0
        ),
        name="read_matrix",
    )(flat)


def write_flat(segs, parts):
    specs = piece_specs()
    block_rows = 192
    total = sum(rows_of * cols_of // segs for rows_of, cols_of, _ in specs)
    flat_rows = total // LANE
    places = []
    offset = 0
    big, small = [], []
    for (rows_of, cols_of, _), value in zip(specs, parts):
        width = cols_of // segs
        length = rows_of * width
        if rows_of > 9:
            assert rows_of % block_rows == 0
            places.append((True, offset, rows_of, width, len(big)))
            big.append(value)
        else:
            lead = offset % LANE
            rest = -(lead + length) % LANE
            padded = jnp.pad(value.reshape(-1), (lead, rest)).reshape(-1, LANE)
            places.append((False, offset, length, None, len(small)))
            small.append(padded)
        offset += length
    widths = sorted({place[3] for place in places if place[0]})
    chunk = 144

    def kernel(*refs):
        big_refs = refs[: len(big)]
        small_refs = refs[len(big) : len(big) + len(small)]
        out_ref = refs[len(big) + len(small)]
        flat = refs[len(big) + len(small) + 1]
        bufs = refs[len(big) + len(small) + 2 : len(big) + len(small) + 2 + len(widths)]
        in_sem = refs[-1]
        lane_unit = lax.broadcasted_iota(jnp.int32, (8, LANE), 1) // UNIT
        row_unit = lax.broadcasted_iota(jnp.int32, (1, LANE), 1) // UNIT

        def place_small(ref, offset, length):
            first = offset // LANE
            last = (offset + length - 1) // LANE
            lead = offset % LANE // UNIT
            tail = (offset + length) % LANE // UNIT
            count = last - first + 1
            if count > 2:

                def copy_row(at, _):
                    flat[pl.ds(first + 1 + at, 1), :] = ref[pl.ds(1 + at, 1), :]
                    return 0

                lax.fori_loop(0, count - 2, copy_row, 0)
            keep = row_unit >= lead
            if count == 1 and tail:
                keep = keep & (row_unit < tail)
            flat[first : first + 1, :] = jnp.where(keep, ref[0:1, :], flat[first : first + 1, :])
            if count > 1:
                flat[last : last + 1, :] = (
                    jnp.where(
                        row_unit < tail, ref[count - 1 : count, :], flat[last : last + 1, :]
                    )
                    if tail
                    else ref[count - 1 : count, :]
                )

        def fetch_block(ref, buf, width, at, slot):
            row = pl.multiple_of(at * block_rows, 64)
            return [
                pltpu.make_async_copy(
                    ref.at[pl.ds(row, block_rows), tile * LANE : (tile + 1) * LANE],
                    buf.at[slot, tile],
                    in_sem.at[widths.index(width), slot, tile],
                )
                for tile in range(-(-width // LANE))
            ]

        def place_big(ref, buf, offset, rows_of, width):
            per_row = width // UNIT
            first = offset // LANE
            shift = offset % LANE // UNIT
            block = block_rows
            blocks = rows_of // block

            def fetch(at, slot):
                return fetch_block(ref, buf, width, at, slot)

            def one_block(at, _):
                slot = lax.rem(at, 2)

                @pl.when(at + 1 < blocks)
                def _():
                    for copy in fetch(at + 1, 1 - slot):
                        copy.start()

                for copy in fetch(at, slot):
                    copy.wait()

                def group(sub, _):
                    loaded = {}
                    turned = {}

                    def unit_value(phase, unit, lane):
                        key = (phase, unit // 4)
                        if key not in loaded:
                            loaded[key] = buf[
                                slot, key[1], pl.ds(phase + sub * 32, 8, stride=4), :
                            ]
                        turn = (lane - unit) % 4
                        if (key, turn) not in turned:
                            turned[key, turn] = rolled(loaded[key], turn)
                        return turned[key, turn]

                    start = first + (at * (block // 4) + sub * 8) * per_row
                    for row in range(per_row + (1 if shift else 0)):
                        where = pl.ds(start + row, 8, stride=per_row)
                        parts = []
                        kept = None
                        for lane in range(4):
                            unit = 4 * row + lane - shift
                            if unit < 0 or unit >= 4 * per_row:
                                if kept is None:
                                    kept = flat[where, :]
                                parts.append(kept)
                            else:
                                parts.append(unit_value(unit // per_row, unit % per_row, lane))
                        flat[where, :] = merge_units(parts, lane_unit)
                    return 0

                lax.fori_loop(0, block // 32, group, 0, unroll=3)
                return 0

            lax.fori_loop(0, blocks, one_block, 0)

        def first_fetch(width, after):
            for is_big, _, _, other, index in places:
                if is_big and other == width and index > after:
                    buf = bufs[widths.index(width)]
                    for copy in fetch_block(big_refs[index], buf, width, 0, 0):
                        copy.start()
                    return

        for width in widths:
            first_fetch(width, -1)
        for is_big, offset, rows_of, width, index in places:
            if is_big:
                place_big(big_refs[index], bufs[widths.index(width)], offset, rows_of, width)
                first_fetch(width, index)
            else:
                place_small(small_refs[index], offset, rows_of)

        def narrow(at, _):
            where = pl.ds(pl.multiple_of(at * chunk, 16), chunk)
            out_ref[where, :] = flat[where, :].astype(jnp.bfloat16)
            return 0

        lax.fori_loop(0, flat_rows // chunk, narrow, 0)

    return pl.pallas_call(
        kernel,
        in_specs=[pl.BlockSpec(memory_space=pl.ANY)] * len(big)
        + [pl.BlockSpec(memory_space=pltpu.VMEM)] * len(small),
        out_specs=pl.BlockSpec(memory_space=pltpu.VMEM),
        out_shape=jax.ShapeDtypeStruct((flat_rows, LANE), jnp.bfloat16),
        scratch_shapes=[pltpu.VMEM((flat_rows, LANE), jnp.float32)]
        + [
            pltpu.VMEM((2, -(-width // LANE), block_rows, LANE), jnp.float32) for width in widths
        ]
        + [
            pltpu.SemaphoreType.DMA((len(widths), 2, -(-widths[-1] // LANE))),
        ],
        compiler_params=pltpu.CompilerParams(vmem_limit_bytes=56 << 20),
        cost_estimate=pl.CostEstimate(flops=0, bytes_accessed=6 * total, transcendentals=0),
        name="write_flat",
    )(*big, *small)


def gather_flat(shard):
    rows = shard.shape[0]
    first = (rows // 2 + 15) // 16 * 16
    parts = ((0, first), (first, rows - first))

    def kernel(
        in_ref,
        out_ref,
        own_sem,
        z_send,
        z_recv,
        x_send,
        x_recv,
        y_send,
        y_recv,
        d_send,
        d_recv,
        c_send,
        c_recv,
    ):
        dp = lax.axis_index("dp")
        seq = lax.axis_index("seq")
        near, far = lax.rem(dp, 2), lax.div(dp, 2)
        core, side = lax.rem(seq, 2), lax.div(seq, 2)

        half = lax.div(far, 2)
        place = far + half * (3 - 2 * far)
        inner = far + 1 - 2 * half
        outer = far - 1 + 2 * half

        def dp_of(turn, flip):
            at = place if turn == 0 else 1 - place if turn == 1 else turn
            return 2 * (at + half * (3 - 2 * at)) + (1 - near if flip else near)

        def seq_of(flip, other_core):
            return 2 * (1 - side if flip else side) + (1 - core if other_core else core)

        def region(seq_at, dp_at, part):
            start, length = parts[part]
            return out_ref.at[
                seq_at, pl.ds(pl.multiple_of(dp_at * rows + start, 16), length), :
            ]

        def own_region(part):
            start, length = parts[part]
            return in_ref.at[pl.ds(start, length), :]

        def column(turn, part):
            return region(seq, dp_of(turn, False), part)

        def source(turn, part):
            return column(turn, part) if turn else own_region(part)

        def remote(src, dst, send, recv, target):
            return pltpu.make_async_remote_copy(
                src_ref=src,
                dst_ref=dst,
                send_sem=send,
                recv_sem=recv,
                device_id=target,
                device_id_type=MESH,
            )

        x_peer = {"dp": dp_of(0, True)}
        y_peer = {"seq": seq_of(True, False)}
        c_peer = {"seq": seq_of(False, True)}

        def z_copy(kind, part):
            turn = (0, 0, 1, 2, 3)[kind]
            arrives = (place, 0, 2, 1, 2)[kind]
            return remote(
                source(turn, part),
                column(turn, part),
                z_send.at[kind, part],
                z_recv.at[arrives, part],
                {"dp": 2 * (inner if kind in (0, 2) else outer) + near},
            )

        def z_in(turn, part):
            here = column(turn, part)
            return remote(
                here, here, z_send.at[0, part], z_recv.at[turn - 1, part], {"dp": 2 * inner + near}
            )

        def x_out(turn, part):
            return remote(
                source(turn, part),
                column(turn, part),
                x_send.at[turn, part],
                x_recv.at[turn, part],
                x_peer,
            )

        def x_in(turn, part):
            here = region(seq, dp_of(turn, True), part)
            return remote(here, here, x_send.at[turn, part], x_recv.at[turn, part], x_peer)

        def y_out(turn, part):
            return remote(
                source(turn, part),
                column(turn, part),
                y_send.at[turn, part],
                y_recv.at[turn, part],
                y_peer,
            )

        def y_in(turn, part):
            here = region(seq_of(True, False), dp_of(turn, False), part)
            return remote(here, here, y_send.at[turn, part], y_recv.at[turn, part], y_peer)

        def d_out(turn, part):
            if part == 0:
                here, target = region(seq, dp_of(turn, True), part), y_peer
            else:
                here, target = region(seq_of(True, False), dp_of(turn, False), part), x_peer
            return remote(here, here, d_send.at[turn, part], d_recv.at[turn, part], target)

        def d_in(turn, part):
            here = region(seq_of(True, False), dp_of(turn, True), part)
            target = y_peer if part == 0 else x_peer
            return remote(here, here, d_send.at[turn, part], d_recv.at[turn, part], target)

        def c_copy(kind, turn, part, incoming):
            where = region(
                seq_of(kind in (2, 3), incoming), dp_of(turn, kind in (1, 3)), part
            )
            src = own_region(part) if kind == 0 and turn == 0 else where
            return remote(
                src if not incoming else where,
                where,
                c_send.at[kind, turn, part],
                c_recv.at[kind, turn, part],
                c_peer,
            )

        barrier = pltpu.get_barrier_semaphore()
        for target in (x_peer, y_peer, c_peer, {"dp": 2 * inner + near}):
            pl.semaphore_signal(barrier, inc=1, device_id=target, device_id_type=MESH)

        @pl.when(place == 1)
        def _():
            pl.semaphore_signal(
                barrier, inc=1, device_id={"dp": 2 * outer + near}, device_id_type=MESH
            )
            pl.semaphore_wait(barrier, 5)

        @pl.when(place == 0)
        def _():
            pl.semaphore_wait(barrier, 4)

        keep = [
            pltpu.make_async_copy(own_region(part), region(seq, dp, part), own_sem.at[part])
            for part in range(2)
        ]
        def outwards(kind, part):
            @pl.when(place == 1)
            def _():
                z_copy(kind, part).start()

        for part in range(2):
            z_copy(0, part).start()
            outwards(1, part)
            x_out(0, part).start()
            y_out(0, part).start()
        for part in range(2):
            keep[part].start()
            c_copy(0, 0, part, False).start()

        def sideways(turn):
            for part in range(2):
                x_in(turn, part).wait_recv()
                if part == 0:
                    d_out(turn, part).start()
                c_copy(1, turn, part, False).start()
                y_in(turn, part).wait_recv()
                if part == 1:
                    d_out(turn, part).start()
                c_copy(2, turn, part, False).start()

        def diagonal(turn):
            for part in range(2):
                d_in(turn, part).wait_recv()
                c_copy(3, turn, part, False).start()

        for turn in range(1, 4):
            for part in range(2):
                z_in(turn, part).wait_recv()
                outwards(turn + 1, part)
                x_out(turn, part).start()
                y_out(turn, part).start()
                c_copy(0, turn, part, False).start()
            sideways(turn - 1)
            if turn > 1:
                diagonal(turn - 2)
        sideways(3)
        diagonal(2)
        diagonal(3)

        @pl.when(place == 1)
        def _():
            for kind in range(1, 5):
                for part in range(2):
                    z_copy(kind, part).wait_send()

        for part in range(2):
            keep[part].wait()
            z_copy(0, part).wait_send()
            for turn in range(4):
                x_out(turn, part).wait_send()
                y_out(turn, part).wait_send()
                d_out(turn, part).wait_send()
                for kind in range(4):
                    c_copy(kind, turn, part, False).wait_send()
                    c_copy(kind, turn, part, True).wait_recv()

    return pl.pallas_call(
        kernel,
        in_specs=[pl.BlockSpec(memory_space=pltpu.VMEM)],
        out_specs=pl.BlockSpec(memory_space=pl.ANY),
        out_shape=jax.ShapeDtypeStruct((4, 8 * rows, LANE), jnp.bfloat16),
        scratch_shapes=[
            pltpu.SemaphoreType.DMA((2,)),
            pltpu.SemaphoreType.DMA((5, 2)),
            pltpu.SemaphoreType.DMA((3, 2)),
        ]
        + [pltpu.SemaphoreType.DMA((4, 2))] * 6
        + [pltpu.SemaphoreType.DMA((4, 4, 2))] * 2,
        compiler_params=pltpu.CompilerParams(collective_id=5, has_side_effects=True),
        name="gather_flat",
    )(shard)


def round_rows(values):
    def kernel(in_ref, out_ref):
        out_ref[...] = in_ref[...].astype(jnp.bfloat16)

    return pl.pallas_call(
        kernel,
        in_specs=[pl.BlockSpec(memory_space=pltpu.VMEM)],
        out_specs=pl.BlockSpec(memory_space=pltpu.VMEM),
        out_shape=jax.ShapeDtypeStruct(values.shape, jnp.bfloat16),
        name="round_rows",
    )(values)


def gather_weights(shard_low, segs):
    if segs == 4 and lax.axis_size("dp") == 8 and shard_low.shape[0] % 16 == 0:
        flat = gather_flat(shard_low)
    else:
        whole = lax.all_gather(shard_low, ("seq", "dp"), axis=0, tiled=True)
        flat = whole.reshape(segs, -1, LANE)
    pieces = []
    offset = 0
    for rows_of, cols_of, vector in piece_specs():
        length = rows_of * cols_of // segs
        if rows_of > 9:
            pieces.append(read_matrix(flat, offset, rows_of, cols_of, segs))
        else:
            first, last = offset // LANE, -(-(offset + length) // LANE)
            lead = offset - first * LANE
            block = flat[:, first:last].reshape(segs, -1)[:, lead : lead + length]
            block = block.reshape(segs, rows_of, cols_of // segs).transpose(1, 0, 2)
            pieces.append(block.reshape(cols_of) if vector else block.reshape(rows_of, cols_of))
        offset = offset + length
    return pieces


def peer_barrier(groups):
    barrier = pltpu.get_barrier_semaphore()
    total = 0
    for axis, count in groups:
        me = lax.axis_index(axis)
        for step in range(1, count):
            pl.semaphore_signal(
                barrier, inc=1, device_id={axis: lax.rem(me + step, count)}, device_id_type=MESH
            )
        total += count - 1
    pl.semaphore_wait(barrier, total)


def exchange(axis, count, source, slots, send_sem, recv_sem):
    me = lax.axis_index(axis)
    for step in range(1, count):
        pltpu.make_async_remote_copy(
            src_ref=source,
            dst_ref=slots.at[me],
            send_sem=send_sem.at[step - 1],
            recv_sem=recv_sem.at[me],
            device_id={axis: lax.rem(me + step, count)},
            device_id_type=MESH,
        ).start()


def exchange_wait(axis, count, source, slots, send_sem, recv_sem):
    me = lax.axis_index(axis)
    for step in range(1, count):
        peer = lax.rem(me + step, count)
        copy = pltpu.make_async_remote_copy(
            src_ref=source,
            dst_ref=slots.at[peer],
            send_sem=send_sem.at[step - 1],
            recv_sem=recv_sem.at[peer],
            device_id={axis: peer},
            device_id_type=MESH,
        )
        copy.wait_send()
        copy.wait_recv()


def in_order(axis, count, own, slots):
    me = lax.axis_index(axis)
    total = None
    for index in range(count):
        term = jnp.where(me == index, own, slots[index].astype(jnp.float32))
        total = term if total is None else total + term
    return total


def seq_sum(block, collective_id):
    count = lax.axis_size("seq")

    def kernel(in_ref, out_ref, slots, send_sem, recv_sem):
        peer_barrier([("seq", count)])
        exchange("seq", count, in_ref, slots, send_sem, recv_sem)
        exchange_wait("seq", count, in_ref, slots, send_sem, recv_sem)
        out_ref[...] = in_order("seq", count, in_ref[...].astype(jnp.float32), slots)

    return pl.pallas_call(
        kernel,
        in_specs=[pl.BlockSpec(memory_space=pltpu.VMEM)],
        out_specs=pl.BlockSpec(memory_space=pltpu.VMEM),
        out_shape=jax.ShapeDtypeStruct(block.shape, jnp.float32),
        scratch_shapes=[
            pltpu.VMEM((count,) + block.shape, block.dtype),
            pltpu.SemaphoreType.DMA((count - 1,)),
            pltpu.SemaphoreType.DMA((count,)),
        ],
        compiler_params=pltpu.CompilerParams(collective_id=collective_id, has_side_effects=True),
        name="seq_sum",
    )(block)


def state_sum(state, sums, kind, collective_id):
    heads = state.shape[1]
    flat = jnp.concatenate(
        [state.reshape(-1, LANE), jnp.pad(sums.reshape(-1), (0, -sums.size % LANE)).reshape(-1, LANE)]
    ).astype(kind)
    rows = flat.shape[0]
    flat = jnp.pad(flat, ((0, -rows % 16), (0, 0)))
    total = seq_sum(flat, collective_id)
    split = state.size // LANE
    return (
        total[:split].reshape(state.shape),
        total[split:].reshape(-1)[: sums.size].reshape(1, heads, -1),
    )


def reduce_shard(flat):
    rows = flat.shape[0] // 8
    pieces = 3
    part = rows // pieces
    step = 80

    def kernel(in_ref, out_ref, recv_x, send_z, recv_z, x_send, x_recv, z_send, z_recv):
        me = lax.axis_index("dp")
        near = lax.rem(me, 2)
        far = lax.div(me, 2)
        partner = me + 1 - 2 * near

        def far_of(shift):
            return lax.rem(far + shift, 4)

        barrier = pltpu.get_barrier_semaphore()
        pl.semaphore_signal(barrier, inc=1, device_id={"dp": partner}, device_id_type=MESH)
        for shift in range(1, 4):
            pl.semaphore_signal(
                barrier,
                inc=1,
                device_id={"dp": 2 * far_of(shift) + near},
                device_id_type=MESH,
            )
        pl.semaphore_wait(barrier, 4)

        def window(shard, piece):
            return pl.ds(pl.multiple_of(shard * rows + piece * part, 16), part)

        def x_copy(shift, piece):
            return pltpu.make_async_remote_copy(
                src_ref=in_ref.at[window(2 * far_of(shift) + 1 - near, piece), :],
                dst_ref=recv_x.at[shift, pl.ds(piece * part, part), :],
                send_sem=x_send.at[shift, piece],
                recv_sem=x_recv.at[shift, piece],
                device_id={"dp": partner},
                device_id_type=MESH,
            )

        def z_copy(shift, piece):
            return pltpu.make_async_remote_copy(
                src_ref=send_z.at[shift - 1, pl.ds(piece * part, part), :],
                dst_ref=recv_z.at[shift - 1, pl.ds(piece * part, part), :],
                send_sem=z_send.at[shift - 1, piece],
                recv_sem=z_recv.at[shift - 1, piece],
                device_id={"dp": 2 * far_of(shift) + near},
                device_id_type=MESH,
            )

        order = (1, 2, 3, 0)
        for shift in order:
            for piece in range(pieces):
                x_copy(shift, piece).start()

        def own_sum(shift, row, at):
            start = (2 * far_of(shift) + near) * rows + row + at * step
            own = in_ref[pl.ds(pl.multiple_of(start, 16), step), :]
            other = recv_x[shift, pl.ds(pl.multiple_of(row + at * step, 16), step), :]
            return own.astype(jnp.float32) + other.astype(jnp.float32)

        for shift in order:
            for piece in range(pieces):
                x_copy(shift, piece).wait_recv()
                row = piece * part

                def add(at, _, shift=shift, row=row):
                    where = pl.ds(pl.multiple_of(row + at * step, 16), step)
                    total = own_sum(shift, row, at)
                    if shift:
                        send_z[shift - 1, where, :] = total.astype(jnp.bfloat16)
                    else:
                        out_ref[where, :] = total
                    return 0

                lax.fori_loop(0, part // step, add, 0)
                if shift:
                    z_copy(shift, piece).start()
        for shift in range(1, 4):
            for piece in range(pieces):
                z_copy(shift, piece).wait_recv()
                row = piece * part

                def gather(at, _, shift=shift, row=row):
                    where = pl.ds(pl.multiple_of(row + at * step, 16), step)
                    out_ref[where, :] = out_ref[where, :] + recv_z[shift - 1, where, :].astype(
                        jnp.float32
                    )
                    return 0

                lax.fori_loop(0, part // step, gather, 0)
        for shift in range(4):
            for piece in range(pieces):
                x_copy(shift, piece).wait_send()
                if shift:
                    z_copy(shift, piece).wait_send()

    block = (rows, LANE)
    return pl.pallas_call(
        kernel,
        in_specs=[pl.BlockSpec(memory_space=pltpu.VMEM)],
        out_specs=pl.BlockSpec(memory_space=pltpu.VMEM),
        out_shape=jax.ShapeDtypeStruct(block, jnp.float32),
        scratch_shapes=[
            pltpu.VMEM((4,) + block, jnp.bfloat16),
            pltpu.VMEM((3,) + block, jnp.bfloat16),
            pltpu.VMEM((3,) + block, jnp.bfloat16),
            pltpu.SemaphoreType.DMA((4, pieces)),
            pltpu.SemaphoreType.DMA((4, pieces)),
            pltpu.SemaphoreType.DMA((3, pieces)),
            pltpu.SemaphoreType.DMA((3, pieces)),
        ],
        compiler_params=pltpu.CompilerParams(
            collective_id=4, has_side_effects=True, vmem_limit_bytes=40 << 20
        ),
        name="reduce_shard",
    )(flat)


def finish(grad_shard, bias_part, params, moment_one, moment_two):
    rows = grad_shard.shape[0]
    count_dp = lax.axis_size("dp")
    count_seq = lax.axis_size("seq")
    entries = rows * LANE * count_dp * count_seq
    chunk = 48 if rows % 48 == 0 else rows
    bias_rows = bias_part.shape[0]

    def kernel(
        grad_ref,
        bias_ref,
        param_ref,
        one_ref,
        two_ref,
        gradient_ref,
        one_out,
        two_out,
        update_ref,
        bias_out,
        square,
        square_dp,
        square_seq,
        partial,
        bias_slots,
        send_bias,
        recv_bias,
        send_dp,
        recv_dp,
        send_seq,
        recv_seq,
    ):
        peer_barrier([("dp", count_dp), ("seq", count_seq)])
        exchange("dp", count_dp, bias_ref, bias_slots, send_bias, recv_bias)

        def squares(at, total):
            part = grad_ref[pl.ds(at * chunk, chunk), :].astype(jnp.float32)
            return total + jnp.sum(part * part, axis=0, keepdims=True)

        total = lax.fori_loop(0, rows // chunk, squares, jnp.zeros((1, LANE), jnp.float32))
        square[...] = jnp.broadcast_to(total, (8, LANE))
        exchange("dp", count_dp, square, square_dp, send_dp, recv_dp)
        exchange_wait("dp", count_dp, square, square_dp, send_dp, recv_dp)
        partial[...] = in_order("dp", count_dp, square[...], square_dp)
        exchange("seq", count_seq, partial, square_seq, send_seq, recv_seq)
        exchange_wait("seq", count_seq, partial, square_seq, send_seq, recv_seq)
        whole = jnp.sum(
            in_order("seq", count_seq, partial[...], square_seq)[0:1], axis=1, keepdims=True
        )
        factor = lax.rsqrt(whole / entries + 1e-06)
        exchange_wait("dp", count_dp, bias_ref, bias_slots, send_bias, recv_bias)
        bias_out[...] = in_order("dp", count_dp, bias_ref[...], bias_slots) * factor

        def step(at, _):
            where = pl.ds(at * chunk, chunk)
            gradient = grad_ref[where, :].astype(jnp.float32) * factor
            first = beta_first * one_ref[where, :] + (1.0 - beta_first) * gradient
            second = beta_second * two_ref[where, :] + (1.0 - beta_second) * gradient * gradient
            gradient_ref[where, :] = gradient
            one_out[where, :] = first
            two_out[where, :] = second
            first_hat = first / (1.0 - beta_first**adam_steps)
            second_hat = second / (1.0 - beta_second**adam_steps)
            update_ref[where, :] = (
                first_hat / (jnp.sqrt(second_hat) + adam_eps) + weight_decay * param_ref[where, :]
            )
            return 0

        lax.fori_loop(0, rows // chunk, step, 0)

    flat = jax.ShapeDtypeStruct((rows, LANE), jnp.float32)
    tile = (8, LANE)
    return pl.pallas_call(
        kernel,
        in_specs=[pl.BlockSpec(memory_space=pltpu.VMEM)] * 5,
        out_specs=[pl.BlockSpec(memory_space=pltpu.VMEM)] * 5,
        out_shape=[flat] * 4 + [jax.ShapeDtypeStruct((bias_rows, LANE), jnp.float32)],
        scratch_shapes=[
            pltpu.VMEM(tile, jnp.float32),
            pltpu.VMEM((count_dp,) + tile, jnp.float32),
            pltpu.VMEM((count_seq,) + tile, jnp.float32),
            pltpu.VMEM(tile, jnp.float32),
            pltpu.VMEM((count_dp, bias_rows, LANE), jnp.float32),
            pltpu.SemaphoreType.DMA((count_dp - 1,)),
            pltpu.SemaphoreType.DMA((count_dp,)),
            pltpu.SemaphoreType.DMA((count_dp - 1,)),
            pltpu.SemaphoreType.DMA((count_dp,)),
            pltpu.SemaphoreType.DMA((count_seq - 1,)),
            pltpu.SemaphoreType.DMA((count_seq,)),
        ],
        compiler_params=pltpu.CompilerParams(
            collective_id=1, has_side_effects=True, vmem_limit_bytes=48 << 20
        ),
        name="finish",
    )(grad_shard, bias_part, params, moment_one, moment_two)


def norm_parts(values):
    centred = values - jnp.mean(values, axis=-1, keepdims=True)
    inverse = lax.rsqrt(jnp.mean(centred * centred, axis=-1, keepdims=True) + eps_norm)
    return (centred * inverse, inverse)


def norm_back(grad_normed, normed, inverse):
    return inverse * (
        grad_normed
        - jnp.mean(grad_normed, axis=-1, keepdims=True)
        - normed * jnp.mean(grad_normed * normed, axis=-1, keepdims=True)
    )


def silu_slope(values):
    sigmoid_v = jax.nn.sigmoid(values)
    return sigmoid_v * (1.0 + values * (1.0 - sigmoid_v))


def to_low(values):
    return values.astype(jnp.bfloat16)


def matmul(left_op, right_op):
    return jnp.dot(left_op, right_op, preferred_element_type=jnp.float32)


def matmul_t(left_op, right_op):
    return lax.dot_general(
        left_op,
        right_op,
        (((left_op.ndim - 1,), (1,)), ((), ())),
        preferred_element_type=jnp.float32,
    )


def outer_sum(left_op, right_op):
    left_flat = left_op.reshape(-1, left_op.shape[-1])
    right_flat = right_op.reshape(-1, right_op.shape[-1])
    right_flat = jnp.pad(right_flat, ((0, 0), (0, -right_flat.shape[1] % LANE)))
    return lax.dot_general(
        left_flat, right_flat, (((0,), (0,)), ((), ())), preferred_element_type=jnp.float32
    )


def depth_conv(padded, kernel, row_dev, col_dev, flipped):
    kernel_f = kernel.astype(jnp.float32)
    summed = jnp.zeros(padded.shape[:1] + (row_dev, col_dev) + padded.shape[3:], jnp.float32)
    for tap_row in range(3):
        for tap_col in range(3):
            row_at = 2 - tap_row if flipped else tap_row
            col_at = 2 - tap_col if flipped else tap_col
            summed = (
                summed
                + kernel_f[tap_row * 3 + tap_col]
                * padded[:, row_at : row_at + row_dev, col_at : col_at + col_dev, :]
            )
    return summed


def shards(latents, text, time_embed, cotangent, params, moment_one, moment_two):
    lat_dev, row_dev, col_dev, width = latents.shape
    tokens_dev = row_dev * col_dev
    heads_lin = D // 32
    cross_dim = D // CROSS_HEADS
    score_scale = 1.0 / math.sqrt(cross_dim)
    text_len = text.shape[1]
    segs = lax.axis_size("seq")
    count_dp = lax.axis_size("dp")
    def spread(values):
        joined = jnp.concatenate(values, axis=-1).reshape(-1, sum(v.shape[-1] for v in values))
        whole = lax.all_gather(joined, "seq", axis=0, tiled=True)
        parts = []
        at = 0
        for value in values:
            parts.append(whole[:, at : at + value.shape[-1]])
            at += value.shape[-1]
        return parts

    def collect(values):
        blocks = jnp.stack(
            [
                jnp.concatenate(
                    [
                        value.reshape(-1, value.shape[-1])[
                            :, seg * (value.shape[-1] // segs) : (seg + 1) * (value.shape[-1] // segs)
                        ]
                        for value in values
                    ],
                    axis=1,
                )
                for seg in range(segs)
            ]
        )
        mine = lax.all_to_all(blocks, "seq", split_axis=0, concat_axis=0, tiled=True)
        mine = mine.reshape(-1, mine.shape[-1])
        parts = []
        at = 0
        for value in values:
            width = value.shape[-1] // segs
            parts.append(mine[:, at : at + width])
            at += width
        return parts

    params_rows = params.reshape(-1, LANE)
    shard_low = round_rows(params_rows)
    (
        mod_table,
        w_qkv,
        w_attn_out,
        b_attn_out,
        w_cross_q,
        w_cross_kv,
        w_cross_out,
        b_cross_out,
        w_in,
        b_in,
        w_depth,
        b_depth,
        w_point,
        b_point,
    ) = gather_weights(shard_low, segs)
    modulation = mod_table.astype(jnp.float32)[None] + time_embed.reshape(lat_dev, 6, D)
    shift_one = modulation[:, 0][:, None, :]
    scale_one = modulation[:, 1][:, None, :]
    gate_one = modulation[:, 2][:, None, :]
    shift_two = modulation[:, 3][:, None, :]
    scale_two = modulation[:, 4][:, None, :]
    gate_two = modulation[:, 5][:, None, :]
    tokens = latents.reshape(lat_dev, tokens_dev, D).astype(jnp.float32)
    normed_one, inverse_one = norm_parts(tokens)
    hidden_one = to_low(normed_one * (1.0 + scale_one) + shift_one)
    projected = matmul(hidden_one, w_qkv)
    query_pre = projected[..., :D]
    key_pre = projected[..., D : 2 * D]
    queries = to_low(jnp.maximum(query_pre, 0.0)).reshape(lat_dev, tokens_dev, heads_lin, 32)
    keys_lin = to_low(jnp.maximum(key_pre, 0.0)).reshape(lat_dev, tokens_dev, heads_lin, 32)
    values_lin = to_low(projected[..., 2 * D :]).reshape(lat_dev, tokens_dev, heads_lin, 32)
    state_part = jnp.einsum(
        "lrhd,lrhe->lhde", keys_lin, values_lin, preferred_element_type=jnp.float32
    )
    sum_part = jnp.sum(keys_lin, axis=1, dtype=jnp.float32)
    kv_state, key_sum = state_sum(state_part, sum_part, jnp.float32, 2)
    query_f = queries.astype(jnp.float32)
    numerator = jnp.einsum("lrhd,lhde->lrhe", query_f, kv_state, precision=precise)
    denominator = jnp.einsum("lrhd,lhd->lrh", query_f, key_sum, precision=precise) + eps_linear
    attn_val = numerator / denominator[..., None]
    attended = to_low(attn_val.reshape(lat_dev, tokens_dev, D))
    branch_one = matmul(attended, w_attn_out) + b_attn_out.astype(jnp.float32)
    after_attn = tokens + gate_one * branch_one
    after_low, x_qkv = lax.optimization_barrier((to_low(after_attn), *spread([hidden_one])))
    query_c = to_low(matmul(after_low, w_cross_q)).reshape(
        lat_dev, tokens_dev, CROSS_HEADS, cross_dim
    )
    keyval = to_low(matmul(text, w_cross_kv))
    keys_c = keyval[..., :D].reshape(lat_dev, text_len, CROSS_HEADS, cross_dim)
    values_c = keyval[..., D:].reshape(lat_dev, text_len, CROSS_HEADS, cross_dim)
    scores = (
        jnp.einsum("lrhc,lthc->lhrt", query_c, keys_c, preferred_element_type=jnp.float32)
        * score_scale
    )
    row_peak = jnp.max(scores, axis=-1, keepdims=True)
    log_total = row_peak + jnp.log(jnp.sum(jnp.exp(scores - row_peak), axis=-1, keepdims=True))
    probs_low = to_low(jnp.exp(scores - log_total))
    cross_mixed = to_low(
        jnp.einsum(
            "lhrt,lthc->lrhc", probs_low, values_c, preferred_element_type=jnp.float32
        ).reshape(lat_dev, tokens_dev, D)
    )
    after_cross = after_attn + matmul(cross_mixed, w_cross_out) + b_cross_out.astype(jnp.float32)
    normed_two, inverse_two = norm_parts(after_cross)
    hidden_two, x_attn, x_cross_q = lax.optimization_barrier(
        (
            to_low(normed_two * (1.0 + scale_two) + shift_two),
            *spread([attended, after_low]),
        )
    )
    inner_pre = matmul(hidden_two, w_in) + b_in.astype(jnp.float32)
    active = to_low(jax.nn.silu(inner_pre)).reshape(lat_dev, row_dev, col_dev, 2 * FF)
    padded = jnp.pad(with_halo(active, (("seq", 1),), 1), ((0, 0), (0, 0), (1, 1), (0, 0)))
    conv_out = (
        depth_conv(padded, w_depth, row_dev, col_dev, False) + b_depth.astype(jnp.float32)
    ).reshape(lat_dev, tokens_dev, 2 * FF)
    up_part = conv_out[..., :FF]
    gate_part = conv_out[..., FF:]
    gated_mix = to_low(up_part * jax.nn.silu(gate_part))
    branch_two = lax.optimization_barrier(
        matmul(gated_mix, w_point) + b_point.astype(jnp.float32)
    )
    output = (after_cross + gate_two * branch_two).astype(jnp.bfloat16).reshape(latents.shape)
    grad_out = cotangent.reshape(lat_dev, tokens_dev, D).astype(jnp.float32)
    grad_gate_two = jnp.sum(grad_out * branch_two, axis=1)
    grad_branch_two = to_low(grad_out * gate_two)
    grad_branch_two, x_cross_out, x_inner = lax.optimization_barrier(
        (grad_branch_two, *spread([cross_mixed, hidden_two]))
    )
    grad_gated = matmul_t(grad_branch_two, w_point)
    grad_up = grad_gated * jax.nn.silu(gate_part)
    grad_gate = grad_gated * up_part * silu_slope(gate_part)
    grad_conv = to_low(jnp.concatenate([grad_up, grad_gate], axis=-1)).reshape(
        lat_dev, row_dev, col_dev, 2 * FF
    )
    grad_b_depth = jnp.sum(grad_conv, axis=(0, 1, 2), dtype=jnp.float32)
    tap_grads = []
    for tap_row in range(3):
        for tap_col in range(3):
            tap_grads.append(
                jnp.einsum(
                    "lrcf,lrcf->f",
                    padded[:, tap_row : tap_row + row_dev, tap_col : tap_col + col_dev],
                    grad_conv,
                    preferred_element_type=jnp.float32,
                )
            )
    grad_w_depth = jnp.stack(tap_grads)
    grad_padded = jnp.pad(with_halo(grad_conv, (("seq", 1),), 1), ((0, 0), (0, 0), (1, 1), (0, 0)))
    grad_active = depth_conv(grad_padded, w_depth, row_dev, col_dev, True).reshape(
        lat_dev, tokens_dev, 2 * FF
    )
    grad_inner = to_low(grad_active * silu_slope(inner_pre))
    grad_inner, x_point = lax.optimization_barrier((grad_inner, *spread([gated_mix])))
    grad_hidden_two = matmul_t(grad_inner, w_in)
    grad_shift_two = jnp.sum(grad_hidden_two, axis=1)
    grad_scale_two = jnp.sum(grad_hidden_two * normed_two, axis=1)
    grad_second = grad_out + norm_back(grad_hidden_two * (1.0 + scale_two), normed_two, inverse_two)
    grad_cross_out = to_low(grad_second)
    grad_mixed = to_low(matmul_t(grad_cross_out, w_cross_out)).reshape(
        lat_dev, tokens_dev, CROSS_HEADS, cross_dim
    )
    scores_again = (
        jnp.einsum("lrhc,lthc->lhrt", query_c, keys_c, preferred_element_type=jnp.float32)
        * score_scale
    )
    probs = jnp.exp(scores_again - log_total)
    grad_probs = jnp.einsum(
        "lrhc,lthc->lhrt", grad_mixed, values_c, preferred_element_type=jnp.float32
    )
    grad_values_c = jnp.einsum(
        "lhrt,lrhc->lthc", to_low(probs), grad_mixed, preferred_element_type=jnp.float32
    )
    grad_scores = to_low(probs * (grad_probs - jnp.sum(probs * grad_probs, axis=-1, keepdims=True)))
    grad_query_c = to_low(
        jnp.einsum("lhrt,lthc->lrhc", grad_scores, keys_c, preferred_element_type=jnp.float32)
        * score_scale
    ).reshape(lat_dev, tokens_dev, D)
    grad_keys_c = (
        jnp.einsum("lhrt,lrhc->lthc", grad_scores, query_c, preferred_element_type=jnp.float32)
        * score_scale
    )
    grad_keyval_part = jnp.concatenate(
        [grad_keys_c.reshape(lat_dev, text_len, D), grad_values_c.reshape(lat_dev, text_len, D)],
        axis=-1,
    )
    grad_keyval_part = grad_keyval_part.reshape(lat_dev, text_len, segs, 2 * D // segs)
    grad_keyval = to_low(
        lax.psum_scatter(
            grad_keyval_part.astype(jnp.bfloat16), "seq", scatter_dimension=2, tiled=True
        ).astype(jnp.float32)
    ).reshape(lat_dev, text_len, 2 * D // segs)
    grad_w_cross_kv = outer_sum(text, grad_keyval)
    grad_first = grad_second + matmul_t(grad_query_c, w_cross_q)
    grad_gate_one = jnp.sum(grad_first * branch_one, axis=1)
    grad_branch_one = to_low(grad_first * gate_one)
    grad_branch_one, y_point, y_inner = lax.optimization_barrier(
        (grad_branch_one, *collect([grad_branch_two, grad_inner]))
    )
    grad_attended = matmul_t(grad_branch_one, w_attn_out).reshape(
        lat_dev, tokens_dev, heads_lin, 32
    )
    grad_numer = grad_attended / denominator[..., None]
    grad_denom = -jnp.sum(grad_attended * attn_val, axis=-1) / denominator
    grad_query = (
        jnp.einsum("lrhe,lhde->lrhd", grad_numer, kv_state, precision=precise)
        + grad_denom[..., None] * key_sum[:, None]
    )
    state_grad_part = jnp.einsum("lrhd,lrhe->lhde", query_f, grad_numer, precision=precise)
    sum_grad_part = jnp.einsum("lrhd,lrh->lhd", query_f, grad_denom, precision=precise)
    state_grad, sum_grad = state_sum(state_grad_part, sum_grad_part, jnp.bfloat16, 3)
    keys_f = keys_lin.astype(jnp.float32)
    values_f = values_lin.astype(jnp.float32)
    grad_keys = (
        jnp.einsum("lrhe,lhde->lrhd", values_f, state_grad, precision=precise) + sum_grad[:, None]
    )
    grad_values = jnp.einsum("lrhd,lhde->lrhe", keys_f, state_grad, precision=precise)
    grad_projected = to_low(
        jnp.concatenate(
            [
                grad_query.reshape(lat_dev, tokens_dev, D) * (query_pre > 0.0),
                grad_keys.reshape(lat_dev, tokens_dev, D) * (key_pre > 0.0),
                grad_values.reshape(lat_dev, tokens_dev, D),
            ],
            axis=-1,
        )
    )
    grad_projected, y_cross_out, y_cross_q, y_attn = lax.optimization_barrier(
        (grad_projected, *collect([grad_cross_out, grad_query_c, grad_branch_one]))
    )
    grad_hidden_one = matmul_t(grad_projected, w_qkv)
    grad_input = grad_first + norm_back(
        grad_hidden_one * (1.0 + scale_one), normed_one, inverse_one
    )
    grad_table = jnp.sum(
        jnp.stack(
            [
                jnp.sum(grad_hidden_one, axis=1),
                jnp.sum(grad_hidden_one * normed_one, axis=1),
                grad_gate_one,
                grad_shift_two,
                grad_scale_two,
                grad_gate_two,
            ],
            axis=1,
        ),
        axis=0,
    )
    grad_table = lax.optimization_barrier(grad_table)
    col_d = D // segs
    col_ff = 2 * FF // segs
    small_parts = jnp.concatenate(
        [
            grad_table.reshape(6, segs, col_d).transpose(1, 0, 2).reshape(segs, -1),
            grad_w_depth.reshape(9, segs, col_ff).transpose(1, 0, 2).reshape(segs, -1),
            grad_b_depth.reshape(segs, col_ff),
        ],
        axis=1,
    ).astype(jnp.bfloat16)
    small_parts = small_parts.reshape(segs, -1, LANE)
    small_mine = (
        lax.psum_scatter(small_parts, "seq", scatter_dimension=0, tiled=True)
        .astype(jnp.float32)
        .reshape(-1)
    )
    table_q = small_mine[: 6 * col_d].reshape(6, col_d)
    depth_q = small_mine[6 * col_d : 6 * col_d + 9 * col_ff].reshape(9, col_ff)
    depth_bias_q = small_mine[6 * col_d + 9 * col_ff :].reshape(1, col_ff)

    (y_qkv,) = collect([grad_projected])
    grad_w_qkv = outer_sum(x_qkv, y_qkv)
    grad_w_attn_out = outer_sum(x_attn, y_attn)
    grad_w_cross_q = outer_sum(x_cross_q, y_cross_q)
    grad_w_cross_out = outer_sum(x_cross_out, y_cross_out)
    grad_w_in = outer_sum(x_inner, y_inner)
    grad_w_point = outer_sum(x_point, y_point)
    grad_b_attn_out = jnp.sum(y_attn, axis=0, dtype=jnp.float32)
    grad_b_cross_out = jnp.sum(y_cross_out, axis=0, dtype=jnp.float32)
    grad_b_in = jnp.sum(y_inner, axis=0, dtype=jnp.float32)
    grad_b_point = jnp.sum(y_point, axis=0, dtype=jnp.float32)
    bias_part = jnp.concatenate(
        [grad_b_attn_out, grad_b_cross_out, grad_b_in, depth_bias_q.ravel(), grad_b_point]
    )
    len_bias = bias_part.size
    bias_rows = -(-bias_part.size // (8 * LANE)) * 8
    bias_part = jnp.pad(bias_part, (0, bias_rows * LANE - bias_part.size)).reshape(-1, LANE)
    quarter_grad = write_flat(
        segs,
        [
            table_q,
            grad_w_qkv,
            grad_w_attn_out,
            grad_b_attn_out,
            grad_w_cross_q,
            grad_w_cross_kv,
            grad_w_cross_out,
            grad_b_cross_out,
            grad_w_in,
            grad_b_in,
            depth_q,
            depth_bias_q,
            grad_w_point,
            grad_b_point,
        ],
    )
    if count_dp == 8 and quarter_grad.shape[0] % (8 * 240) == 0:
        grad_shard = reduce_shard(quarter_grad)
    else:
        grad_shard = lax.psum_scatter(
            quarter_grad.reshape(count_dp, -1, LANE), "dp", scatter_dimension=0, tiled=True
        ).reshape(-1, LANE)
    *flat_outs, bias_grads = finish(
        grad_shard,
        bias_part,
        params_rows,
        moment_one.reshape(-1, LANE),
        moment_two.reshape(-1, LANE),
    )
    gradient, moment_one_new, moment_two_new, update = [
        value.reshape(params.shape) for value in flat_outs
    ]
    return (
        output,
        grad_input.reshape(latents.shape),
        gradient,
        moment_one_new,
        moment_two_new,
        update,
        bias_grads.reshape(1, -1)[:, :len_bias],
    )


def solution(mesh):
    return jax.shard_map(
        shards,
        mesh=mesh,
        in_specs=(
            P("dp", "seq", None, None),
            P("dp", None, None),
            P("dp", None),
            P("dp", "seq", None, None),
            P("seq", "dp"),
            P("seq", "dp"),
            P("seq", "dp"),
        ),
        out_specs=(
            P("dp", "seq", None, None),
            P("dp", "seq", None, None),
            P("seq", "dp"),
            P("seq", "dp"),
            P("seq", "dp"),
            P("seq", "dp"),
            P("seq", None),
        ),
        check_vma=False,
    )
```

```python
import math

import jax
import jax.numpy as jnp
from jax import lax
from jax.experimental import pallas as pl
from jax.experimental.pallas import tpu as pltpu
from jax.sharding import PartitionSpec as P

D = 1152
FF = 2880
CROSS_HEADS = 16


precise = lax.Precision.HIGHEST
eps_norm = 1e-06
eps_linear = 1e-06
beta_first = 0.9
beta_second = 0.95
adam_eps = 1e-08
weight_decay = 0.01
adam_steps = 100.0


def with_halo(block, sides, width):
    for axis, dim in sides:
        count = lax.axis_size(axis)
        forward = [(i, i + 1) for i in range(count - 1)]
        backward = [(target, source) for source, target in forward]
        low = lax.ppermute(
            lax.slice_in_dim(block, block.shape[dim] - width, None, axis=dim), axis, forward
        )
        high = lax.ppermute(lax.slice_in_dim(block, 0, width, axis=dim), axis, backward)
        block = jnp.concatenate([low, block, high], axis=dim)
    return block


def piece_specs():
    return [
        (6, D, False),
        (D, 3 * D, False),
        (D, D, False),
        (1, D, True),
        (D, D, False),
        (D, 2 * D, False),
        (D, D, False),
        (1, D, True),
        (D, 2 * FF, False),
        (1, 2 * FF, True),
        (9, 2 * FF, False),
        (1, 2 * FF, True),
        (FF, D, False),
        (1, D, True),
    ]


LANE = 128
UNIT = 32
MESH = pl.DeviceIdType.MESH


def merge_units(values, lane_unit):
    out = values[0]
    last = values[0]
    for position in range(1, 4):
        if values[position] is not last:
            out = jnp.where(lane_unit >= position, values[position], out)
            last = values[position]
    return out


def rolled(value, units):
    units = units % 4
    return value if units == 0 else pltpu.roll(value, units * UNIT, 1)


def matrix_rows(count_rows):
    return 192 if count_rows % 192 == 0 else 64


def read_matrix(flat, offset, rows_of, cols_of, segs):
    total_rows = flat.shape[1]
    per_row = cols_of // segs // UNIT
    unit_at = offset // UNIT
    block = matrix_rows(rows_of)
    base = unit_at // 4 // 16 * 16
    shift = unit_at - 4 * base
    step = block * per_row // 4
    need = (shift + block * per_row - 1) // 4 + 1
    need = -(-need // 16) * 16
    assert base + (rows_of // block - 1) * step + need <= total_rows
    tiles = cols_of // LANE

    def kernel(in_ref, out_ref, wide, mixed):
        def widen(at, _):
            row = pl.multiple_of(at * 16, 16)
            for seg in range(segs):
                wide[pl.ds(pl.multiple_of(seg * need + row, 16), 16), :] = in_ref[
                    seg, pl.ds(row, 16), :
                ].astype(jnp.float32)
            return 0

        lax.fori_loop(0, need // 16, widen, 0, unroll=8)
        lane_unit = lax.broadcasted_iota(jnp.int32, (8, LANE), 1) // UNIT

        def group(at, _):
            for phase in range(4):
                loaded = {}
                turned = {}
                for tile in range(tiles):
                    parts = []
                    for slot in range(4):
                        col = 4 * tile + slot
                        seg, unit = col // per_row, col % per_row
                        source = shift + phase * per_row + unit
                        key = (seg, source // 4)
                        if key not in loaded:
                            loaded[key] = wide[
                                pl.ds(seg * need + key[1] + at * (8 * per_row), 8, stride=per_row),
                                :,
                            ]
                        turn = (slot - source) % 4
                        if (key, turn) not in turned:
                            turned[key, turn] = rolled(loaded[key], turn)
                        parts.append(turned[key, turn])
                    mixed[pl.ds(tile * block + phase + at * 32, 8, stride=4), :] = merge_units(
                        parts, lane_unit
                    )
            return 0

        lax.fori_loop(0, block // 32, group, 0, unroll=2)

        def narrow(at, _):
            row = pl.multiple_of(at * 16, 16)
            for tile in range(tiles):
                out_ref[pl.ds(row, 16), tile * LANE : (tile + 1) * LANE] = mixed[
                    pl.ds(pl.multiple_of(tile * block + row, 16), 16), :
                ].astype(jnp.bfloat16)
            return 0

        lax.fori_loop(0, block // 16, narrow, 0, unroll=2)

    return pl.pallas_call(
        kernel,
        grid=(rows_of // block,),
        in_specs=[
            pl.BlockSpec(
                (pl.Element(segs), pl.Element(need), pl.Element(LANE)),
                lambda at: (0, pl.multiple_of(base + at * step, 16), 0),
            )
        ],
        out_specs=pl.BlockSpec((block, cols_of), lambda at: (at, 0)),
        out_shape=jax.ShapeDtypeStruct((rows_of, cols_of), jnp.bfloat16),
        scratch_shapes=[
            pltpu.VMEM((segs * need, LANE), jnp.float32),
            pltpu.VMEM((tiles * block, LANE), jnp.float32),
        ],
        compiler_params=pltpu.CompilerParams(vmem_limit_bytes=48 << 20),
        cost_estimate=pl.CostEstimate(
            flops=0, bytes_accessed=4 * rows_of * cols_of, transcendentals=0
        ),
        name="read_matrix",
    )(flat)


def write_flat(segs, parts):
    specs = piece_specs()
    block_rows = 192
    total = sum(rows_of * cols_of // segs for rows_of, cols_of, _ in specs)
    flat_rows = total // LANE
    places = []
    offset = 0
    big, small = [], []
    for (rows_of, cols_of, _), value in zip(specs, parts):
        width = cols_of // segs
        length = rows_of * width
        if rows_of > 9:
            assert rows_of % block_rows == 0
            places.append((True, offset, rows_of, width, len(big)))
            big.append(value)
        else:
            lead = offset % LANE
            rest = -(lead + length) % LANE
            padded = jnp.pad(value.reshape(-1), (lead, rest)).reshape(-1, LANE)
            places.append((False, offset, length, None, len(small)))
            small.append(padded)
        offset += length
    widths = sorted({place[3] for place in places if place[0]})
    chunk = 144

    def kernel(*refs):
        big_refs = refs[: len(big)]
        small_refs = refs[len(big) : len(big) + len(small)]
        out_ref = refs[len(big) + len(small)]
        flat = refs[len(big) + len(small) + 1]
        bufs = refs[len(big) + len(small) + 2 : len(big) + len(small) + 2 + len(widths)]
        in_sem = refs[-1]
        lane_unit = lax.broadcasted_iota(jnp.int32, (8, LANE), 1) // UNIT
        row_unit = lax.broadcasted_iota(jnp.int32, (1, LANE), 1) // UNIT

        def place_small(ref, offset, length):
            first = offset // LANE
            last = (offset + length - 1) // LANE
            lead = offset % LANE // UNIT
            tail = (offset + length) % LANE // UNIT
            count = last - first + 1
            if count > 2:

                def copy_row(at, _):
                    flat[pl.ds(first + 1 + at, 1), :] = ref[pl.ds(1 + at, 1), :]
                    return 0

                lax.fori_loop(0, count - 2, copy_row, 0)
            keep = row_unit >= lead
            if count == 1 and tail:
                keep = keep & (row_unit < tail)
            flat[first : first + 1, :] = jnp.where(keep, ref[0:1, :], flat[first : first + 1, :])
            if count > 1:
                flat[last : last + 1, :] = (
                    jnp.where(
                        row_unit < tail, ref[count - 1 : count, :], flat[last : last + 1, :]
                    )
                    if tail
                    else ref[count - 1 : count, :]
                )

        def fetch_block(ref, buf, width, at, slot):
            row = pl.multiple_of(at * block_rows, 64)
            return [
                pltpu.make_async_copy(
                    ref.at[pl.ds(row, block_rows), tile * LANE : (tile + 1) * LANE],
                    buf.at[slot, tile],
                    in_sem.at[widths.index(width), slot, tile],
                )
                for tile in range(-(-width // LANE))
            ]

        def place_big(ref, buf, offset, rows_of, width):
            per_row = width // UNIT
            first = offset // LANE
            shift = offset % LANE // UNIT
            block = block_rows
            blocks = rows_of // block

            def fetch(at, slot):
                return fetch_block(ref, buf, width, at, slot)

            def one_block(at, _):
                slot = lax.rem(at, 2)

                @pl.when(at + 1 < blocks)
                def _():
                    for copy in fetch(at + 1, 1 - slot):
                        copy.start()

                for copy in fetch(at, slot):
                    copy.wait()

                def group(sub, _):
                    loaded = {}
                    turned = {}

                    def unit_value(phase, unit, lane):
                        key = (phase, unit // 4)
                        if key not in loaded:
                            loaded[key] = buf[
                                slot, key[1], pl.ds(phase + sub * 32, 8, stride=4), :
                            ]
                        turn = (lane - unit) % 4
                        if (key, turn) not in turned:
                            turned[key, turn] = rolled(loaded[key], turn)
                        return turned[key, turn]

                    start = first + (at * (block // 4) + sub * 8) * per_row
                    for row in range(per_row + (1 if shift else 0)):
                        where = pl.ds(start + row, 8, stride=per_row)
                        parts = []
                        kept = None
                        for lane in range(4):
                            unit = 4 * row + lane - shift
                            if unit < 0 or unit >= 4 * per_row:
                                if kept is None:
                                    kept = flat[where, :]
                                parts.append(kept)
                            else:
                                parts.append(unit_value(unit // per_row, unit % per_row, lane))
                        flat[where, :] = merge_units(parts, lane_unit)
                    return 0

                lax.fori_loop(0, block // 32, group, 0, unroll=3)
                return 0

            lax.fori_loop(0, blocks, one_block, 0)

        def first_fetch(width, after):
            for is_big, _, _, other, index in places:
                if is_big and other == width and index > after:
                    buf = bufs[widths.index(width)]
                    for copy in fetch_block(big_refs[index], buf, width, 0, 0):
                        copy.start()
                    return

        for width in widths:
            first_fetch(width, -1)
        for is_big, offset, rows_of, width, index in places:
            if is_big:
                place_big(big_refs[index], bufs[widths.index(width)], offset, rows_of, width)
                first_fetch(width, index)
            else:
                place_small(small_refs[index], offset, rows_of)

        def narrow(at, _):
            where = pl.ds(pl.multiple_of(at * chunk, 16), chunk)
            out_ref[where, :] = flat[where, :].astype(jnp.bfloat16)
            return 0

        lax.fori_loop(0, flat_rows // chunk, narrow, 0)

    return pl.pallas_call(
        kernel,
        in_specs=[pl.BlockSpec(memory_space=pl.ANY)] * len(big)
        + [pl.BlockSpec(memory_space=pltpu.VMEM)] * len(small),
        out_specs=pl.BlockSpec(memory_space=pltpu.VMEM),
        out_shape=jax.ShapeDtypeStruct((flat_rows, LANE), jnp.bfloat16),
        scratch_shapes=[pltpu.VMEM((flat_rows, LANE), jnp.float32)]
        + [
            pltpu.VMEM((2, -(-width // LANE), block_rows, LANE), jnp.float32) for width in widths
        ]
        + [
            pltpu.SemaphoreType.DMA((len(widths), 2, -(-widths[-1] // LANE))),
        ],
        compiler_params=pltpu.CompilerParams(vmem_limit_bytes=56 << 20),
        cost_estimate=pl.CostEstimate(flops=0, bytes_accessed=6 * total, transcendentals=0),
        name="write_flat",
    )(*big, *small)


def gather_flat(shard):
    rows = shard.shape[0]
    first = (rows // 2 + 15) // 16 * 16
    parts = ((0, first), (first, rows - first))

    def kernel(
        in_ref,
        out_ref,
        own_sem,
        z_send,
        z_recv,
        x_send,
        x_recv,
        y_send,
        y_recv,
        d_send,
        d_recv,
        c_send,
        c_recv,
    ):
        dp = lax.axis_index("dp")
        seq = lax.axis_index("seq")
        near, far = lax.rem(dp, 2), lax.div(dp, 2)
        core, side = lax.rem(seq, 2), lax.div(seq, 2)

        half = lax.div(far, 2)
        place = far + half * (3 - 2 * far)
        inner = far + 1 - 2 * half
        outer = far - 1 + 2 * half

        def dp_of(turn, flip):
            at = place if turn == 0 else 1 - place if turn == 1 else turn
            return 2 * (at + half * (3 - 2 * at)) + (1 - near if flip else near)

        def seq_of(flip, other_core):
            return 2 * (1 - side if flip else side) + (1 - core if other_core else core)

        def region(seq_at, dp_at, part):
            start, length = parts[part]
            return out_ref.at[
                seq_at, pl.ds(pl.multiple_of(dp_at * rows + start, 16), length), :
            ]

        def own_region(part):
            start, length = parts[part]
            return in_ref.at[pl.ds(start, length), :]

        def column(turn, part):
            return region(seq, dp_of(turn, False), part)

        def source(turn, part):
            return column(turn, part) if turn else own_region(part)

        def remote(src, dst, send, recv, target):
            return pltpu.make_async_remote_copy(
                src_ref=src,
                dst_ref=dst,
                send_sem=send,
                recv_sem=recv,
                device_id=target,
                device_id_type=MESH,
            )

        x_peer = {"dp": dp_of(0, True)}
        y_peer = {"seq": seq_of(True, False)}
        c_peer = {"seq": seq_of(False, True)}

        def z_copy(kind, part):
            turn = (0, 0, 1, 2, 3)[kind]
            arrives = (place, 0, 2, 1, 2)[kind]
            return remote(
                source(turn, part),
                column(turn, part),
                z_send.at[kind, part],
                z_recv.at[arrives, part],
                {"dp": 2 * (inner if kind in (0, 2) else outer) + near},
            )

        def z_in(turn, part):
            here = column(turn, part)
            return remote(
                here, here, z_send.at[0, part], z_recv.at[turn - 1, part], {"dp": 2 * inner + near}
            )

        def x_out(turn, part):
            return remote(
                source(turn, part),
                column(turn, part),
                x_send.at[turn, part],
                x_recv.at[turn, part],
                x_peer,
            )

        def x_in(turn, part):
            here = region(seq, dp_of(turn, True), part)
            return remote(here, here, x_send.at[turn, part], x_recv.at[turn, part], x_peer)

        def y_out(turn, part):
            return remote(
                source(turn, part),
                column(turn, part),
                y_send.at[turn, part],
                y_recv.at[turn, part],
                y_peer,
            )

        def y_in(turn, part):
            here = region(seq_of(True, False), dp_of(turn, False), part)
            return remote(here, here, y_send.at[turn, part], y_recv.at[turn, part], y_peer)

        def d_out(turn, part):
            if part == 0:
                here, target = region(seq, dp_of(turn, True), part), y_peer
            else:
                here, target = region(seq_of(True, False), dp_of(turn, False), part), x_peer
            return remote(here, here, d_send.at[turn, part], d_recv.at[turn, part], target)

        def d_in(turn, part):
            here = region(seq_of(True, False), dp_of(turn, True), part)
            target = y_peer if part == 0 else x_peer
            return remote(here, here, d_send.at[turn, part], d_recv.at[turn, part], target)

        def c_copy(kind, turn, part, incoming):
            where = region(
                seq_of(kind in (2, 3), incoming), dp_of(turn, kind in (1, 3)), part
            )
            src = own_region(part) if kind == 0 and turn == 0 else where
            return remote(
                src if not incoming else where,
                where,
                c_send.at[kind, turn, part],
                c_recv.at[kind, turn, part],
                c_peer,
            )

        barrier = pltpu.get_barrier_semaphore()
        for target in (x_peer, y_peer, c_peer, {"dp": 2 * inner + near}):
            pl.semaphore_signal(barrier, inc=1, device_id=target, device_id_type=MESH)

        @pl.when(place == 1)
        def _():
            pl.semaphore_signal(
                barrier, inc=1, device_id={"dp": 2 * outer + near}, device_id_type=MESH
            )
            pl.semaphore_wait(barrier, 5)

        @pl.when(place == 0)
        def _():
            pl.semaphore_wait(barrier, 4)

        keep = [
            pltpu.make_async_copy(own_region(part), region(seq, dp, part), own_sem.at[part])
            for part in range(2)
        ]
        def outwards(kind, part):
            @pl.when(place == 1)
            def _():
                z_copy(kind, part).start()

        for part in range(2):
            z_copy(0, part).start()
            outwards(1, part)
            x_out(0, part).start()
            y_out(0, part).start()
        for part in range(2):
            keep[part].start()
            c_copy(0, 0, part, False).start()

        def sideways(turn):
            for part in range(2):
                x_in(turn, part).wait_recv()
                if part == 0:
                    d_out(turn, part).start()
                c_copy(1, turn, part, False).start()
                y_in(turn, part).wait_recv()
                if part == 1:
                    d_out(turn, part).start()
                c_copy(2, turn, part, False).start()

        def diagonal(turn):
            for part in range(2):
                d_in(turn, part).wait_recv()
                c_copy(3, turn, part, False).start()

        for turn in range(1, 4):
            for part in range(2):
                z_in(turn, part).wait_recv()
                outwards(turn + 1, part)
                x_out(turn, part).start()
                y_out(turn, part).start()
                c_copy(0, turn, part, False).start()
            sideways(turn - 1)
            if turn > 1:
                diagonal(turn - 2)
        sideways(3)
        diagonal(2)
        diagonal(3)

        @pl.when(place == 1)
        def _():
            for kind in range(1, 5):
                for part in range(2):
                    z_copy(kind, part).wait_send()

        for part in range(2):
            keep[part].wait()
            z_copy(0, part).wait_send()
            for turn in range(4):
                x_out(turn, part).wait_send()
                y_out(turn, part).wait_send()
                d_out(turn, part).wait_send()
                for kind in range(4):
                    c_copy(kind, turn, part, False).wait_send()
                    c_copy(kind, turn, part, True).wait_recv()

    return pl.pallas_call(
        kernel,
        in_specs=[pl.BlockSpec(memory_space=pltpu.VMEM)],
        out_specs=pl.BlockSpec(memory_space=pl.ANY),
        out_shape=jax.ShapeDtypeStruct((4, 8 * rows, LANE), jnp.bfloat16),
        scratch_shapes=[
            pltpu.SemaphoreType.DMA((2,)),
            pltpu.SemaphoreType.DMA((5, 2)),
            pltpu.SemaphoreType.DMA((3, 2)),
        ]
        + [pltpu.SemaphoreType.DMA((4, 2))] * 6
        + [pltpu.SemaphoreType.DMA((4, 4, 2))] * 2,
        compiler_params=pltpu.CompilerParams(collective_id=5, has_side_effects=True),
        name="gather_flat",
    )(shard)


def round_rows(values):
    def kernel(in_ref, out_ref):
        out_ref[...] = in_ref[...].astype(jnp.bfloat16)

    return pl.pallas_call(
        kernel,
        in_specs=[pl.BlockSpec(memory_space=pltpu.VMEM)],
        out_specs=pl.BlockSpec(memory_space=pltpu.VMEM),
        out_shape=jax.ShapeDtypeStruct(values.shape, jnp.bfloat16),
        name="round_rows",
    )(values)


def gather_weights(shard_low, segs):
    if segs == 4 and lax.axis_size("dp") == 8 and shard_low.shape[0] % 16 == 0:
        flat = gather_flat(shard_low)
    else:
        whole = lax.all_gather(shard_low, ("seq", "dp"), axis=0, tiled=True)
        flat = whole.reshape(segs, -1, LANE)
    pieces = []
    offset = 0
    for rows_of, cols_of, vector in piece_specs():
        length = rows_of * cols_of // segs
        if rows_of > 9:
            pieces.append(read_matrix(flat, offset, rows_of, cols_of, segs))
        else:
            first, last = offset // LANE, -(-(offset + length) // LANE)
            lead = offset - first * LANE
            block = flat[:, first:last].reshape(segs, -1)[:, lead : lead + length]
            block = block.reshape(segs, rows_of, cols_of // segs).transpose(1, 0, 2)
            pieces.append(block.reshape(cols_of) if vector else block.reshape(rows_of, cols_of))
        offset = offset + length
    return pieces


def peer_barrier(groups):
    barrier = pltpu.get_barrier_semaphore()
    total = 0
    for axis, count in groups:
        me = lax.axis_index(axis)
        for step in range(1, count):
            pl.semaphore_signal(
                barrier, inc=1, device_id={axis: lax.rem(me + step, count)}, device_id_type=MESH
            )
        total += count - 1
    pl.semaphore_wait(barrier, total)


def exchange(axis, count, source, slots, send_sem, recv_sem):
    me = lax.axis_index(axis)
    for step in range(1, count):
        pltpu.make_async_remote_copy(
            src_ref=source,
            dst_ref=slots.at[me],
            send_sem=send_sem.at[step - 1],
            recv_sem=recv_sem.at[me],
            device_id={axis: lax.rem(me + step, count)},
            device_id_type=MESH,
        ).start()


def exchange_wait(axis, count, source, slots, send_sem, recv_sem):
    me = lax.axis_index(axis)
    for step in range(1, count):
        peer = lax.rem(me + step, count)
        copy = pltpu.make_async_remote_copy(
            src_ref=source,
            dst_ref=slots.at[peer],
            send_sem=send_sem.at[step - 1],
            recv_sem=recv_sem.at[peer],
            device_id={axis: peer},
            device_id_type=MESH,
        )
        copy.wait_send()
        copy.wait_recv()


def in_order(axis, count, own, slots):
    me = lax.axis_index(axis)
    total = None
    for index in range(count):
        term = jnp.where(me == index, own, slots[index].astype(jnp.float32))
        total = term if total is None else total + term
    return total


def seq_sum(block, collective_id):
    count = lax.axis_size("seq")

    def kernel(in_ref, out_ref, slots, send_sem, recv_sem):
        peer_barrier([("seq", count)])
        exchange("seq", count, in_ref, slots, send_sem, recv_sem)
        exchange_wait("seq", count, in_ref, slots, send_sem, recv_sem)
        out_ref[...] = in_order("seq", count, in_ref[...].astype(jnp.float32), slots)

    return pl.pallas_call(
        kernel,
        in_specs=[pl.BlockSpec(memory_space=pltpu.VMEM)],
        out_specs=pl.BlockSpec(memory_space=pltpu.VMEM),
        out_shape=jax.ShapeDtypeStruct(block.shape, jnp.float32),
        scratch_shapes=[
            pltpu.VMEM((count,) + block.shape, block.dtype),
            pltpu.SemaphoreType.DMA((count - 1,)),
            pltpu.SemaphoreType.DMA((count,)),
        ],
        compiler_params=pltpu.CompilerParams(collective_id=collective_id, has_side_effects=True),
        name="seq_sum",
    )(block)


def state_sum(state, sums, kind, collective_id):
    heads = state.shape[1]
    flat = jnp.concatenate(
        [state.reshape(-1, LANE), jnp.pad(sums.reshape(-1), (0, -sums.size % LANE)).reshape(-1, LANE)]
    ).astype(kind)
    rows = flat.shape[0]
    flat = jnp.pad(flat, ((0, -rows % 16), (0, 0)))
    total = seq_sum(flat, collective_id)
    split = state.size // LANE
    return (
        total[:split].reshape(state.shape),
        total[split:].reshape(-1)[: sums.size].reshape(1, heads, -1),
    )


def reduce_shard(flat):
    rows = flat.shape[0] // 8
    pieces = 3
    part = rows // pieces
    step = 80

    def kernel(in_ref, out_ref, recv_x, send_z, recv_z, x_send, x_recv, z_send, z_recv):
        me = lax.axis_index("dp")
        near = lax.rem(me, 2)
        far = lax.div(me, 2)
        partner = me + 1 - 2 * near

        def far_of(shift):
            return lax.rem(far + shift, 4)

        barrier = pltpu.get_barrier_semaphore()
        pl.semaphore_signal(barrier, inc=1, device_id={"dp": partner}, device_id_type=MESH)
        for shift in range(1, 4):
            pl.semaphore_signal(
                barrier,
                inc=1,
                device_id={"dp": 2 * far_of(shift) + near},
                device_id_type=MESH,
            )
        pl.semaphore_wait(barrier, 4)

        def window(shard, piece):
            return pl.ds(pl.multiple_of(shard * rows + piece * part, 16), part)

        def x_copy(shift, piece):
            return pltpu.make_async_remote_copy(
                src_ref=in_ref.at[window(2 * far_of(shift) + 1 - near, piece), :],
                dst_ref=recv_x.at[shift, pl.ds(piece * part, part), :],
                send_sem=x_send.at[shift, piece],
                recv_sem=x_recv.at[shift, piece],
                device_id={"dp": partner},
                device_id_type=MESH,
            )

        def z_copy(shift, piece):
            return pltpu.make_async_remote_copy(
                src_ref=send_z.at[shift - 1, pl.ds(piece * part, part), :],
                dst_ref=recv_z.at[shift - 1, pl.ds(piece * part, part), :],
                send_sem=z_send.at[shift - 1, piece],
                recv_sem=z_recv.at[shift - 1, piece],
                device_id={"dp": 2 * far_of(shift) + near},
                device_id_type=MESH,
            )

        order = (1, 2, 3, 0)
        for shift in order:
            for piece in range(pieces):
                x_copy(shift, piece).start()

        def own_sum(shift, row, at):
            start = (2 * far_of(shift) + near) * rows + row + at * step
            own = in_ref[pl.ds(pl.multiple_of(start, 16), step), :]
            other = recv_x[shift, pl.ds(pl.multiple_of(row + at * step, 16), step), :]
            return own.astype(jnp.float32) + other.astype(jnp.float32)

        for shift in order:
            for piece in range(pieces):
                x_copy(shift, piece).wait_recv()
                row = piece * part

                def add(at, _, shift=shift, row=row):
                    where = pl.ds(pl.multiple_of(row + at * step, 16), step)
                    total = own_sum(shift, row, at)
                    if shift:
                        send_z[shift - 1, where, :] = total.astype(jnp.bfloat16)
                    else:
                        out_ref[where, :] = total
                    return 0

                lax.fori_loop(0, part // step, add, 0)
                if shift:
                    z_copy(shift, piece).start()
        for shift in range(1, 4):
            for piece in range(pieces):
                z_copy(shift, piece).wait_recv()
                row = piece * part

                def gather(at, _, shift=shift, row=row):
                    where = pl.ds(pl.multiple_of(row + at * step, 16), step)
                    out_ref[where, :] = out_ref[where, :] + recv_z[shift - 1, where, :].astype(
                        jnp.float32
                    )
                    return 0

                lax.fori_loop(0, part // step, gather, 0)
        for shift in range(4):
            for piece in range(pieces):
                x_copy(shift, piece).wait_send()
                if shift:
                    z_copy(shift, piece).wait_send()

    block = (rows, LANE)
    return pl.pallas_call(
        kernel,
        in_specs=[pl.BlockSpec(memory_space=pltpu.VMEM)],
        out_specs=pl.BlockSpec(memory_space=pltpu.VMEM),
        out_shape=jax.ShapeDtypeStruct(block, jnp.float32),
        scratch_shapes=[
            pltpu.VMEM((4,) + block, jnp.bfloat16),
            pltpu.VMEM((3,) + block, jnp.bfloat16),
            pltpu.VMEM((3,) + block, jnp.bfloat16),
            pltpu.SemaphoreType.DMA((4, pieces)),
            pltpu.SemaphoreType.DMA((4, pieces)),
            pltpu.SemaphoreType.DMA((3, pieces)),
            pltpu.SemaphoreType.DMA((3, pieces)),
        ],
        compiler_params=pltpu.CompilerParams(
            collective_id=4, has_side_effects=True, vmem_limit_bytes=40 << 20
        ),
        name="reduce_shard",
    )(flat)


def scale_of(grad_shard, bias_part):
    rows = grad_shard.shape[0]
    count_dp = lax.axis_size("dp")
    count_seq = lax.axis_size("seq")
    entries = rows * LANE * count_dp * count_seq
    chunk = 48 if rows % 48 == 0 else rows
    bias_rows = bias_part.shape[0]

    def kernel(
        grad_ref,
        bias_ref,
        factor_out,
        bias_out,
        square,
        square_dp,
        square_seq,
        partial,
        bias_slots,
        send_bias,
        recv_bias,
        send_dp,
        recv_dp,
        send_seq,
        recv_seq,
    ):
        peer_barrier([("dp", count_dp), ("seq", count_seq)])
        exchange("dp", count_dp, bias_ref, bias_slots, send_bias, recv_bias)

        def squares(at, total):
            part = grad_ref[pl.ds(at * chunk, chunk), :].astype(jnp.float32)
            return total + jnp.sum(part * part, axis=0, keepdims=True)

        total = lax.fori_loop(0, rows // chunk, squares, jnp.zeros((1, LANE), jnp.float32))
        square[...] = jnp.broadcast_to(total, (8, LANE))
        exchange("dp", count_dp, square, square_dp, send_dp, recv_dp)
        exchange_wait("dp", count_dp, square, square_dp, send_dp, recv_dp)
        partial[...] = in_order("dp", count_dp, square[...], square_dp)
        exchange("seq", count_seq, partial, square_seq, send_seq, recv_seq)
        exchange_wait("seq", count_seq, partial, square_seq, send_seq, recv_seq)
        whole = jnp.sum(
            in_order("seq", count_seq, partial[...], square_seq)[0:1], axis=1, keepdims=True
        )
        factor = lax.rsqrt(whole / entries + 1e-06)
        exchange_wait("dp", count_dp, bias_ref, bias_slots, send_bias, recv_bias)
        bias_out[...] = in_order("dp", count_dp, bias_ref[...], bias_slots) * factor
        factor_out[...] = jnp.broadcast_to(factor, (8, LANE))

    tile = (8, LANE)
    return pl.pallas_call(
        kernel,
        in_specs=[pl.BlockSpec(memory_space=pltpu.VMEM)] * 2,
        out_specs=[pl.BlockSpec(memory_space=pltpu.VMEM)] * 2,
        out_shape=[
            jax.ShapeDtypeStruct(tile, jnp.float32),
            jax.ShapeDtypeStruct((bias_rows, LANE), jnp.float32),
        ],
        scratch_shapes=[
            pltpu.VMEM(tile, jnp.float32),
            pltpu.VMEM((count_dp,) + tile, jnp.float32),
            pltpu.VMEM((count_seq,) + tile, jnp.float32),
            pltpu.VMEM(tile, jnp.float32),
            pltpu.VMEM((count_dp, bias_rows, LANE), jnp.float32),
            pltpu.SemaphoreType.DMA((count_dp - 1,)),
            pltpu.SemaphoreType.DMA((count_dp,)),
            pltpu.SemaphoreType.DMA((count_dp - 1,)),
            pltpu.SemaphoreType.DMA((count_dp,)),
            pltpu.SemaphoreType.DMA((count_seq - 1,)),
            pltpu.SemaphoreType.DMA((count_seq,)),
        ],
        compiler_params=pltpu.CompilerParams(
            collective_id=1, has_side_effects=True, vmem_limit_bytes=16 << 20
        ),
        name="scale_of",
    )(grad_shard, bias_part)


def adam(factor, grad_shard, params, moment_one, moment_two):
    rows = grad_shard.shape[0]
    block = 504 if rows % 504 == 0 else rows

    def kernel(
        factor_ref, grad_ref, param_ref, one_ref, two_ref, gradient_ref, one_out, two_out, update_ref
    ):
        gradient = grad_ref[...] * factor_ref[0:1, :]
        first = beta_first * one_ref[...] + (1.0 - beta_first) * gradient
        second = beta_second * two_ref[...] + (1.0 - beta_second) * gradient * gradient
        gradient_ref[...] = gradient
        one_out[...] = first
        two_out[...] = second
        first_hat = first / (1.0 - beta_first**adam_steps)
        second_hat = second / (1.0 - beta_second**adam_steps)
        update_ref[...] = (
            first_hat / (jnp.sqrt(second_hat) + adam_eps) + weight_decay * param_ref[...]
        )

    spec = pl.BlockSpec((block, LANE), lambda at: (at, 0))
    return pl.pallas_call(
        kernel,
        grid=(rows // block,),
        in_specs=[pl.BlockSpec((8, LANE), lambda at: (0, 0))] + [spec] * 4,
        out_specs=[spec] * 4,
        out_shape=[jax.ShapeDtypeStruct((rows, LANE), jnp.float32)] * 4,
        name="adam",
    )(factor, grad_shard, params, moment_one, moment_two)


def norm_parts(values):
    centred = values - jnp.mean(values, axis=-1, keepdims=True)
    inverse = lax.rsqrt(jnp.mean(centred * centred, axis=-1, keepdims=True) + eps_norm)
    return (centred * inverse, inverse)


def norm_back(grad_normed, normed, inverse):
    return inverse * (
        grad_normed
        - jnp.mean(grad_normed, axis=-1, keepdims=True)
        - normed * jnp.mean(grad_normed * normed, axis=-1, keepdims=True)
    )


def silu_slope(values):
    sigmoid_v = jax.nn.sigmoid(values)
    return sigmoid_v * (1.0 + values * (1.0 - sigmoid_v))


def to_low(values):
    return values.astype(jnp.bfloat16)


def matmul(left_op, right_op):
    return jnp.dot(left_op, right_op, preferred_element_type=jnp.float32)


def matmul_t(left_op, right_op):
    return lax.dot_general(
        left_op,
        right_op,
        (((left_op.ndim - 1,), (1,)), ((), ())),
        preferred_element_type=jnp.float32,
    )


def outer_sum(left_op, right_op):
    left_flat = left_op.reshape(-1, left_op.shape[-1])
    right_flat = right_op.reshape(-1, right_op.shape[-1])
    right_flat = jnp.pad(right_flat, ((0, 0), (0, -right_flat.shape[1] % LANE)))
    return lax.dot_general(
        left_flat, right_flat, (((0,), (0,)), ((), ())), preferred_element_type=jnp.float32
    )


def depth_conv(padded, kernel, row_dev, col_dev, flipped):
    kernel_f = kernel.astype(jnp.float32)
    summed = jnp.zeros(padded.shape[:1] + (row_dev, col_dev) + padded.shape[3:], jnp.float32)
    for tap_row in range(3):
        for tap_col in range(3):
            row_at = 2 - tap_row if flipped else tap_row
            col_at = 2 - tap_col if flipped else tap_col
            summed = (
                summed
                + kernel_f[tap_row * 3 + tap_col]
                * padded[:, row_at : row_at + row_dev, col_at : col_at + col_dev, :]
            )
    return summed


def shards(latents, text, time_embed, cotangent, params, moment_one, moment_two):
    lat_dev, row_dev, col_dev, width = latents.shape
    tokens_dev = row_dev * col_dev
    heads_lin = D // 32
    cross_dim = D // CROSS_HEADS
    score_scale = 1.0 / math.sqrt(cross_dim)
    text_len = text.shape[1]
    segs = lax.axis_size("seq")
    count_dp = lax.axis_size("dp")
    def spread(values):
        joined = jnp.concatenate(values, axis=-1).reshape(-1, sum(v.shape[-1] for v in values))
        whole = lax.all_gather(joined, "seq", axis=0, tiled=True)
        parts = []
        at = 0
        for value in values:
            parts.append(whole[:, at : at + value.shape[-1]])
            at += value.shape[-1]
        return parts

    def collect(values):
        blocks = jnp.stack(
            [
                jnp.concatenate(
                    [
                        value.reshape(-1, value.shape[-1])[
                            :, seg * (value.shape[-1] // segs) : (seg + 1) * (value.shape[-1] // segs)
                        ]
                        for value in values
                    ],
                    axis=1,
                )
                for seg in range(segs)
            ]
        )
        mine = lax.all_to_all(blocks, "seq", split_axis=0, concat_axis=0, tiled=True)
        mine = mine.reshape(-1, mine.shape[-1])
        parts = []
        at = 0
        for value in values:
            width = value.shape[-1] // segs
            parts.append(mine[:, at : at + width])
            at += width
        return parts

    params_rows = params.reshape(-1, LANE)
    shard_low = round_rows(params_rows)
    (
        mod_table,
        w_qkv,
        w_attn_out,
        b_attn_out,
        w_cross_q,
        w_cross_kv,
        w_cross_out,
        b_cross_out,
        w_in,
        b_in,
        w_depth,
        b_depth,
        w_point,
        b_point,
    ) = gather_weights(shard_low, segs)
    modulation = mod_table.astype(jnp.float32)[None] + time_embed.reshape(lat_dev, 6, D)
    shift_one = modulation[:, 0][:, None, :]
    scale_one = modulation[:, 1][:, None, :]
    gate_one = modulation[:, 2][:, None, :]
    shift_two = modulation[:, 3][:, None, :]
    scale_two = modulation[:, 4][:, None, :]
    gate_two = modulation[:, 5][:, None, :]
    tokens = latents.reshape(lat_dev, tokens_dev, D).astype(jnp.float32)
    normed_one, inverse_one = norm_parts(tokens)
    hidden_one = to_low(normed_one * (1.0 + scale_one) + shift_one)
    projected = matmul(hidden_one, w_qkv)
    query_pre = projected[..., :D]
    key_pre = projected[..., D : 2 * D]
    queries = to_low(jnp.maximum(query_pre, 0.0)).reshape(lat_dev, tokens_dev, heads_lin, 32)
    keys_lin = to_low(jnp.maximum(key_pre, 0.0)).reshape(lat_dev, tokens_dev, heads_lin, 32)
    values_lin = to_low(projected[..., 2 * D :]).reshape(lat_dev, tokens_dev, heads_lin, 32)
    state_part = jnp.einsum(
        "lrhd,lrhe->lhde", keys_lin, values_lin, preferred_element_type=jnp.float32
    )
    sum_part = jnp.sum(keys_lin, axis=1, dtype=jnp.float32)
    kv_state, key_sum = state_sum(state_part, sum_part, jnp.float32, 2)
    query_f = queries.astype(jnp.float32)
    numerator = jnp.einsum("lrhd,lhde->lrhe", query_f, kv_state, precision=precise)
    denominator = jnp.einsum("lrhd,lhd->lrh", query_f, key_sum, precision=precise) + eps_linear
    attn_val = numerator / denominator[..., None]
    attended = to_low(attn_val.reshape(lat_dev, tokens_dev, D))
    branch_one = matmul(attended, w_attn_out) + b_attn_out.astype(jnp.float32)
    after_attn = tokens + gate_one * branch_one
    after_low, x_qkv = lax.optimization_barrier((to_low(after_attn), *spread([hidden_one])))
    query_c = to_low(matmul(after_low, w_cross_q)).reshape(
        lat_dev, tokens_dev, CROSS_HEADS, cross_dim
    )
    keyval = to_low(matmul(text, w_cross_kv))
    keys_c = keyval[..., :D].reshape(lat_dev, text_len, CROSS_HEADS, cross_dim)
    values_c = keyval[..., D:].reshape(lat_dev, text_len, CROSS_HEADS, cross_dim)
    scores = (
        jnp.einsum("lrhc,lthc->lhrt", query_c, keys_c, preferred_element_type=jnp.float32)
        * score_scale
    )
    row_peak = jnp.max(scores, axis=-1, keepdims=True)
    log_total = row_peak + jnp.log(jnp.sum(jnp.exp(scores - row_peak), axis=-1, keepdims=True))
    probs_low = to_low(jnp.exp(scores - log_total))
    cross_mixed = to_low(
        jnp.einsum(
            "lhrt,lthc->lrhc", probs_low, values_c, preferred_element_type=jnp.float32
        ).reshape(lat_dev, tokens_dev, D)
    )
    after_cross = after_attn + matmul(cross_mixed, w_cross_out) + b_cross_out.astype(jnp.float32)
    normed_two, inverse_two = norm_parts(after_cross)
    hidden_two, x_attn, x_cross_q = lax.optimization_barrier(
        (
            to_low(normed_two * (1.0 + scale_two) + shift_two),
            *spread([attended, after_low]),
        )
    )
    inner_pre = matmul(hidden_two, w_in) + b_in.astype(jnp.float32)
    active = to_low(jax.nn.silu(inner_pre)).reshape(lat_dev, row_dev, col_dev, 2 * FF)
    padded = jnp.pad(with_halo(active, (("seq", 1),), 1), ((0, 0), (0, 0), (1, 1), (0, 0)))
    conv_out = (
        depth_conv(padded, w_depth, row_dev, col_dev, False) + b_depth.astype(jnp.float32)
    ).reshape(lat_dev, tokens_dev, 2 * FF)
    up_part = conv_out[..., :FF]
    gate_part = conv_out[..., FF:]
    gated_mix = to_low(up_part * jax.nn.silu(gate_part))
    branch_two = lax.optimization_barrier(
        matmul(gated_mix, w_point) + b_point.astype(jnp.float32)
    )
    output = (after_cross + gate_two * branch_two).astype(jnp.bfloat16).reshape(latents.shape)
    grad_out = cotangent.reshape(lat_dev, tokens_dev, D).astype(jnp.float32)
    grad_gate_two = jnp.sum(grad_out * branch_two, axis=1)
    grad_branch_two = to_low(grad_out * gate_two)
    grad_branch_two, x_cross_out, x_inner = lax.optimization_barrier(
        (grad_branch_two, *spread([cross_mixed, hidden_two]))
    )
    grad_gated = matmul_t(grad_branch_two, w_point)
    grad_up = grad_gated * jax.nn.silu(gate_part)
    grad_gate = grad_gated * up_part * silu_slope(gate_part)
    grad_conv = to_low(jnp.concatenate([grad_up, grad_gate], axis=-1)).reshape(
        lat_dev, row_dev, col_dev, 2 * FF
    )
    grad_b_depth = jnp.sum(grad_conv, axis=(0, 1, 2), dtype=jnp.float32)
    tap_grads = []
    for tap_row in range(3):
        for tap_col in range(3):
            tap_grads.append(
                jnp.einsum(
                    "lrcf,lrcf->f",
                    padded[:, tap_row : tap_row + row_dev, tap_col : tap_col + col_dev],
                    grad_conv,
                    preferred_element_type=jnp.float32,
                )
            )
    grad_w_depth = jnp.stack(tap_grads)
    grad_padded = jnp.pad(with_halo(grad_conv, (("seq", 1),), 1), ((0, 0), (0, 0), (1, 1), (0, 0)))
    grad_active = depth_conv(grad_padded, w_depth, row_dev, col_dev, True).reshape(
        lat_dev, tokens_dev, 2 * FF
    )
    grad_inner = to_low(grad_active * silu_slope(inner_pre))
    grad_inner, x_point = lax.optimization_barrier((grad_inner, *spread([gated_mix])))
    grad_hidden_two = matmul_t(grad_inner, w_in)
    grad_shift_two = jnp.sum(grad_hidden_two, axis=1)
    grad_scale_two = jnp.sum(grad_hidden_two * normed_two, axis=1)
    grad_second = grad_out + norm_back(grad_hidden_two * (1.0 + scale_two), normed_two, inverse_two)
    grad_cross_out = to_low(grad_second)
    grad_mixed = to_low(matmul_t(grad_cross_out, w_cross_out)).reshape(
        lat_dev, tokens_dev, CROSS_HEADS, cross_dim
    )
    scores_again = (
        jnp.einsum("lrhc,lthc->lhrt", query_c, keys_c, preferred_element_type=jnp.float32)
        * score_scale
    )
    probs = jnp.exp(scores_again - log_total)
    grad_probs = jnp.einsum(
        "lrhc,lthc->lhrt", grad_mixed, values_c, preferred_element_type=jnp.float32
    )
    grad_values_c = jnp.einsum(
        "lhrt,lrhc->lthc", to_low(probs), grad_mixed, preferred_element_type=jnp.float32
    )
    grad_scores = to_low(probs * (grad_probs - jnp.sum(probs * grad_probs, axis=-1, keepdims=True)))
    grad_query_c = to_low(
        jnp.einsum("lhrt,lthc->lrhc", grad_scores, keys_c, preferred_element_type=jnp.float32)
        * score_scale
    ).reshape(lat_dev, tokens_dev, D)
    grad_keys_c = (
        jnp.einsum("lhrt,lrhc->lthc", grad_scores, query_c, preferred_element_type=jnp.float32)
        * score_scale
    )
    grad_keyval_part = jnp.concatenate(
        [grad_keys_c.reshape(lat_dev, text_len, D), grad_values_c.reshape(lat_dev, text_len, D)],
        axis=-1,
    )
    grad_keyval_part = grad_keyval_part.reshape(lat_dev, text_len, segs, 2 * D // segs)
    grad_keyval = to_low(
        lax.psum_scatter(
            grad_keyval_part.astype(jnp.bfloat16), "seq", scatter_dimension=2, tiled=True
        ).astype(jnp.float32)
    ).reshape(lat_dev, text_len, 2 * D // segs)
    grad_w_cross_kv = outer_sum(text, grad_keyval)
    grad_first = grad_second + matmul_t(grad_query_c, w_cross_q)
    grad_gate_one = jnp.sum(grad_first * branch_one, axis=1)
    grad_branch_one = to_low(grad_first * gate_one)
    grad_branch_one, y_inner, y_point = lax.optimization_barrier(
        (grad_branch_one, *collect([grad_inner, grad_branch_two]))
    )
    grad_attended = matmul_t(grad_branch_one, w_attn_out).reshape(
        lat_dev, tokens_dev, heads_lin, 32
    )
    grad_numer = grad_attended / denominator[..., None]
    grad_denom = -jnp.sum(grad_attended * attn_val, axis=-1) / denominator
    grad_query = (
        jnp.einsum("lrhe,lhde->lrhd", grad_numer, kv_state, precision=precise)
        + grad_denom[..., None] * key_sum[:, None]
    )
    state_grad_part = jnp.einsum("lrhd,lrhe->lhde", query_f, grad_numer, precision=precise)
    sum_grad_part = jnp.einsum("lrhd,lrh->lhd", query_f, grad_denom, precision=precise)
    state_grad, sum_grad = state_sum(state_grad_part, sum_grad_part, jnp.bfloat16, 3)
    keys_f = keys_lin.astype(jnp.float32)
    values_f = values_lin.astype(jnp.float32)
    grad_keys = (
        jnp.einsum("lrhe,lhde->lrhd", values_f, state_grad, precision=precise) + sum_grad[:, None]
    )
    grad_values = jnp.einsum("lrhd,lhde->lrhe", keys_f, state_grad, precision=precise)
    grad_projected = to_low(
        jnp.concatenate(
            [
                grad_query.reshape(lat_dev, tokens_dev, D) * (query_pre > 0.0),
                grad_keys.reshape(lat_dev, tokens_dev, D) * (key_pre > 0.0),
                grad_values.reshape(lat_dev, tokens_dev, D),
            ],
            axis=-1,
        )
    )
    grad_projected, y_cross_out, y_cross_q, y_attn = lax.optimization_barrier(
        (grad_projected, *collect([grad_cross_out, grad_query_c, grad_branch_one]))
    )
    grad_hidden_one = matmul_t(grad_projected, w_qkv)
    grad_input = grad_first + norm_back(
        grad_hidden_one * (1.0 + scale_one), normed_one, inverse_one
    )
    grad_table = jnp.sum(
        jnp.stack(
            [
                jnp.sum(grad_hidden_one, axis=1),
                jnp.sum(grad_hidden_one * normed_one, axis=1),
                grad_gate_one,
                grad_shift_two,
                grad_scale_two,
                grad_gate_two,
            ],
            axis=1,
        ),
        axis=0,
    )
    grad_table = lax.optimization_barrier(grad_table)
    col_d = D // segs
    col_ff = 2 * FF // segs
    small_parts = jnp.concatenate(
        [
            grad_table.reshape(6, segs, col_d).transpose(1, 0, 2).reshape(segs, -1),
            grad_w_depth.reshape(9, segs, col_ff).transpose(1, 0, 2).reshape(segs, -1),
            grad_b_depth.reshape(segs, col_ff),
        ],
        axis=1,
    ).astype(jnp.bfloat16)
    small_parts = small_parts.reshape(segs, -1, LANE)
    small_mine = (
        lax.psum_scatter(small_parts, "seq", scatter_dimension=0, tiled=True)
        .astype(jnp.float32)
        .reshape(-1)
    )
    table_q = small_mine[: 6 * col_d].reshape(6, col_d)
    depth_q = small_mine[6 * col_d : 6 * col_d + 9 * col_ff].reshape(9, col_ff)
    depth_bias_q = small_mine[6 * col_d + 9 * col_ff :].reshape(1, col_ff)

    (y_qkv,) = collect([grad_projected])
    grad_w_qkv = outer_sum(x_qkv, y_qkv)
    grad_w_attn_out = outer_sum(x_attn, y_attn)
    grad_w_cross_q = outer_sum(x_cross_q, y_cross_q)
    grad_w_cross_out = outer_sum(x_cross_out, y_cross_out)
    grad_w_in = outer_sum(x_inner, y_inner)
    grad_w_point = outer_sum(x_point, y_point)
    grad_b_attn_out = jnp.sum(y_attn, axis=0, dtype=jnp.float32)
    grad_b_cross_out = jnp.sum(y_cross_out, axis=0, dtype=jnp.float32)
    grad_b_in = jnp.sum(y_inner, axis=0, dtype=jnp.float32)
    grad_b_point = jnp.sum(y_point, axis=0, dtype=jnp.float32)
    bias_part = jnp.concatenate(
        [grad_b_attn_out, grad_b_cross_out, grad_b_in, depth_bias_q.ravel(), grad_b_point]
    )
    len_bias = bias_part.size
    bias_rows = -(-bias_part.size // (8 * LANE)) * 8
    bias_part = jnp.pad(bias_part, (0, bias_rows * LANE - bias_part.size)).reshape(-1, LANE)
    quarter_grad = write_flat(
        segs,
        [
            table_q,
            grad_w_qkv,
            grad_w_attn_out,
            grad_b_attn_out,
            grad_w_cross_q,
            grad_w_cross_kv,
            grad_w_cross_out,
            grad_b_cross_out,
            grad_w_in,
            grad_b_in,
            depth_q,
            depth_bias_q,
            grad_w_point,
            grad_b_point,
        ],
    )
    if count_dp == 8 and quarter_grad.shape[0] % (8 * 240) == 0:
        grad_shard = reduce_shard(quarter_grad)
    else:
        grad_shard = lax.psum_scatter(
            quarter_grad.reshape(count_dp, -1, LANE), "dp", scatter_dimension=0, tiled=True
        )
        grad_shard = grad_shard.reshape(-1, LANE).astype(jnp.float32)
    factor, bias_grads = scale_of(grad_shard, bias_part)
    flat_outs = adam(
        factor,
        grad_shard,
        params_rows,
        moment_one.reshape(-1, LANE),
        moment_two.reshape(-1, LANE),
    )
    gradient, moment_one_new, moment_two_new, update = [
        value.reshape(params.shape) for value in flat_outs
    ]
    return (
        output,
        grad_input.reshape(latents.shape),
        gradient,
        moment_one_new,
        moment_two_new,
        update,
        bias_grads.reshape(1, -1)[:, :len_bias],
    )


def solution(mesh):
    return jax.shard_map(
        shards,
        mesh=mesh,
        in_specs=(
            P("dp", "seq", None, None),
            P("dp", None, None),
            P("dp", None),
            P("dp", "seq", None, None),
            P("seq", "dp"),
            P("seq", "dp"),
            P("seq", "dp"),
        ),
        out_specs=(
            P("dp", "seq", None, None),
            P("dp", "seq", None, None),
            P("seq", "dp"),
            P("seq", "dp"),
            P("seq", "dp"),
            P("seq", "dp"),
            P("seq", None),
        ),
        check_vma=False,
    )
```

```python
import math

import jax
import jax.numpy as jnp
from jax import lax
from jax.experimental import pallas as pl
from jax.experimental.pallas import tpu as pltpu
from jax.sharding import PartitionSpec as P

D = 1152
FF = 2880
CROSS_HEADS = 16


precise = lax.Precision.HIGHEST
eps_norm = 1e-06
eps_linear = 1e-06
beta_first = 0.9
beta_second = 0.95
adam_eps = 1e-08
weight_decay = 0.01
adam_steps = 100.0


def with_halo(block, sides, width):
    for axis, dim in sides:
        count = lax.axis_size(axis)
        forward = [(i, i + 1) for i in range(count - 1)]
        backward = [(target, source) for source, target in forward]
        low = lax.ppermute(
            lax.slice_in_dim(block, block.shape[dim] - width, None, axis=dim), axis, forward
        )
        high = lax.ppermute(lax.slice_in_dim(block, 0, width, axis=dim), axis, backward)
        block = jnp.concatenate([low, block, high], axis=dim)
    return block


def piece_specs():
    return [
        (6, D, False),
        (D, 3 * D, False),
        (D, D, False),
        (1, D, True),
        (D, D, False),
        (D, 2 * D, False),
        (D, D, False),
        (1, D, True),
        (D, 2 * FF, False),
        (1, 2 * FF, True),
        (9, 2 * FF, False),
        (1, 2 * FF, True),
        (FF, D, False),
        (1, D, True),
    ]


LANE = 128
UNIT = 32
MESH = pl.DeviceIdType.MESH


def merge_units(values, lane_unit):
    out = values[0]
    last = values[0]
    for position in range(1, 4):
        if values[position] is not last:
            out = jnp.where(lane_unit >= position, values[position], out)
            last = values[position]
    return out


def rolled(value, units):
    units = units % 4
    return value if units == 0 else pltpu.roll(value, units * UNIT, 1)


def matrix_rows(count_rows):
    return 384 if count_rows % 384 == 0 else 576 if count_rows % 576 == 0 else 64


def read_matrix(flat, offset, rows_of, cols_of, segs):
    total_rows = flat.shape[1]
    per_row = cols_of // segs // UNIT
    unit_at = offset // UNIT
    block = matrix_rows(rows_of)
    base = unit_at // 4 // 16 * 16
    shift = unit_at - 4 * base
    step = block * per_row // 4
    need = (shift + block * per_row - 1) // 4 + 1
    need = -(-need // 16) * 16
    assert base + (rows_of // block - 1) * step + need <= total_rows
    tiles = cols_of // LANE

    def kernel(in_ref, out_ref, wide, mixed):
        def widen(at, _):
            row = pl.multiple_of(at * 16, 16)
            for seg in range(segs):
                wide[pl.ds(pl.multiple_of(seg * need + row, 16), 16), :] = in_ref[
                    seg, pl.ds(row, 16), :
                ].astype(jnp.float32)
            return 0

        lax.fori_loop(0, need // 16, widen, 0, unroll=8)
        lane_unit = lax.broadcasted_iota(jnp.int32, (8, LANE), 1) // UNIT

        def group(at, _):
            for phase in range(4):
                loaded = {}
                turned = {}
                for tile in range(tiles):
                    parts = []
                    for slot in range(4):
                        col = 4 * tile + slot
                        seg, unit = col // per_row, col % per_row
                        source = shift + phase * per_row + unit
                        key = (seg, source // 4)
                        if key not in loaded:
                            loaded[key] = wide[
                                pl.ds(seg * need + key[1] + at * (8 * per_row), 8, stride=per_row),
                                :,
                            ]
                        turn = (slot - source) % 4
                        if (key, turn) not in turned:
                            turned[key, turn] = rolled(loaded[key], turn)
                        parts.append(turned[key, turn])
                    mixed[pl.ds(tile * block + phase + at * 32, 8, stride=4), :] = merge_units(
                        parts, lane_unit
                    )
            return 0

        lax.fori_loop(0, block // 32, group, 0, unroll=2)

        def narrow(at, _):
            row = pl.multiple_of(at * 16, 16)
            for tile in range(tiles):
                out_ref[pl.ds(row, 16), tile * LANE : (tile + 1) * LANE] = mixed[
                    pl.ds(pl.multiple_of(tile * block + row, 16), 16), :
                ].astype(jnp.bfloat16)
            return 0

        lax.fori_loop(0, block // 16, narrow, 0, unroll=2)

    return pl.pallas_call(
        kernel,
        grid=(rows_of // block,),
        in_specs=[
            pl.BlockSpec(
                (pl.Element(segs), pl.Element(need), pl.Element(LANE)),
                lambda at: (0, pl.multiple_of(base + at * step, 16), 0),
            )
        ],
        out_specs=pl.BlockSpec((block, cols_of), lambda at: (at, 0)),
        out_shape=jax.ShapeDtypeStruct((rows_of, cols_of), jnp.bfloat16),
        scratch_shapes=[
            pltpu.VMEM((segs * need, LANE), jnp.float32),
            pltpu.VMEM((tiles * block, LANE), jnp.float32),
        ],
        compiler_params=pltpu.CompilerParams(vmem_limit_bytes=48 << 20),
        cost_estimate=pl.CostEstimate(
            flops=0, bytes_accessed=4 * rows_of * cols_of, transcendentals=0
        ),
        name="read_matrix",
    )(flat)


def write_flat(segs, parts):
    specs = piece_specs()
    block_rows = 576
    total = sum(rows_of * cols_of // segs for rows_of, cols_of, _ in specs)
    flat_rows = total // LANE
    places = []
    offset = 0
    big, small = [], []
    for (rows_of, cols_of, _), value in zip(specs, parts):
        width = cols_of // segs
        length = rows_of * width
        if rows_of > 9:
            assert rows_of % block_rows == 0
            places.append((True, offset, rows_of, width, len(big)))
            big.append(value)
        else:
            lead = offset % LANE
            rest = -(lead + length) % LANE
            padded = jnp.pad(value.reshape(-1), (lead, rest)).reshape(-1, LANE)
            places.append((False, offset, length, None, len(small)))
            small.append(padded)
        offset += length
    widths = sorted({place[3] for place in places if place[0]})
    chunk = 144

    def kernel(*refs):
        big_refs = refs[: len(big)]
        small_refs = refs[len(big) : len(big) + len(small)]
        out_ref = refs[len(big) + len(small)]
        flat = refs[len(big) + len(small) + 1]
        bufs = refs[len(big) + len(small) + 2 : len(big) + len(small) + 2 + len(widths)]
        in_sem = refs[-1]
        lane_unit = lax.broadcasted_iota(jnp.int32, (8, LANE), 1) // UNIT
        row_unit = lax.broadcasted_iota(jnp.int32, (1, LANE), 1) // UNIT

        def place_small(ref, offset, length):
            first = offset // LANE
            last = (offset + length - 1) // LANE
            lead = offset % LANE // UNIT
            tail = (offset + length) % LANE // UNIT
            count = last - first + 1
            if count > 2:

                def copy_row(at, _):
                    flat[pl.ds(first + 1 + at, 1), :] = ref[pl.ds(1 + at, 1), :]
                    return 0

                lax.fori_loop(0, count - 2, copy_row, 0)
            keep = row_unit >= lead
            if count == 1 and tail:
                keep = keep & (row_unit < tail)
            flat[first : first + 1, :] = jnp.where(keep, ref[0:1, :], flat[first : first + 1, :])
            if count > 1:
                flat[last : last + 1, :] = (
                    jnp.where(
                        row_unit < tail, ref[count - 1 : count, :], flat[last : last + 1, :]
                    )
                    if tail
                    else ref[count - 1 : count, :]
                )

        def fetch_block(ref, buf, width, at, slot):
            row = pl.multiple_of(at * block_rows, 64)
            return [
                pltpu.make_async_copy(
                    ref.at[pl.ds(row, block_rows), tile * LANE : (tile + 1) * LANE],
                    buf.at[slot, tile],
                    in_sem.at[widths.index(width), slot, tile],
                )
                for tile in range(-(-width // LANE))
            ]

        def place_big(ref, buf, offset, rows_of, width):
            per_row = width // UNIT
            first = offset // LANE
            shift = offset % LANE // UNIT
            block = block_rows
            blocks = rows_of // block

            def fetch(at, slot):
                return fetch_block(ref, buf, width, at, slot)

            def one_block(at, _):
                slot = lax.rem(at, 2)

                @pl.when(at + 1 < blocks)
                def _():
                    for copy in fetch(at + 1, 1 - slot):
                        copy.start()

                for copy in fetch(at, slot):
                    copy.wait()

                def group(sub, _):
                    loaded = {}
                    turned = {}

                    def unit_value(phase, unit, lane):
                        key = (phase, unit // 4)
                        if key not in loaded:
                            loaded[key] = buf[
                                slot, key[1], pl.ds(phase + sub * 32, 8, stride=4), :
                            ]
                        turn = (lane - unit) % 4
                        if (key, turn) not in turned:
                            turned[key, turn] = rolled(loaded[key], turn)
                        return turned[key, turn]

                    start = first + (at * (block // 4) + sub * 8) * per_row
                    for row in range(per_row + (1 if shift else 0)):
                        where = pl.ds(start + row, 8, stride=per_row)
                        parts = []
                        kept = None
                        for lane in range(4):
                            unit = 4 * row + lane - shift
                            if unit < 0 or unit >= 4 * per_row:
                                if kept is None:
                                    kept = flat[where, :]
                                parts.append(kept)
                            else:
                                parts.append(unit_value(unit // per_row, unit % per_row, lane))
                        flat[where, :] = merge_units(parts, lane_unit)
                    return 0

                lax.fori_loop(0, block // 32, group, 0, unroll=6)
                return 0

            lax.fori_loop(0, blocks, one_block, 0)

        def first_fetch(width, after):
            for is_big, _, _, other, index in places:
                if is_big and other == width and index > after:
                    buf = bufs[widths.index(width)]
                    for copy in fetch_block(big_refs[index], buf, width, 0, 0):
                        copy.start()
                    return

        for width in widths:
            first_fetch(width, -1)
        for is_big, offset, rows_of, width, index in places:
            if is_big:
                place_big(big_refs[index], bufs[widths.index(width)], offset, rows_of, width)
                first_fetch(width, index)
            else:
                place_small(small_refs[index], offset, rows_of)

        def narrow(at, _):
            where = pl.ds(pl.multiple_of(at * chunk, 16), chunk)
            out_ref[where, :] = flat[where, :].astype(jnp.bfloat16)
            return 0

        lax.fori_loop(0, flat_rows // chunk, narrow, 0)

    return pl.pallas_call(
        kernel,
        in_specs=[pl.BlockSpec(memory_space=pl.ANY)] * len(big)
        + [pl.BlockSpec(memory_space=pltpu.VMEM)] * len(small),
        out_specs=pl.BlockSpec(memory_space=pltpu.VMEM),
        out_shape=jax.ShapeDtypeStruct((flat_rows, LANE), jnp.bfloat16),
        scratch_shapes=[pltpu.VMEM((flat_rows, LANE), jnp.float32)]
        + [
            pltpu.VMEM((2, -(-width // LANE), block_rows, LANE), jnp.float32) for width in widths
        ]
        + [
            pltpu.SemaphoreType.DMA((len(widths), 2, -(-widths[-1] // LANE))),
        ],
        compiler_params=pltpu.CompilerParams(vmem_limit_bytes=56 << 20),
        cost_estimate=pl.CostEstimate(flops=0, bytes_accessed=6 * total, transcendentals=0),
        name="write_flat",
    )(*big, *small)


def gather_flat(shard):
    rows = shard.shape[0]
    first = (rows // 2 + 15) // 16 * 16
    parts = ((0, first), (first, rows - first))

    def kernel(
        in_ref,
        out_ref,
        own_sem,
        z_send,
        z_recv,
        x_send,
        x_recv,
        y_send,
        y_recv,
        d_send,
        d_recv,
        c_send,
        c_recv,
    ):
        dp = lax.axis_index("dp")
        seq = lax.axis_index("seq")
        near, far = lax.rem(dp, 2), lax.div(dp, 2)
        core, side = lax.rem(seq, 2), lax.div(seq, 2)

        half = lax.div(far, 2)
        place = far + half * (3 - 2 * far)
        inner = far + 1 - 2 * half
        outer = far - 1 + 2 * half

        def dp_of(turn, flip):
            at = place if turn == 0 else 1 - place if turn == 1 else turn
            return 2 * (at + half * (3 - 2 * at)) + (1 - near if flip else near)

        def seq_of(flip, other_core):
            return 2 * (1 - side if flip else side) + (1 - core if other_core else core)

        def region(seq_at, dp_at, part):
            start, length = parts[part]
            return out_ref.at[
                seq_at, pl.ds(pl.multiple_of(dp_at * rows + start, 16), length), :
            ]

        def own_region(part):
            start, length = parts[part]
            return in_ref.at[pl.ds(start, length), :]

        def column(turn, part):
            return region(seq, dp_of(turn, False), part)

        def source(turn, part):
            return column(turn, part) if turn else own_region(part)

        def remote(src, dst, send, recv, target):
            return pltpu.make_async_remote_copy(
                src_ref=src,
                dst_ref=dst,
                send_sem=send,
                recv_sem=recv,
                device_id=target,
                device_id_type=MESH,
            )

        x_peer = {"dp": dp_of(0, True)}
        y_peer = {"seq": seq_of(True, False)}
        c_peer = {"seq": seq_of(False, True)}

        def z_copy(kind, part):
            turn = (0, 0, 1, 2, 3)[kind]
            arrives = (place, 0, 2, 1, 2)[kind]
            return remote(
                source(turn, part),
                column(turn, part),
                z_send.at[kind, part],
                z_recv.at[arrives, part],
                {"dp": 2 * (inner if kind in (0, 2) else outer) + near},
            )

        def z_in(turn, part):
            here = column(turn, part)
            return remote(
                here, here, z_send.at[0, part], z_recv.at[turn - 1, part], {"dp": 2 * inner + near}
            )

        def x_out(turn, part):
            return remote(
                source(turn, part),
                column(turn, part),
                x_send.at[turn, part],
                x_recv.at[turn, part],
                x_peer,
            )

        def x_in(turn, part):
            here = region(seq, dp_of(turn, True), part)
            return remote(here, here, x_send.at[turn, part], x_recv.at[turn, part], x_peer)

        def y_out(turn, part):
            return remote(
                source(turn, part),
                column(turn, part),
                y_send.at[turn, part],
                y_recv.at[turn, part],
                y_peer,
            )

        def y_in(turn, part):
            here = region(seq_of(True, False), dp_of(turn, False), part)
            return remote(here, here, y_send.at[turn, part], y_recv.at[turn, part], y_peer)

        def d_out(turn, part):
            if part == 0:
                here, target = region(seq, dp_of(turn, True), part), y_peer
            else:
                here, target = region(seq_of(True, False), dp_of(turn, False), part), x_peer
            return remote(here, here, d_send.at[turn, part], d_recv.at[turn, part], target)

        def d_in(turn, part):
            here = region(seq_of(True, False), dp_of(turn, True), part)
            target = y_peer if part == 0 else x_peer
            return remote(here, here, d_send.at[turn, part], d_recv.at[turn, part], target)

        def c_copy(kind, turn, part, incoming):
            where = region(
                seq_of(kind in (2, 3), incoming), dp_of(turn, kind in (1, 3)), part
            )
            src = own_region(part) if kind == 0 and turn == 0 else where
            return remote(
                src if not incoming else where,
                where,
                c_send.at[kind, turn, part],
                c_recv.at[kind, turn, part],
                c_peer,
            )

        barrier = pltpu.get_barrier_semaphore()
        for target in (x_peer, y_peer, c_peer, {"dp": 2 * inner + near}):
            pl.semaphore_signal(barrier, inc=1, device_id=target, device_id_type=MESH)

        @pl.when(place == 1)
        def _():
            pl.semaphore_signal(
                barrier, inc=1, device_id={"dp": 2 * outer + near}, device_id_type=MESH
            )
            pl.semaphore_wait(barrier, 5)

        @pl.when(place == 0)
        def _():
            pl.semaphore_wait(barrier, 4)

        keep = [
            pltpu.make_async_copy(own_region(part), region(seq, dp, part), own_sem.at[part])
            for part in range(2)
        ]
        def outwards(kind, part):
            @pl.when(place == 1)
            def _():
                z_copy(kind, part).start()

        for part in range(2):
            z_copy(0, part).start()
            outwards(1, part)
            x_out(0, part).start()
            y_out(0, part).start()
        for part in range(2):
            keep[part].start()
            c_copy(0, 0, part, False).start()

        def sideways(turn):
            for part in range(2):
                x_in(turn, part).wait_recv()
                if part == 0:
                    d_out(turn, part).start()
                c_copy(1, turn, part, False).start()
                y_in(turn, part).wait_recv()
                if part == 1:
                    d_out(turn, part).start()
                c_copy(2, turn, part, False).start()

        def diagonal(turn):
            for part in range(2):
                d_in(turn, part).wait_recv()
                c_copy(3, turn, part, False).start()

        for turn in range(1, 4):
            for part in range(2):
                z_in(turn, part).wait_recv()
                outwards(turn + 1, part)
                x_out(turn, part).start()
                y_out(turn, part).start()
                c_copy(0, turn, part, False).start()
            sideways(turn - 1)
            if turn > 1:
                diagonal(turn - 2)
        sideways(3)
        diagonal(2)
        diagonal(3)

        @pl.when(place == 1)
        def _():
            for kind in range(1, 5):
                for part in range(2):
                    z_copy(kind, part).wait_send()

        for part in range(2):
            keep[part].wait()
            z_copy(0, part).wait_send()
            for turn in range(4):
                x_out(turn, part).wait_send()
                y_out(turn, part).wait_send()
                d_out(turn, part).wait_send()
                for kind in range(4):
                    c_copy(kind, turn, part, False).wait_send()
                    c_copy(kind, turn, part, True).wait_recv()

    return pl.pallas_call(
        kernel,
        in_specs=[pl.BlockSpec(memory_space=pltpu.VMEM)],
        out_specs=pl.BlockSpec(memory_space=pl.ANY),
        out_shape=jax.ShapeDtypeStruct((4, 8 * rows, LANE), jnp.bfloat16),
        scratch_shapes=[
            pltpu.SemaphoreType.DMA((2,)),
            pltpu.SemaphoreType.DMA((5, 2)),
            pltpu.SemaphoreType.DMA((3, 2)),
        ]
        + [pltpu.SemaphoreType.DMA((4, 2))] * 6
        + [pltpu.SemaphoreType.DMA((4, 4, 2))] * 2,
        compiler_params=pltpu.CompilerParams(collective_id=5, has_side_effects=True),
        name="gather_flat",
    )(shard)


def round_rows(values):
    def kernel(in_ref, out_ref):
        out_ref[...] = in_ref[...].astype(jnp.bfloat16)

    return pl.pallas_call(
        kernel,
        in_specs=[pl.BlockSpec(memory_space=pltpu.VMEM)],
        out_specs=pl.BlockSpec(memory_space=pltpu.VMEM),
        out_shape=jax.ShapeDtypeStruct(values.shape, jnp.bfloat16),
        name="round_rows",
    )(values)


def gather_weights(shard_low, segs):
    if segs == 4 and lax.axis_size("dp") == 8 and shard_low.shape[0] % 16 == 0:
        flat = gather_flat(shard_low)
    else:
        whole = lax.all_gather(shard_low, ("seq", "dp"), axis=0, tiled=True)
        flat = whole.reshape(segs, -1, LANE)
    pieces = []
    offset = 0
    for rows_of, cols_of, vector in piece_specs():
        length = rows_of * cols_of // segs
        if rows_of > 9:
            pieces.append(read_matrix(flat, offset, rows_of, cols_of, segs))
        else:
            first, last = offset // LANE, -(-(offset + length) // LANE)
            lead = offset - first * LANE
            block = flat[:, first:last].reshape(segs, -1)[:, lead : lead + length]
            block = block.reshape(segs, rows_of, cols_of // segs).transpose(1, 0, 2)
            pieces.append(block.reshape(cols_of) if vector else block.reshape(rows_of, cols_of))
        offset = offset + length
    return pieces


def peer_barrier(groups):
    barrier = pltpu.get_barrier_semaphore()
    total = 0
    for axis, count in groups:
        me = lax.axis_index(axis)
        for step in range(1, count):
            pl.semaphore_signal(
                barrier, inc=1, device_id={axis: lax.rem(me + step, count)}, device_id_type=MESH
            )
        total += count - 1
    pl.semaphore_wait(barrier, total)


def exchange(axis, count, source, slots, send_sem, recv_sem):
    me = lax.axis_index(axis)
    for step in range(1, count):
        pltpu.make_async_remote_copy(
            src_ref=source,
            dst_ref=slots.at[me],
            send_sem=send_sem.at[step - 1],
            recv_sem=recv_sem.at[me],
            device_id={axis: lax.rem(me + step, count)},
            device_id_type=MESH,
        ).start()


def exchange_wait(axis, count, source, slots, send_sem, recv_sem):
    me = lax.axis_index(axis)
    for step in range(1, count):
        peer = lax.rem(me + step, count)
        copy = pltpu.make_async_remote_copy(
            src_ref=source,
            dst_ref=slots.at[peer],
            send_sem=send_sem.at[step - 1],
            recv_sem=recv_sem.at[peer],
            device_id={axis: peer},
            device_id_type=MESH,
        )
        copy.wait_send()
        copy.wait_recv()


def in_order(axis, count, own, slots):
    me = lax.axis_index(axis)
    total = None
    for index in range(count):
        term = jnp.where(me == index, own, slots[index].astype(jnp.float32))
        total = term if total is None else total + term
    return total


def seq_sum(block, collective_id):
    count = lax.axis_size("seq")

    def kernel(in_ref, out_ref, slots, send_sem, recv_sem):
        peer_barrier([("seq", count)])
        exchange("seq", count, in_ref, slots, send_sem, recv_sem)
        exchange_wait("seq", count, in_ref, slots, send_sem, recv_sem)
        out_ref[...] = in_order("seq", count, in_ref[...].astype(jnp.float32), slots)

    return pl.pallas_call(
        kernel,
        in_specs=[pl.BlockSpec(memory_space=pltpu.VMEM)],
        out_specs=pl.BlockSpec(memory_space=pltpu.VMEM),
        out_shape=jax.ShapeDtypeStruct(block.shape, jnp.float32),
        scratch_shapes=[
            pltpu.VMEM((count,) + block.shape, block.dtype),
            pltpu.SemaphoreType.DMA((count - 1,)),
            pltpu.SemaphoreType.DMA((count,)),
        ],
        compiler_params=pltpu.CompilerParams(collective_id=collective_id, has_side_effects=True),
        name="seq_sum",
    )(block)


def state_sum(state, sums, kind, collective_id):
    heads = state.shape[1]
    flat = jnp.concatenate(
        [state.reshape(-1, LANE), jnp.pad(sums.reshape(-1), (0, -sums.size % LANE)).reshape(-1, LANE)]
    ).astype(kind)
    rows = flat.shape[0]
    flat = jnp.pad(flat, ((0, -rows % 16), (0, 0)))
    total = seq_sum(flat, collective_id)
    split = state.size // LANE
    return (
        total[:split].reshape(state.shape),
        total[split:].reshape(-1)[: sums.size].reshape(1, heads, -1),
    )


def reduce_shard(flat):
    rows = flat.shape[0] // 8
    pieces = 3
    part = rows // pieces
    step = 80

    def kernel(in_ref, out_ref, recv_x, send_z, recv_z, x_send, x_recv, z_send, z_recv):
        me = lax.axis_index("dp")
        near = lax.rem(me, 2)
        far = lax.div(me, 2)
        partner = me + 1 - 2 * near

        def far_of(shift):
            return lax.rem(far + shift, 4)

        barrier = pltpu.get_barrier_semaphore()
        pl.semaphore_signal(barrier, inc=1, device_id={"dp": partner}, device_id_type=MESH)
        for shift in range(1, 4):
            pl.semaphore_signal(
                barrier,
                inc=1,
                device_id={"dp": 2 * far_of(shift) + near},
                device_id_type=MESH,
            )
        pl.semaphore_wait(barrier, 4)

        def window(shard, piece):
            return pl.ds(pl.multiple_of(shard * rows + piece * part, 16), part)

        def x_copy(shift, piece):
            return pltpu.make_async_remote_copy(
                src_ref=in_ref.at[window(2 * far_of(shift) + 1 - near, piece), :],
                dst_ref=recv_x.at[shift, pl.ds(piece * part, part), :],
                send_sem=x_send.at[shift, piece],
                recv_sem=x_recv.at[shift, piece],
                device_id={"dp": partner},
                device_id_type=MESH,
            )

        def z_copy(shift, piece):
            return pltpu.make_async_remote_copy(
                src_ref=send_z.at[shift - 1, pl.ds(piece * part, part), :],
                dst_ref=recv_z.at[shift - 1, pl.ds(piece * part, part), :],
                send_sem=z_send.at[shift - 1, piece],
                recv_sem=z_recv.at[shift - 1, piece],
                device_id={"dp": 2 * far_of(shift) + near},
                device_id_type=MESH,
            )

        order = (1, 2, 3, 0)
        for shift in order:
            for piece in range(pieces):
                x_copy(shift, piece).start()

        def own_sum(shift, row, at):
            start = (2 * far_of(shift) + near) * rows + row + at * step
            own = in_ref[pl.ds(pl.multiple_of(start, 16), step), :]
            other = recv_x[shift, pl.ds(pl.multiple_of(row + at * step, 16), step), :]
            return own.astype(jnp.float32) + other.astype(jnp.float32)

        for shift in order:
            for piece in range(pieces):
                x_copy(shift, piece).wait_recv()
                row = piece * part

                def add(at, _, shift=shift, row=row):
                    where = pl.ds(pl.multiple_of(row + at * step, 16), step)
                    total = own_sum(shift, row, at)
                    if shift:
                        send_z[shift - 1, where, :] = total.astype(jnp.bfloat16)
                    else:
                        out_ref[where, :] = total
                    return 0

                lax.fori_loop(0, part // step, add, 0)
                if shift:
                    z_copy(shift, piece).start()
        for shift in range(1, 4):
            for piece in range(pieces):
                z_copy(shift, piece).wait_recv()
                row = piece * part

                def gather(at, _, shift=shift, row=row):
                    where = pl.ds(pl.multiple_of(row + at * step, 16), step)
                    out_ref[where, :] = out_ref[where, :] + recv_z[shift - 1, where, :].astype(
                        jnp.float32
                    )
                    return 0

                lax.fori_loop(0, part // step, gather, 0)
        for shift in range(4):
            for piece in range(pieces):
                x_copy(shift, piece).wait_send()
                if shift:
                    z_copy(shift, piece).wait_send()

    block = (rows, LANE)
    return pl.pallas_call(
        kernel,
        in_specs=[pl.BlockSpec(memory_space=pltpu.VMEM)],
        out_specs=pl.BlockSpec(memory_space=pltpu.VMEM),
        out_shape=jax.ShapeDtypeStruct(block, jnp.float32),
        scratch_shapes=[
            pltpu.VMEM((4,) + block, jnp.bfloat16),
            pltpu.VMEM((3,) + block, jnp.bfloat16),
            pltpu.VMEM((3,) + block, jnp.bfloat16),
            pltpu.SemaphoreType.DMA((4, pieces)),
            pltpu.SemaphoreType.DMA((4, pieces)),
            pltpu.SemaphoreType.DMA((3, pieces)),
            pltpu.SemaphoreType.DMA((3, pieces)),
        ],
        compiler_params=pltpu.CompilerParams(
            collective_id=4, has_side_effects=True, vmem_limit_bytes=40 << 20
        ),
        name="reduce_shard",
    )(flat)


def scale_of(grad_shard, bias_part):
    rows = grad_shard.shape[0]
    count_dp = lax.axis_size("dp")
    count_seq = lax.axis_size("seq")
    entries = rows * LANE * count_dp * count_seq
    chunk = 48 if rows % 48 == 0 else rows
    bias_rows = bias_part.shape[0]

    def kernel(
        grad_ref,
        bias_ref,
        factor_out,
        bias_out,
        square,
        square_dp,
        square_seq,
        partial,
        bias_slots,
        send_bias,
        recv_bias,
        send_dp,
        recv_dp,
        send_seq,
        recv_seq,
    ):
        peer_barrier([("dp", count_dp), ("seq", count_seq)])
        exchange("dp", count_dp, bias_ref, bias_slots, send_bias, recv_bias)

        def squares(at, total):
            part = grad_ref[pl.ds(at * chunk, chunk), :].astype(jnp.float32)
            return total + jnp.sum(part * part, axis=0, keepdims=True)

        total = lax.fori_loop(0, rows // chunk, squares, jnp.zeros((1, LANE), jnp.float32))
        square[...] = jnp.broadcast_to(total, (8, LANE))
        exchange("dp", count_dp, square, square_dp, send_dp, recv_dp)
        exchange_wait("dp", count_dp, square, square_dp, send_dp, recv_dp)
        partial[...] = in_order("dp", count_dp, square[...], square_dp)
        exchange("seq", count_seq, partial, square_seq, send_seq, recv_seq)
        exchange_wait("seq", count_seq, partial, square_seq, send_seq, recv_seq)
        whole = jnp.sum(
            in_order("seq", count_seq, partial[...], square_seq)[0:1], axis=1, keepdims=True
        )
        factor = lax.rsqrt(whole / entries + 1e-06)
        exchange_wait("dp", count_dp, bias_ref, bias_slots, send_bias, recv_bias)
        bias_out[...] = in_order("dp", count_dp, bias_ref[...], bias_slots) * factor
        factor_out[...] = jnp.broadcast_to(factor, (8, LANE))

    tile = (8, LANE)
    return pl.pallas_call(
        kernel,
        in_specs=[pl.BlockSpec(memory_space=pltpu.VMEM)] * 2,
        out_specs=[pl.BlockSpec(memory_space=pltpu.VMEM)] * 2,
        out_shape=[
            jax.ShapeDtypeStruct(tile, jnp.float32),
            jax.ShapeDtypeStruct((bias_rows, LANE), jnp.float32),
        ],
        scratch_shapes=[
            pltpu.VMEM(tile, jnp.float32),
            pltpu.VMEM((count_dp,) + tile, jnp.float32),
            pltpu.VMEM((count_seq,) + tile, jnp.float32),
            pltpu.VMEM(tile, jnp.float32),
            pltpu.VMEM((count_dp, bias_rows, LANE), jnp.float32),
            pltpu.SemaphoreType.DMA((count_dp - 1,)),
            pltpu.SemaphoreType.DMA((count_dp,)),
            pltpu.SemaphoreType.DMA((count_dp - 1,)),
            pltpu.SemaphoreType.DMA((count_dp,)),
            pltpu.SemaphoreType.DMA((count_seq - 1,)),
            pltpu.SemaphoreType.DMA((count_seq,)),
        ],
        compiler_params=pltpu.CompilerParams(
            collective_id=1, has_side_effects=True, vmem_limit_bytes=16 << 20
        ),
        name="scale_of",
    )(grad_shard, bias_part)


def adam(factor, grad_shard, params, moment_one, moment_two):
    rows = grad_shard.shape[0]
    block = 504 if rows % 504 == 0 else rows

    def kernel(
        factor_ref, grad_ref, param_ref, one_ref, two_ref, gradient_ref, one_out, two_out, update_ref
    ):
        gradient = grad_ref[...] * factor_ref[0:1, :]
        first = beta_first * one_ref[...] + (1.0 - beta_first) * gradient
        second = beta_second * two_ref[...] + (1.0 - beta_second) * gradient * gradient
        gradient_ref[...] = gradient
        one_out[...] = first
        two_out[...] = second
        first_hat = first / (1.0 - beta_first**adam_steps)
        second_hat = second / (1.0 - beta_second**adam_steps)
        update_ref[...] = (
            first_hat / (jnp.sqrt(second_hat) + adam_eps) + weight_decay * param_ref[...]
        )

    spec = pl.BlockSpec((block, LANE), lambda at: (at, 0))
    return pl.pallas_call(
        kernel,
        grid=(rows // block,),
        in_specs=[pl.BlockSpec((8, LANE), lambda at: (0, 0))] + [spec] * 4,
        out_specs=[spec] * 4,
        out_shape=[jax.ShapeDtypeStruct((rows, LANE), jnp.float32)] * 4,
        name="adam",
    )(factor, grad_shard, params, moment_one, moment_two)


def norm_parts(values):
    centred = values - jnp.mean(values, axis=-1, keepdims=True)
    inverse = lax.rsqrt(jnp.mean(centred * centred, axis=-1, keepdims=True) + eps_norm)
    return (centred * inverse, inverse)


def norm_back(grad_normed, normed, inverse):
    return inverse * (
        grad_normed
        - jnp.mean(grad_normed, axis=-1, keepdims=True)
        - normed * jnp.mean(grad_normed * normed, axis=-1, keepdims=True)
    )


def silu_slope(values):
    sigmoid_v = jax.nn.sigmoid(values)
    return sigmoid_v * (1.0 + values * (1.0 - sigmoid_v))


def to_low(values):
    return values.astype(jnp.bfloat16)


def matmul(left_op, right_op):
    return jnp.dot(left_op, right_op, preferred_element_type=jnp.float32)


def matmul_t(left_op, right_op):
    return lax.dot_general(
        left_op,
        right_op,
        (((left_op.ndim - 1,), (1,)), ((), ())),
        preferred_element_type=jnp.float32,
    )


def outer_sum(left_op, right_op):
    left_flat = left_op.reshape(-1, left_op.shape[-1])
    right_flat = right_op.reshape(-1, right_op.shape[-1])
    right_flat = jnp.pad(right_flat, ((0, 0), (0, -right_flat.shape[1] % LANE)))
    return lax.dot_general(
        left_flat, right_flat, (((0,), (0,)), ((), ())), preferred_element_type=jnp.float32
    )


def depth_conv(padded, kernel, row_dev, col_dev, flipped):
    kernel_f = kernel.astype(jnp.float32)
    summed = jnp.zeros(padded.shape[:1] + (row_dev, col_dev) + padded.shape[3:], jnp.float32)
    for tap_row in range(3):
        for tap_col in range(3):
            row_at = 2 - tap_row if flipped else tap_row
            col_at = 2 - tap_col if flipped else tap_col
            summed = (
                summed
                + kernel_f[tap_row * 3 + tap_col]
                * padded[:, row_at : row_at + row_dev, col_at : col_at + col_dev, :]
            )
    return summed


def shards(latents, text, time_embed, cotangent, params, moment_one, moment_two):
    lat_dev, row_dev, col_dev, width = latents.shape
    tokens_dev = row_dev * col_dev
    heads_lin = D // 32
    cross_dim = D // CROSS_HEADS
    score_scale = 1.0 / math.sqrt(cross_dim)
    text_len = text.shape[1]
    segs = lax.axis_size("seq")
    count_dp = lax.axis_size("dp")
    def spread(values):
        joined = jnp.concatenate(values, axis=-1).reshape(-1, sum(v.shape[-1] for v in values))
        whole = lax.all_gather(joined, "seq", axis=0, tiled=True)
        parts = []
        at = 0
        for value in values:
            parts.append(whole[:, at : at + value.shape[-1]])
            at += value.shape[-1]
        return parts

    def collect(values):
        blocks = jnp.stack(
            [
                jnp.concatenate(
                    [
                        value.reshape(-1, value.shape[-1])[
                            :, seg * (value.shape[-1] // segs) : (seg + 1) * (value.shape[-1] // segs)
                        ]
                        for value in values
                    ],
                    axis=1,
                )
                for seg in range(segs)
            ]
        )
        mine = lax.all_to_all(blocks, "seq", split_axis=0, concat_axis=0, tiled=True)
        mine = mine.reshape(-1, mine.shape[-1])
        parts = []
        at = 0
        for value in values:
            width = value.shape[-1] // segs
            parts.append(mine[:, at : at + width])
            at += width
        return parts

    params_rows = params.reshape(-1, LANE)
    shard_low = round_rows(params_rows)
    (
        mod_table,
        w_qkv,
        w_attn_out,
        b_attn_out,
        w_cross_q,
        w_cross_kv,
        w_cross_out,
        b_cross_out,
        w_in,
        b_in,
        w_depth,
        b_depth,
        w_point,
        b_point,
    ) = gather_weights(shard_low, segs)
    modulation = mod_table.astype(jnp.float32)[None] + time_embed.reshape(lat_dev, 6, D)
    shift_one = modulation[:, 0][:, None, :]
    scale_one = modulation[:, 1][:, None, :]
    gate_one = modulation[:, 2][:, None, :]
    shift_two = modulation[:, 3][:, None, :]
    scale_two = modulation[:, 4][:, None, :]
    gate_two = modulation[:, 5][:, None, :]
    tokens = latents.reshape(lat_dev, tokens_dev, D).astype(jnp.float32)
    normed_one, inverse_one = norm_parts(tokens)
    hidden_one = to_low(normed_one * (1.0 + scale_one) + shift_one)
    projected = matmul(hidden_one, w_qkv)
    query_pre = projected[..., :D]
    key_pre = projected[..., D : 2 * D]
    queries = to_low(jnp.maximum(query_pre, 0.0)).reshape(lat_dev, tokens_dev, heads_lin, 32)
    keys_lin = to_low(jnp.maximum(key_pre, 0.0)).reshape(lat_dev, tokens_dev, heads_lin, 32)
    values_lin = to_low(projected[..., 2 * D :]).reshape(lat_dev, tokens_dev, heads_lin, 32)
    state_part = jnp.einsum(
        "lrhd,lrhe->lhde", keys_lin, values_lin, preferred_element_type=jnp.float32
    )
    sum_part = jnp.sum(keys_lin, axis=1, dtype=jnp.float32)
    kv_state, key_sum = state_sum(state_part, sum_part, jnp.float32, 2)
    query_f = queries.astype(jnp.float32)
    numerator = jnp.einsum("lrhd,lhde->lrhe", query_f, kv_state, precision=precise)
    denominator = jnp.einsum("lrhd,lhd->lrh", query_f, key_sum, precision=precise) + eps_linear
    attn_val = numerator / denominator[..., None]
    attended = to_low(attn_val.reshape(lat_dev, tokens_dev, D))
    branch_one = matmul(attended, w_attn_out) + b_attn_out.astype(jnp.float32)
    after_attn = tokens + gate_one * branch_one
    after_low, x_qkv = lax.optimization_barrier((to_low(after_attn), *spread([hidden_one])))
    query_c = to_low(matmul(after_low, w_cross_q)).reshape(
        lat_dev, tokens_dev, CROSS_HEADS, cross_dim
    )
    keyval = to_low(matmul(text, w_cross_kv))
    keys_c = keyval[..., :D].reshape(lat_dev, text_len, CROSS_HEADS, cross_dim)
    values_c = keyval[..., D:].reshape(lat_dev, text_len, CROSS_HEADS, cross_dim)
    scores = (
        jnp.einsum("lrhc,lthc->lhrt", query_c, keys_c, preferred_element_type=jnp.float32)
        * score_scale
    )
    row_peak = jnp.max(scores, axis=-1, keepdims=True)
    log_total = row_peak + jnp.log(jnp.sum(jnp.exp(scores - row_peak), axis=-1, keepdims=True))
    probs_low = to_low(jnp.exp(scores - log_total))
    cross_mixed = to_low(
        jnp.einsum(
            "lhrt,lthc->lrhc", probs_low, values_c, preferred_element_type=jnp.float32
        ).reshape(lat_dev, tokens_dev, D)
    )
    after_cross = after_attn + matmul(cross_mixed, w_cross_out) + b_cross_out.astype(jnp.float32)
    normed_two, inverse_two = norm_parts(after_cross)
    hidden_two, x_attn, x_cross_q = lax.optimization_barrier(
        (
            to_low(normed_two * (1.0 + scale_two) + shift_two),
            *spread([attended, after_low]),
        )
    )
    inner_pre = matmul(hidden_two, w_in) + b_in.astype(jnp.float32)
    active = to_low(jax.nn.silu(inner_pre)).reshape(lat_dev, row_dev, col_dev, 2 * FF)
    padded = jnp.pad(with_halo(active, (("seq", 1),), 1), ((0, 0), (0, 0), (1, 1), (0, 0)))
    conv_out = (
        depth_conv(padded, w_depth, row_dev, col_dev, False) + b_depth.astype(jnp.float32)
    ).reshape(lat_dev, tokens_dev, 2 * FF)
    up_part = conv_out[..., :FF]
    gate_part = conv_out[..., FF:]
    gated_mix = to_low(up_part * jax.nn.silu(gate_part))
    branch_two = lax.optimization_barrier(
        matmul(gated_mix, w_point) + b_point.astype(jnp.float32)
    )
    output = (after_cross + gate_two * branch_two).astype(jnp.bfloat16).reshape(latents.shape)
    grad_out = cotangent.reshape(lat_dev, tokens_dev, D).astype(jnp.float32)
    grad_gate_two = jnp.sum(grad_out * branch_two, axis=1)
    grad_branch_two = to_low(grad_out * gate_two)
    grad_branch_two, x_cross_out, x_inner = lax.optimization_barrier(
        (grad_branch_two, *spread([cross_mixed, hidden_two]))
    )
    grad_gated = matmul_t(grad_branch_two, w_point)
    grad_up = grad_gated * jax.nn.silu(gate_part)
    grad_gate = grad_gated * up_part * silu_slope(gate_part)
    grad_conv = to_low(jnp.concatenate([grad_up, grad_gate], axis=-1)).reshape(
        lat_dev, row_dev, col_dev, 2 * FF
    )
    grad_b_depth = jnp.sum(grad_conv, axis=(0, 1, 2), dtype=jnp.float32)
    tap_grads = []
    for tap_row in range(3):
        for tap_col in range(3):
            tap_grads.append(
                jnp.einsum(
                    "lrcf,lrcf->f",
                    padded[:, tap_row : tap_row + row_dev, tap_col : tap_col + col_dev],
                    grad_conv,
                    preferred_element_type=jnp.float32,
                )
            )
    grad_w_depth = jnp.stack(tap_grads)
    grad_padded = jnp.pad(with_halo(grad_conv, (("seq", 1),), 1), ((0, 0), (0, 0), (1, 1), (0, 0)))
    grad_active = depth_conv(grad_padded, w_depth, row_dev, col_dev, True).reshape(
        lat_dev, tokens_dev, 2 * FF
    )
    grad_inner = to_low(grad_active * silu_slope(inner_pre))
    grad_inner, x_point = lax.optimization_barrier((grad_inner, *spread([gated_mix])))
    grad_hidden_two = matmul_t(grad_inner, w_in)
    grad_shift_two = jnp.sum(grad_hidden_two, axis=1)
    grad_scale_two = jnp.sum(grad_hidden_two * normed_two, axis=1)
    grad_second = grad_out + norm_back(grad_hidden_two * (1.0 + scale_two), normed_two, inverse_two)
    grad_cross_out = to_low(grad_second)
    grad_mixed = to_low(matmul_t(grad_cross_out, w_cross_out)).reshape(
        lat_dev, tokens_dev, CROSS_HEADS, cross_dim
    )
    scores_again = (
        jnp.einsum("lrhc,lthc->lhrt", query_c, keys_c, preferred_element_type=jnp.float32)
        * score_scale
    )
    probs = jnp.exp(scores_again - log_total)
    grad_probs = jnp.einsum(
        "lrhc,lthc->lhrt", grad_mixed, values_c, preferred_element_type=jnp.float32
    )
    grad_values_c = jnp.einsum(
        "lhrt,lrhc->lthc", to_low(probs), grad_mixed, preferred_element_type=jnp.float32
    )
    grad_scores = to_low(probs * (grad_probs - jnp.sum(probs * grad_probs, axis=-1, keepdims=True)))
    grad_query_c = to_low(
        jnp.einsum("lhrt,lthc->lrhc", grad_scores, keys_c, preferred_element_type=jnp.float32)
        * score_scale
    ).reshape(lat_dev, tokens_dev, D)
    grad_keys_c = (
        jnp.einsum("lhrt,lrhc->lthc", grad_scores, query_c, preferred_element_type=jnp.float32)
        * score_scale
    )
    grad_keyval_part = jnp.concatenate(
        [grad_keys_c.reshape(lat_dev, text_len, D), grad_values_c.reshape(lat_dev, text_len, D)],
        axis=-1,
    )
    grad_keyval_part = grad_keyval_part.reshape(lat_dev, text_len, segs, 2 * D // segs)
    grad_keyval = to_low(
        lax.psum_scatter(
            grad_keyval_part.astype(jnp.bfloat16), "seq", scatter_dimension=2, tiled=True
        ).astype(jnp.float32)
    ).reshape(lat_dev, text_len, 2 * D // segs)
    grad_w_cross_kv = outer_sum(text, grad_keyval)
    grad_first = grad_second + matmul_t(grad_query_c, w_cross_q)
    grad_gate_one = jnp.sum(grad_first * branch_one, axis=1)
    grad_branch_one = to_low(grad_first * gate_one)
    grad_branch_one, y_inner, y_point = lax.optimization_barrier(
        (grad_branch_one, *collect([grad_inner, grad_branch_two]))
    )
    grad_attended = matmul_t(grad_branch_one, w_attn_out).reshape(
        lat_dev, tokens_dev, heads_lin, 32
    )
    grad_numer = grad_attended / denominator[..., None]
    grad_denom = -jnp.sum(grad_attended * attn_val, axis=-1) / denominator
    grad_query = (
        jnp.einsum("lrhe,lhde->lrhd", grad_numer, kv_state, precision=precise)
        + grad_denom[..., None] * key_sum[:, None]
    )
    state_grad_part = jnp.einsum("lrhd,lrhe->lhde", query_f, grad_numer, precision=precise)
    sum_grad_part = jnp.einsum("lrhd,lrh->lhd", query_f, grad_denom, precision=precise)
    state_grad, sum_grad = state_sum(state_grad_part, sum_grad_part, jnp.bfloat16, 3)
    keys_f = keys_lin.astype(jnp.float32)
    values_f = values_lin.astype(jnp.float32)
    grad_keys = (
        jnp.einsum("lrhe,lhde->lrhd", values_f, state_grad, precision=precise) + sum_grad[:, None]
    )
    grad_values = jnp.einsum("lrhd,lhde->lrhe", keys_f, state_grad, precision=precise)
    grad_projected = to_low(
        jnp.concatenate(
            [
                grad_query.reshape(lat_dev, tokens_dev, D) * (query_pre > 0.0),
                grad_keys.reshape(lat_dev, tokens_dev, D) * (key_pre > 0.0),
                grad_values.reshape(lat_dev, tokens_dev, D),
            ],
            axis=-1,
        )
    )
    grad_projected, y_cross_out, y_cross_q, y_attn = lax.optimization_barrier(
        (grad_projected, *collect([grad_cross_out, grad_query_c, grad_branch_one]))
    )
    grad_hidden_one = matmul_t(grad_projected, w_qkv)
    grad_input = grad_first + norm_back(
        grad_hidden_one * (1.0 + scale_one), normed_one, inverse_one
    )
    grad_table = jnp.sum(
        jnp.stack(
            [
                jnp.sum(grad_hidden_one, axis=1),
                jnp.sum(grad_hidden_one * normed_one, axis=1),
                grad_gate_one,
                grad_shift_two,
                grad_scale_two,
                grad_gate_two,
            ],
            axis=1,
        ),
        axis=0,
    )
    grad_table = lax.optimization_barrier(grad_table)
    col_d = D // segs
    col_ff = 2 * FF // segs
    small_parts = jnp.concatenate(
        [
            grad_table.reshape(6, segs, col_d).transpose(1, 0, 2).reshape(segs, -1),
            grad_w_depth.reshape(9, segs, col_ff).transpose(1, 0, 2).reshape(segs, -1),
            grad_b_depth.reshape(segs, col_ff),
        ],
        axis=1,
    ).astype(jnp.bfloat16)
    small_parts = small_parts.reshape(segs, -1, LANE)
    small_mine = (
        lax.psum_scatter(small_parts, "seq", scatter_dimension=0, tiled=True)
        .astype(jnp.float32)
        .reshape(-1)
    )
    table_q = small_mine[: 6 * col_d].reshape(6, col_d)
    depth_q = small_mine[6 * col_d : 6 * col_d + 9 * col_ff].reshape(9, col_ff)
    depth_bias_q = small_mine[6 * col_d + 9 * col_ff :].reshape(1, col_ff)

    (y_qkv,) = collect([grad_projected])
    grad_w_qkv = outer_sum(x_qkv, y_qkv)
    grad_w_attn_out = outer_sum(x_attn, y_attn)
    grad_w_cross_q = outer_sum(x_cross_q, y_cross_q)
    grad_w_cross_out = outer_sum(x_cross_out, y_cross_out)
    grad_w_in = outer_sum(x_inner, y_inner)
    grad_w_point = outer_sum(x_point, y_point)
    grad_b_attn_out = jnp.sum(y_attn, axis=0, dtype=jnp.float32)
    grad_b_cross_out = jnp.sum(y_cross_out, axis=0, dtype=jnp.float32)
    grad_b_in = jnp.sum(y_inner, axis=0, dtype=jnp.float32)
    grad_b_point = jnp.sum(y_point, axis=0, dtype=jnp.float32)
    bias_part = jnp.concatenate(
        [grad_b_attn_out, grad_b_cross_out, grad_b_in, depth_bias_q.ravel(), grad_b_point]
    )
    len_bias = bias_part.size
    bias_rows = -(-bias_part.size // (8 * LANE)) * 8
    bias_part = jnp.pad(bias_part, (0, bias_rows * LANE - bias_part.size)).reshape(-1, LANE)
    quarter_grad = write_flat(
        segs,
        [
            table_q,
            grad_w_qkv,
            grad_w_attn_out,
            grad_b_attn_out,
            grad_w_cross_q,
            grad_w_cross_kv,
            grad_w_cross_out,
            grad_b_cross_out,
            grad_w_in,
            grad_b_in,
            depth_q,
            depth_bias_q,
            grad_w_point,
            grad_b_point,
        ],
    )
    if count_dp == 8 and quarter_grad.shape[0] % (8 * 240) == 0:
        grad_shard = reduce_shard(quarter_grad)
    else:
        grad_shard = lax.psum_scatter(
            quarter_grad.reshape(count_dp, -1, LANE), "dp", scatter_dimension=0, tiled=True
        )
        grad_shard = grad_shard.reshape(-1, LANE).astype(jnp.float32)
    factor, bias_grads = scale_of(grad_shard, bias_part)
    flat_outs = adam(
        factor,
        grad_shard,
        params_rows,
        moment_one.reshape(-1, LANE),
        moment_two.reshape(-1, LANE),
    )
    gradient, moment_one_new, moment_two_new, update = [
        value.reshape(params.shape) for value in flat_outs
    ]
    return (
        output,
        grad_input.reshape(latents.shape),
        gradient,
        moment_one_new,
        moment_two_new,
        update,
        bias_grads.reshape(1, -1)[:, :len_bias],
    )


def solution(mesh):
    return jax.shard_map(
        shards,
        mesh=mesh,
        in_specs=(
            P("dp", "seq", None, None),
            P("dp", None, None),
            P("dp", None),
            P("dp", "seq", None, None),
            P("seq", "dp"),
            P("seq", "dp"),
            P("seq", "dp"),
        ),
        out_specs=(
            P("dp", "seq", None, None),
            P("dp", "seq", None, None),
            P("seq", "dp"),
            P("seq", "dp"),
            P("seq", "dp"),
            P("seq", "dp"),
            P("seq", None),
        ),
        check_vma=False,
    )
```

```python
import math

import jax
import jax.numpy as jnp
from jax import lax
from jax.experimental import pallas as pl
from jax.experimental.pallas import tpu as pltpu
from jax.sharding import PartitionSpec as P

D = 1152
FF = 2880
CROSS_HEADS = 16


precise = lax.Precision.HIGHEST
eps_norm = 1e-06
eps_linear = 1e-06
beta_first = 0.9
beta_second = 0.95
adam_eps = 1e-08
weight_decay = 0.01
adam_steps = 100.0


def with_halo(block, sides, width):
    for axis, dim in sides:
        count = lax.axis_size(axis)
        forward = [(i, i + 1) for i in range(count - 1)]
        backward = [(target, source) for source, target in forward]
        low = lax.ppermute(
            lax.slice_in_dim(block, block.shape[dim] - width, None, axis=dim), axis, forward
        )
        high = lax.ppermute(lax.slice_in_dim(block, 0, width, axis=dim), axis, backward)
        block = jnp.concatenate([low, block, high], axis=dim)
    return block


def piece_specs():
    return [
        (6, D, False),
        (D, 3 * D, False),
        (D, D, False),
        (1, D, True),
        (D, D, False),
        (D, 2 * D, False),
        (D, D, False),
        (1, D, True),
        (D, 2 * FF, False),
        (1, 2 * FF, True),
        (9, 2 * FF, False),
        (1, 2 * FF, True),
        (FF, D, False),
        (1, D, True),
    ]


LANE = 128
UNIT = 32
MESH = pl.DeviceIdType.MESH


def merge_units(values, lane_unit):
    out = values[0]
    last = values[0]
    for position in range(1, 4):
        if values[position] is not last:
            out = jnp.where(lane_unit >= position, values[position], out)
            last = values[position]
    return out


def rolled(value, units):
    units = units % 4
    return value if units == 0 else pltpu.roll(value, units * UNIT, 1)


def matrix_rows(count_rows):
    return 384 if count_rows % 384 == 0 else 576 if count_rows % 576 == 0 else 64


def read_matrix(flat, offset, rows_of, cols_of, segs):
    total_rows = flat.shape[1]
    per_row = cols_of // segs // UNIT
    unit_at = offset // UNIT
    block = matrix_rows(rows_of)
    base = unit_at // 4 // 16 * 16
    shift = unit_at - 4 * base
    step = block * per_row // 4
    need = (shift + block * per_row - 1) // 4 + 1
    need = -(-need // 16) * 16
    assert base + (rows_of // block - 1) * step + need <= total_rows
    tiles = cols_of // LANE

    def kernel(in_ref, out_ref, wide, mixed):
        def widen(at, _):
            row = pl.multiple_of(at * 16, 16)
            for seg in range(segs):
                wide[pl.ds(pl.multiple_of(seg * need + row, 16), 16), :] = in_ref[
                    seg, pl.ds(row, 16), :
                ].astype(jnp.float32)
            return 0

        lax.fori_loop(0, need // 16, widen, 0, unroll=8)
        lane_unit = lax.broadcasted_iota(jnp.int32, (8, LANE), 1) // UNIT

        def group(at, _):
            for phase in range(4):
                loaded = {}
                turned = {}
                for tile in range(tiles):
                    parts = []
                    for slot in range(4):
                        col = 4 * tile + slot
                        seg, unit = col // per_row, col % per_row
                        source = shift + phase * per_row + unit
                        key = (seg, source // 4)
                        if key not in loaded:
                            loaded[key] = wide[
                                pl.ds(seg * need + key[1] + at * (8 * per_row), 8, stride=per_row),
                                :,
                            ]
                        turn = (slot - source) % 4
                        if (key, turn) not in turned:
                            turned[key, turn] = rolled(loaded[key], turn)
                        parts.append(turned[key, turn])
                    mixed[pl.ds(tile * block + phase + at * 32, 8, stride=4), :] = merge_units(
                        parts, lane_unit
                    )
            return 0

        lax.fori_loop(0, block // 32, group, 0, unroll=2)

        def narrow(at, _):
            row = pl.multiple_of(at * 16, 16)
            for tile in range(tiles):
                out_ref[pl.ds(row, 16), tile * LANE : (tile + 1) * LANE] = mixed[
                    pl.ds(pl.multiple_of(tile * block + row, 16), 16), :
                ].astype(jnp.bfloat16)
            return 0

        lax.fori_loop(0, block // 16, narrow, 0, unroll=2)

    return pl.pallas_call(
        kernel,
        grid=(rows_of // block,),
        in_specs=[
            pl.BlockSpec(
                (pl.Element(segs), pl.Element(need), pl.Element(LANE)),
                lambda at: (0, pl.multiple_of(base + at * step, 16), 0),
            )
        ],
        out_specs=pl.BlockSpec((block, cols_of), lambda at: (at, 0)),
        out_shape=jax.ShapeDtypeStruct((rows_of, cols_of), jnp.bfloat16),
        scratch_shapes=[
            pltpu.VMEM((segs * need, LANE), jnp.float32),
            pltpu.VMEM((tiles * block, LANE), jnp.float32),
        ],
        compiler_params=pltpu.CompilerParams(vmem_limit_bytes=48 << 20),
        cost_estimate=pl.CostEstimate(
            flops=0, bytes_accessed=4 * rows_of * cols_of, transcendentals=0
        ),
        name="read_matrix",
    )(flat)


def write_flat(segs, parts):
    specs = piece_specs()
    block_rows = 576
    total = sum(rows_of * cols_of // segs for rows_of, cols_of, _ in specs)
    flat_rows = total // LANE
    places = []
    offset = 0
    big, small = [], []
    for (rows_of, cols_of, _), value in zip(specs, parts):
        width = cols_of // segs
        length = rows_of * width
        if rows_of > 9:
            assert rows_of % block_rows == 0
            places.append((True, offset, rows_of, width, len(big)))
            big.append(value)
        else:
            lead = offset % LANE
            rest = -(lead + length) % LANE
            padded = jnp.pad(value.reshape(-1), (lead, rest)).reshape(-1, LANE)
            places.append((False, offset, length, None, len(small)))
            small.append(padded)
        offset += length
    widths = sorted({place[3] for place in places if place[0]})
    chunk = 144

    def kernel(*refs):
        big_refs = refs[: len(big)]
        small_refs = refs[len(big) : len(big) + len(small)]
        out_ref = refs[len(big) + len(small)]
        flat = refs[len(big) + len(small) + 1]
        bufs = refs[len(big) + len(small) + 2 : len(big) + len(small) + 2 + len(widths)]
        in_sem = refs[-1]
        lane_unit = lax.broadcasted_iota(jnp.int32, (8, LANE), 1) // UNIT
        row_unit = lax.broadcasted_iota(jnp.int32, (1, LANE), 1) // UNIT

        def place_small(ref, offset, length):
            first = offset // LANE
            last = (offset + length - 1) // LANE
            lead = offset % LANE // UNIT
            tail = (offset + length) % LANE // UNIT
            count = last - first + 1
            if count > 2:

                def copy_row(at, _):
                    flat[pl.ds(first + 1 + at, 1), :] = ref[pl.ds(1 + at, 1), :]
                    return 0

                lax.fori_loop(0, count - 2, copy_row, 0)
            keep = row_unit >= lead
            if count == 1 and tail:
                keep = keep & (row_unit < tail)
            flat[first : first + 1, :] = jnp.where(keep, ref[0:1, :], flat[first : first + 1, :])
            if count > 1:
                flat[last : last + 1, :] = (
                    jnp.where(
                        row_unit < tail, ref[count - 1 : count, :], flat[last : last + 1, :]
                    )
                    if tail
                    else ref[count - 1 : count, :]
                )

        def fetch_block(ref, buf, width, at, slot):
            row = pl.multiple_of(at * block_rows, 64)
            return [
                pltpu.make_async_copy(
                    ref.at[pl.ds(row, block_rows), tile * LANE : (tile + 1) * LANE],
                    buf.at[slot, tile],
                    in_sem.at[widths.index(width), slot, tile],
                )
                for tile in range(-(-width // LANE))
            ]

        def place_big(ref, buf, offset, rows_of, width):
            per_row = width // UNIT
            first = offset // LANE
            shift = offset % LANE // UNIT
            block = block_rows
            blocks = rows_of // block

            def fetch(at, slot):
                return fetch_block(ref, buf, width, at, slot)

            def one_block(at, _):
                slot = lax.rem(at, 2)

                @pl.when(at + 1 < blocks)
                def _():
                    for copy in fetch(at + 1, 1 - slot):
                        copy.start()

                for copy in fetch(at, slot):
                    copy.wait()

                def group(sub, _):
                    loaded = {}
                    turned = {}

                    def unit_value(phase, unit, lane):
                        key = (phase, unit // 4)
                        if key not in loaded:
                            loaded[key] = buf[
                                slot, key[1], pl.ds(phase + sub * 32, 8, stride=4), :
                            ]
                        turn = (lane - unit) % 4
                        if (key, turn) not in turned:
                            turned[key, turn] = rolled(loaded[key], turn)
                        return turned[key, turn]

                    start = first + (at * (block // 4) + sub * 8) * per_row
                    for row in range(per_row + (1 if shift else 0)):
                        where = pl.ds(start + row, 8, stride=per_row)
                        parts = []
                        kept = None
                        for lane in range(4):
                            unit = 4 * row + lane - shift
                            if unit < 0 or unit >= 4 * per_row:
                                if kept is None:
                                    kept = flat[where, :]
                                parts.append(kept)
                            else:
                                parts.append(unit_value(unit // per_row, unit % per_row, lane))
                        flat[where, :] = merge_units(parts, lane_unit)
                    return 0

                lax.fori_loop(0, block // 32, group, 0, unroll=6)
                return 0

            lax.fori_loop(0, blocks, one_block, 0)

        def first_fetch(width, after):
            for is_big, _, _, other, index in places:
                if is_big and other == width and index > after:
                    buf = bufs[widths.index(width)]
                    for copy in fetch_block(big_refs[index], buf, width, 0, 0):
                        copy.start()
                    return

        for width in widths:
            first_fetch(width, -1)
        for is_big, offset, rows_of, width, index in places:
            if is_big:
                place_big(big_refs[index], bufs[widths.index(width)], offset, rows_of, width)
                first_fetch(width, index)
            else:
                place_small(small_refs[index], offset, rows_of)

        def narrow(at, _):
            where = pl.ds(pl.multiple_of(at * chunk, 16), chunk)
            out_ref[where, :] = flat[where, :].astype(jnp.bfloat16)
            return 0

        lax.fori_loop(0, flat_rows // chunk, narrow, 0)

    return pl.pallas_call(
        kernel,
        in_specs=[pl.BlockSpec(memory_space=pl.ANY)] * len(big)
        + [pl.BlockSpec(memory_space=pltpu.VMEM)] * len(small),
        out_specs=pl.BlockSpec(memory_space=pltpu.VMEM),
        out_shape=jax.ShapeDtypeStruct((flat_rows, LANE), jnp.bfloat16),
        scratch_shapes=[pltpu.VMEM((flat_rows, LANE), jnp.float32)]
        + [
            pltpu.VMEM((2, -(-width // LANE), block_rows, LANE), jnp.float32) for width in widths
        ]
        + [
            pltpu.SemaphoreType.DMA((len(widths), 2, -(-widths[-1] // LANE))),
        ],
        compiler_params=pltpu.CompilerParams(vmem_limit_bytes=56 << 20),
        cost_estimate=pl.CostEstimate(flops=0, bytes_accessed=6 * total, transcendentals=0),
        name="write_flat",
    )(*big, *small)


def gather_flat(shard):
    rows = shard.shape[0]
    first = (rows // 2 + 15) // 16 * 16
    parts = ((0, first), (first, rows - first))

    def kernel(
        in_ref,
        out_ref,
        own_sem,
        z_send,
        z_recv,
        x_send,
        x_recv,
        y_send,
        y_recv,
        d_send,
        d_recv,
        c_send,
        c_recv,
    ):
        dp = lax.axis_index("dp")
        seq = lax.axis_index("seq")
        near, far = lax.rem(dp, 2), lax.div(dp, 2)
        core, side = lax.rem(seq, 2), lax.div(seq, 2)

        half = lax.div(far, 2)
        place = far + half * (3 - 2 * far)
        inner = far + 1 - 2 * half
        outer = far - 1 + 2 * half

        def dp_of(turn, flip):
            at = place if turn == 0 else 1 - place if turn == 1 else turn
            return 2 * (at + half * (3 - 2 * at)) + (1 - near if flip else near)

        def seq_of(flip, other_core):
            return 2 * (1 - side if flip else side) + (1 - core if other_core else core)

        def region(seq_at, dp_at, part):
            start, length = parts[part]
            return out_ref.at[
                seq_at, pl.ds(pl.multiple_of(dp_at * rows + start, 16), length), :
            ]

        def own_region(part):
            start, length = parts[part]
            return in_ref.at[pl.ds(start, length), :]

        def column(turn, part):
            return region(seq, dp_of(turn, False), part)

        def source(turn, part):
            return column(turn, part) if turn else own_region(part)

        def remote(src, dst, send, recv, target):
            return pltpu.make_async_remote_copy(
                src_ref=src,
                dst_ref=dst,
                send_sem=send,
                recv_sem=recv,
                device_id=target,
                device_id_type=MESH,
            )

        x_peer = {"dp": dp_of(0, True)}
        y_peer = {"seq": seq_of(True, False)}
        c_peer = {"seq": seq_of(False, True)}

        def z_copy(kind, part):
            turn = (0, 0, 1, 2, 3)[kind]
            arrives = (place, 0, 2, 1, 2)[kind]
            return remote(
                source(turn, part),
                column(turn, part),
                z_send.at[kind, part],
                z_recv.at[arrives, part],
                {"dp": 2 * (inner if kind in (0, 2) else outer) + near},
            )

        def z_in(turn, part):
            here = column(turn, part)
            return remote(
                here, here, z_send.at[0, part], z_recv.at[turn - 1, part], {"dp": 2 * inner + near}
            )

        def x_out(turn, part):
            return remote(
                source(turn, part),
                column(turn, part),
                x_send.at[turn, part],
                x_recv.at[turn, part],
                x_peer,
            )

        def x_in(turn, part):
            here = region(seq, dp_of(turn, True), part)
            return remote(here, here, x_send.at[turn, part], x_recv.at[turn, part], x_peer)

        def y_out(turn, part):
            return remote(
                source(turn, part),
                column(turn, part),
                y_send.at[turn, part],
                y_recv.at[turn, part],
                y_peer,
            )

        def y_in(turn, part):
            here = region(seq_of(True, False), dp_of(turn, False), part)
            return remote(here, here, y_send.at[turn, part], y_recv.at[turn, part], y_peer)

        def d_out(turn, part):
            if part == 0:
                here, target = region(seq, dp_of(turn, True), part), y_peer
            else:
                here, target = region(seq_of(True, False), dp_of(turn, False), part), x_peer
            return remote(here, here, d_send.at[turn, part], d_recv.at[turn, part], target)

        def d_in(turn, part):
            here = region(seq_of(True, False), dp_of(turn, True), part)
            target = y_peer if part == 0 else x_peer
            return remote(here, here, d_send.at[turn, part], d_recv.at[turn, part], target)

        def c_copy(kind, turn, part, incoming):
            where = region(
                seq_of(kind in (2, 3), incoming), dp_of(turn, kind in (1, 3)), part
            )
            src = own_region(part) if kind == 0 and turn == 0 else where
            return remote(
                src if not incoming else where,
                where,
                c_send.at[kind, turn, part],
                c_recv.at[kind, turn, part],
                c_peer,
            )

        barrier = pltpu.get_barrier_semaphore()
        for target in (x_peer, y_peer, c_peer, {"dp": 2 * inner + near}):
            pl.semaphore_signal(barrier, inc=1, device_id=target, device_id_type=MESH)

        @pl.when(place == 1)
        def _():
            pl.semaphore_signal(
                barrier, inc=1, device_id={"dp": 2 * outer + near}, device_id_type=MESH
            )
            pl.semaphore_wait(barrier, 5)

        @pl.when(place == 0)
        def _():
            pl.semaphore_wait(barrier, 4)

        keep = [
            pltpu.make_async_copy(own_region(part), region(seq, dp, part), own_sem.at[part])
            for part in range(2)
        ]
        def outwards(kind, part):
            @pl.when(place == 1)
            def _():
                z_copy(kind, part).start()

        for part in range(2):
            z_copy(0, part).start()
            outwards(1, part)
            x_out(0, part).start()
            y_out(0, part).start()
        for part in range(2):
            keep[part].start()
            c_copy(0, 0, part, False).start()

        def sideways(turn):
            for part in range(2):
                x_in(turn, part).wait_recv()
                if part == 0:
                    d_out(turn, part).start()
                c_copy(1, turn, part, False).start()
                y_in(turn, part).wait_recv()
                if part == 1:
                    d_out(turn, part).start()
                c_copy(2, turn, part, False).start()

        def diagonal(turn):
            for part in range(2):
                d_in(turn, part).wait_recv()
                c_copy(3, turn, part, False).start()

        for turn in range(1, 4):
            for part in range(2):
                z_in(turn, part).wait_recv()
                outwards(turn + 1, part)
                x_out(turn, part).start()
                y_out(turn, part).start()
                c_copy(0, turn, part, False).start()
            sideways(turn - 1)
            if turn > 1:
                diagonal(turn - 2)
        sideways(3)
        diagonal(2)
        diagonal(3)

        @pl.when(place == 1)
        def _():
            for kind in range(1, 5):
                for part in range(2):
                    z_copy(kind, part).wait_send()

        for part in range(2):
            keep[part].wait()
            z_copy(0, part).wait_send()
            for turn in range(4):
                x_out(turn, part).wait_send()
                y_out(turn, part).wait_send()
                d_out(turn, part).wait_send()
                for kind in range(4):
                    c_copy(kind, turn, part, False).wait_send()
                    c_copy(kind, turn, part, True).wait_recv()

    return pl.pallas_call(
        kernel,
        in_specs=[pl.BlockSpec(memory_space=pltpu.VMEM)],
        out_specs=pl.BlockSpec(memory_space=pl.ANY),
        out_shape=jax.ShapeDtypeStruct((4, 8 * rows, LANE), jnp.bfloat16),
        scratch_shapes=[
            pltpu.SemaphoreType.DMA((2,)),
            pltpu.SemaphoreType.DMA((5, 2)),
            pltpu.SemaphoreType.DMA((3, 2)),
        ]
        + [pltpu.SemaphoreType.DMA((4, 2))] * 6
        + [pltpu.SemaphoreType.DMA((4, 4, 2))] * 2,
        compiler_params=pltpu.CompilerParams(collective_id=5, has_side_effects=True),
        name="gather_flat",
    )(shard)


def round_rows(values):
    def kernel(in_ref, out_ref):
        out_ref[...] = in_ref[...].astype(jnp.bfloat16)

    return pl.pallas_call(
        kernel,
        in_specs=[pl.BlockSpec(memory_space=pltpu.VMEM)],
        out_specs=pl.BlockSpec(memory_space=pltpu.VMEM),
        out_shape=jax.ShapeDtypeStruct(values.shape, jnp.bfloat16),
        name="round_rows",
    )(values)


def gather_weights(shard_low, segs):
    if segs == 4 and lax.axis_size("dp") == 8 and shard_low.shape[0] % 16 == 0:
        flat = gather_flat(shard_low)
    else:
        whole = lax.all_gather(shard_low, ("seq", "dp"), axis=0, tiled=True)
        flat = whole.reshape(segs, -1, LANE)
    pieces = []
    offset = 0
    for rows_of, cols_of, vector in piece_specs():
        length = rows_of * cols_of // segs
        if rows_of > 9:
            pieces.append(read_matrix(flat, offset, rows_of, cols_of, segs))
        else:
            first, last = offset // LANE, -(-(offset + length) // LANE)
            lead = offset - first * LANE
            block = flat[:, first:last].reshape(segs, -1)[:, lead : lead + length]
            block = block.reshape(segs, rows_of, cols_of // segs).transpose(1, 0, 2)
            pieces.append(block.reshape(cols_of) if vector else block.reshape(rows_of, cols_of))
        offset = offset + length
    return pieces


def peer_barrier(groups):
    barrier = pltpu.get_barrier_semaphore()
    total = 0
    for axis, count in groups:
        me = lax.axis_index(axis)
        for step in range(1, count):
            pl.semaphore_signal(
                barrier, inc=1, device_id={axis: lax.rem(me + step, count)}, device_id_type=MESH
            )
        total += count - 1
    pl.semaphore_wait(barrier, total)


def exchange(axis, count, source, slots, send_sem, recv_sem):
    me = lax.axis_index(axis)
    for step in range(1, count):
        pltpu.make_async_remote_copy(
            src_ref=source,
            dst_ref=slots.at[me],
            send_sem=send_sem.at[step - 1],
            recv_sem=recv_sem.at[me],
            device_id={axis: lax.rem(me + step, count)},
            device_id_type=MESH,
        ).start()


def exchange_wait(axis, count, source, slots, send_sem, recv_sem):
    me = lax.axis_index(axis)
    for step in range(1, count):
        peer = lax.rem(me + step, count)
        copy = pltpu.make_async_remote_copy(
            src_ref=source,
            dst_ref=slots.at[peer],
            send_sem=send_sem.at[step - 1],
            recv_sem=recv_sem.at[peer],
            device_id={axis: peer},
            device_id_type=MESH,
        )
        copy.wait_send()
        copy.wait_recv()


def in_order(axis, count, own, slots):
    me = lax.axis_index(axis)
    total = None
    for index in range(count):
        term = jnp.where(me == index, own, slots[index].astype(jnp.float32))
        total = term if total is None else total + term
    return total


def seq_sum(block, collective_id):
    count = lax.axis_size("seq")

    def kernel(in_ref, out_ref, slots, send_sem, recv_sem):
        peer_barrier([("seq", count)])
        exchange("seq", count, in_ref, slots, send_sem, recv_sem)
        exchange_wait("seq", count, in_ref, slots, send_sem, recv_sem)
        out_ref[...] = in_order("seq", count, in_ref[...].astype(jnp.float32), slots)

    return pl.pallas_call(
        kernel,
        in_specs=[pl.BlockSpec(memory_space=pltpu.VMEM)],
        out_specs=pl.BlockSpec(memory_space=pltpu.VMEM),
        out_shape=jax.ShapeDtypeStruct(block.shape, jnp.float32),
        scratch_shapes=[
            pltpu.VMEM((count,) + block.shape, block.dtype),
            pltpu.SemaphoreType.DMA((count - 1,)),
            pltpu.SemaphoreType.DMA((count,)),
        ],
        compiler_params=pltpu.CompilerParams(collective_id=collective_id, has_side_effects=True),
        name="seq_sum",
    )(block)


def state_sum(state, sums, kind, collective_id):
    heads = state.shape[1]
    flat = jnp.concatenate(
        [state.reshape(-1, LANE), jnp.pad(sums.reshape(-1), (0, -sums.size % LANE)).reshape(-1, LANE)]
    ).astype(kind)
    rows = flat.shape[0]
    flat = jnp.pad(flat, ((0, -rows % 16), (0, 0)))
    total = seq_sum(flat, collective_id)
    split = state.size // LANE
    return (
        total[:split].reshape(state.shape),
        total[split:].reshape(-1)[: sums.size].reshape(1, heads, -1),
    )


def reduce_shard(flat):
    rows = flat.shape[0] // 8
    pieces = 5
    part = rows // pieces
    step = 112

    def kernel(in_ref, out_ref, recv_x, send_z, recv_z, x_send, x_recv, z_send, z_recv):
        me = lax.axis_index("dp")
        near = lax.rem(me, 2)
        far = lax.div(me, 2)
        partner = me + 1 - 2 * near

        def far_of(shift):
            return lax.rem(far + shift, 4)

        barrier = pltpu.get_barrier_semaphore()
        pl.semaphore_signal(barrier, inc=1, device_id={"dp": partner}, device_id_type=MESH)
        for shift in range(1, 4):
            pl.semaphore_signal(
                barrier,
                inc=1,
                device_id={"dp": 2 * far_of(shift) + near},
                device_id_type=MESH,
            )
        pl.semaphore_wait(barrier, 4)

        def window(shard, piece):
            return pl.ds(pl.multiple_of(shard * rows + piece * part, 16), part)

        def x_copy(shift, piece):
            return pltpu.make_async_remote_copy(
                src_ref=in_ref.at[window(2 * far_of(shift) + 1 - near, piece), :],
                dst_ref=recv_x.at[shift, pl.ds(piece * part, part), :],
                send_sem=x_send.at[shift, piece],
                recv_sem=x_recv.at[shift, piece],
                device_id={"dp": partner},
                device_id_type=MESH,
            )

        def z_copy(shift, piece):
            return pltpu.make_async_remote_copy(
                src_ref=send_z.at[shift - 1, pl.ds(piece * part, part), :],
                dst_ref=recv_z.at[shift - 1, pl.ds(piece * part, part), :],
                send_sem=z_send.at[shift - 1, piece],
                recv_sem=z_recv.at[shift - 1, piece],
                device_id={"dp": 2 * far_of(shift) + near},
                device_id_type=MESH,
            )

        order = (1, 2, 3, 0)
        for shift in order:
            for piece in range(pieces):
                x_copy(shift, piece).start()

        def own_sum(shift, row, at):
            start = (2 * far_of(shift) + near) * rows + row + at * step
            own = in_ref[pl.ds(pl.multiple_of(start, 16), step), :]
            other = recv_x[shift, pl.ds(pl.multiple_of(row + at * step, 16), step), :]
            return own.astype(jnp.float32) + other.astype(jnp.float32)

        for shift in order:
            for piece in range(pieces):
                x_copy(shift, piece).wait_recv()
                row = piece * part

                def add(at, _, shift=shift, row=row):
                    where = pl.ds(pl.multiple_of(row + at * step, 16), step)
                    total = own_sum(shift, row, at)
                    if shift:
                        send_z[shift - 1, where, :] = total.astype(jnp.bfloat16)
                    else:
                        out_ref[where, :] = total
                    return 0

                lax.fori_loop(0, part // step, add, 0)
                if shift:
                    z_copy(shift, piece).start()
        for shift in range(1, 4):
            for piece in range(pieces):
                z_copy(shift, piece).wait_recv()
                row = piece * part

                def gather(at, _, shift=shift, row=row):
                    where = pl.ds(pl.multiple_of(row + at * step, 16), step)
                    out_ref[where, :] = out_ref[where, :] + recv_z[shift - 1, where, :].astype(
                        jnp.float32
                    )
                    return 0

                lax.fori_loop(0, part // step, gather, 0)
        for shift in range(4):
            for piece in range(pieces):
                x_copy(shift, piece).wait_send()
                if shift:
                    z_copy(shift, piece).wait_send()

    block = (rows, LANE)
    return pl.pallas_call(
        kernel,
        in_specs=[pl.BlockSpec(memory_space=pltpu.VMEM)],
        out_specs=pl.BlockSpec(memory_space=pltpu.VMEM),
        out_shape=jax.ShapeDtypeStruct(block, jnp.float32),
        scratch_shapes=[
            pltpu.VMEM((4,) + block, jnp.bfloat16),
            pltpu.VMEM((3,) + block, jnp.bfloat16),
            pltpu.VMEM((3,) + block, jnp.bfloat16),
            pltpu.SemaphoreType.DMA((4, pieces)),
            pltpu.SemaphoreType.DMA((4, pieces)),
            pltpu.SemaphoreType.DMA((3, pieces)),
            pltpu.SemaphoreType.DMA((3, pieces)),
        ],
        compiler_params=pltpu.CompilerParams(
            collective_id=4, has_side_effects=True, vmem_limit_bytes=40 << 20
        ),
        name="reduce_shard",
    )(flat)


def scale_of(grad_shard, bias_part):
    rows = grad_shard.shape[0]
    count_dp = lax.axis_size("dp")
    count_seq = lax.axis_size("seq")
    entries = rows * LANE * count_dp * count_seq
    chunk = 48 if rows % 48 == 0 else rows
    bias_rows = bias_part.shape[0]

    def kernel(
        grad_ref,
        bias_ref,
        factor_out,
        bias_out,
        square,
        square_dp,
        square_seq,
        partial,
        bias_slots,
        send_bias,
        recv_bias,
        send_dp,
        recv_dp,
        send_seq,
        recv_seq,
    ):
        peer_barrier([("dp", count_dp), ("seq", count_seq)])
        exchange("dp", count_dp, bias_ref, bias_slots, send_bias, recv_bias)

        def squares(at, total):
            part = grad_ref[pl.ds(at * chunk, chunk), :].astype(jnp.float32)
            return total + jnp.sum(part * part, axis=0, keepdims=True)

        total = lax.fori_loop(0, rows // chunk, squares, jnp.zeros((1, LANE), jnp.float32))
        square[...] = jnp.broadcast_to(total, (8, LANE))
        exchange("dp", count_dp, square, square_dp, send_dp, recv_dp)
        exchange_wait("dp", count_dp, square, square_dp, send_dp, recv_dp)
        partial[...] = in_order("dp", count_dp, square[...], square_dp)
        exchange("seq", count_seq, partial, square_seq, send_seq, recv_seq)
        exchange_wait("seq", count_seq, partial, square_seq, send_seq, recv_seq)
        whole = jnp.sum(
            in_order("seq", count_seq, partial[...], square_seq)[0:1], axis=1, keepdims=True
        )
        factor = lax.rsqrt(whole / entries + 1e-06)
        exchange_wait("dp", count_dp, bias_ref, bias_slots, send_bias, recv_bias)
        bias_out[...] = in_order("dp", count_dp, bias_ref[...], bias_slots) * factor
        factor_out[...] = jnp.broadcast_to(factor, (8, LANE))

    tile = (8, LANE)
    return pl.pallas_call(
        kernel,
        in_specs=[pl.BlockSpec(memory_space=pltpu.VMEM)] * 2,
        out_specs=[pl.BlockSpec(memory_space=pltpu.VMEM)] * 2,
        out_shape=[
            jax.ShapeDtypeStruct(tile, jnp.float32),
            jax.ShapeDtypeStruct((bias_rows, LANE), jnp.float32),
        ],
        scratch_shapes=[
            pltpu.VMEM(tile, jnp.float32),
            pltpu.VMEM((count_dp,) + tile, jnp.float32),
            pltpu.VMEM((count_seq,) + tile, jnp.float32),
            pltpu.VMEM(tile, jnp.float32),
            pltpu.VMEM((count_dp, bias_rows, LANE), jnp.float32),
            pltpu.SemaphoreType.DMA((count_dp - 1,)),
            pltpu.SemaphoreType.DMA((count_dp,)),
            pltpu.SemaphoreType.DMA((count_dp - 1,)),
            pltpu.SemaphoreType.DMA((count_dp,)),
            pltpu.SemaphoreType.DMA((count_seq - 1,)),
            pltpu.SemaphoreType.DMA((count_seq,)),
        ],
        compiler_params=pltpu.CompilerParams(
            collective_id=1, has_side_effects=True, vmem_limit_bytes=16 << 20
        ),
        name="scale_of",
    )(grad_shard, bias_part)


def adam(factor, grad_shard, params, moment_one, moment_two):
    rows = grad_shard.shape[0]
    block = 1680 if rows % 1680 == 0 else rows

    def kernel(
        factor_ref, grad_ref, param_ref, one_ref, two_ref, gradient_ref, one_out, two_out, update_ref
    ):
        gradient = grad_ref[...] * factor_ref[0:1, :]
        first = beta_first * one_ref[...] + (1.0 - beta_first) * gradient
        second = beta_second * two_ref[...] + (1.0 - beta_second) * gradient * gradient
        gradient_ref[...] = gradient
        one_out[...] = first
        two_out[...] = second
        first_hat = first / (1.0 - beta_first**adam_steps)
        second_hat = second / (1.0 - beta_second**adam_steps)
        update_ref[...] = (
            first_hat / (jnp.sqrt(second_hat) + adam_eps) + weight_decay * param_ref[...]
        )

    spec = pl.BlockSpec((block, LANE), lambda at: (at, 0))
    return pl.pallas_call(
        kernel,
        grid=(rows // block,),
        in_specs=[pl.BlockSpec((8, LANE), lambda at: (0, 0))] + [spec] * 4,
        out_specs=[spec] * 4,
        out_shape=[jax.ShapeDtypeStruct((rows, LANE), jnp.float32)] * 4,
        name="adam",
    )(factor, grad_shard, params, moment_one, moment_two)


def norm_parts(values):
    centred = values - jnp.mean(values, axis=-1, keepdims=True)
    inverse = lax.rsqrt(jnp.mean(centred * centred, axis=-1, keepdims=True) + eps_norm)
    return (centred * inverse, inverse)


def norm_back(grad_normed, normed, inverse):
    return inverse * (
        grad_normed
        - jnp.mean(grad_normed, axis=-1, keepdims=True)
        - normed * jnp.mean(grad_normed * normed, axis=-1, keepdims=True)
    )


def silu_slope(values):
    sigmoid_v = jax.nn.sigmoid(values)
    return sigmoid_v * (1.0 + values * (1.0 - sigmoid_v))


def to_low(values):
    return values.astype(jnp.bfloat16)


def matmul(left_op, right_op):
    return jnp.dot(left_op, right_op, preferred_element_type=jnp.float32)


def matmul_t(left_op, right_op):
    return lax.dot_general(
        left_op,
        right_op,
        (((left_op.ndim - 1,), (1,)), ((), ())),
        preferred_element_type=jnp.float32,
    )


def outer_sum(left_op, right_op):
    left_flat = left_op.reshape(-1, left_op.shape[-1])
    right_flat = right_op.reshape(-1, right_op.shape[-1])
    right_flat = jnp.pad(right_flat, ((0, 0), (0, -right_flat.shape[1] % LANE)))
    return lax.dot_general(
        left_flat, right_flat, (((0,), (0,)), ((), ())), preferred_element_type=jnp.float32
    )


def depth_conv(padded, kernel, row_dev, col_dev, flipped):
    kernel_f = kernel.astype(jnp.float32)
    summed = jnp.zeros(padded.shape[:1] + (row_dev, col_dev) + padded.shape[3:], jnp.float32)
    for tap_row in range(3):
        for tap_col in range(3):
            row_at = 2 - tap_row if flipped else tap_row
            col_at = 2 - tap_col if flipped else tap_col
            summed = (
                summed
                + kernel_f[tap_row * 3 + tap_col]
                * padded[:, row_at : row_at + row_dev, col_at : col_at + col_dev, :]
            )
    return summed


def shards(latents, text, time_embed, cotangent, params, moment_one, moment_two):
    lat_dev, row_dev, col_dev, width = latents.shape
    tokens_dev = row_dev * col_dev
    heads_lin = D // 32
    cross_dim = D // CROSS_HEADS
    score_scale = 1.0 / math.sqrt(cross_dim)
    text_len = text.shape[1]
    segs = lax.axis_size("seq")
    count_dp = lax.axis_size("dp")
    def spread(values):
        joined = jnp.concatenate(values, axis=-1).reshape(-1, sum(v.shape[-1] for v in values))
        whole = lax.all_gather(joined, "seq", axis=0, tiled=True)
        parts = []
        at = 0
        for value in values:
            parts.append(whole[:, at : at + value.shape[-1]])
            at += value.shape[-1]
        return parts

    def collect(values):
        blocks = jnp.stack(
            [
                jnp.concatenate(
                    [
                        value.reshape(-1, value.shape[-1])[
                            :, seg * (value.shape[-1] // segs) : (seg + 1) * (value.shape[-1] // segs)
                        ]
                        for value in values
                    ],
                    axis=1,
                )
                for seg in range(segs)
            ]
        )
        mine = lax.all_to_all(blocks, "seq", split_axis=0, concat_axis=0, tiled=True)
        mine = mine.reshape(-1, mine.shape[-1])
        parts = []
        at = 0
        for value in values:
            width = value.shape[-1] // segs
            parts.append(mine[:, at : at + width])
            at += width
        return parts

    params_rows = params.reshape(-1, LANE)
    shard_low = round_rows(params_rows)
    (
        mod_table,
        w_qkv,
        w_attn_out,
        b_attn_out,
        w_cross_q,
        w_cross_kv,
        w_cross_out,
        b_cross_out,
        w_in,
        b_in,
        w_depth,
        b_depth,
        w_point,
        b_point,
    ) = gather_weights(shard_low, segs)
    modulation = mod_table.astype(jnp.float32)[None] + time_embed.reshape(lat_dev, 6, D)
    shift_one = modulation[:, 0][:, None, :]
    scale_one = modulation[:, 1][:, None, :]
    gate_one = modulation[:, 2][:, None, :]
    shift_two = modulation[:, 3][:, None, :]
    scale_two = modulation[:, 4][:, None, :]
    gate_two = modulation[:, 5][:, None, :]
    tokens = latents.reshape(lat_dev, tokens_dev, D).astype(jnp.float32)
    normed_one, inverse_one = norm_parts(tokens)
    hidden_one = to_low(normed_one * (1.0 + scale_one) + shift_one)
    projected = matmul(hidden_one, w_qkv)
    query_pre = projected[..., :D]
    key_pre = projected[..., D : 2 * D]
    queries = to_low(jnp.maximum(query_pre, 0.0)).reshape(lat_dev, tokens_dev, heads_lin, 32)
    keys_lin = to_low(jnp.maximum(key_pre, 0.0)).reshape(lat_dev, tokens_dev, heads_lin, 32)
    values_lin = to_low(projected[..., 2 * D :]).reshape(lat_dev, tokens_dev, heads_lin, 32)
    state_part = jnp.einsum(
        "lrhd,lrhe->lhde", keys_lin, values_lin, preferred_element_type=jnp.float32
    )
    sum_part = jnp.sum(keys_lin, axis=1, dtype=jnp.float32)
    kv_state, key_sum = state_sum(state_part, sum_part, jnp.float32, 2)
    query_f = queries.astype(jnp.float32)
    numerator = jnp.einsum("lrhd,lhde->lrhe", query_f, kv_state, precision=precise)
    denominator = jnp.einsum("lrhd,lhd->lrh", query_f, key_sum, precision=precise) + eps_linear
    attn_val = numerator / denominator[..., None]
    attended = to_low(attn_val.reshape(lat_dev, tokens_dev, D))
    branch_one = matmul(attended, w_attn_out) + b_attn_out.astype(jnp.float32)
    after_attn = tokens + gate_one * branch_one
    after_low, x_qkv = lax.optimization_barrier((to_low(after_attn), *spread([hidden_one])))
    query_c = to_low(matmul(after_low, w_cross_q)).reshape(
        lat_dev, tokens_dev, CROSS_HEADS, cross_dim
    )
    keyval = to_low(matmul(text, w_cross_kv))
    keys_c = keyval[..., :D].reshape(lat_dev, text_len, CROSS_HEADS, cross_dim)
    values_c = keyval[..., D:].reshape(lat_dev, text_len, CROSS_HEADS, cross_dim)
    scores = (
        jnp.einsum("lrhc,lthc->lhrt", query_c, keys_c, preferred_element_type=jnp.float32)
        * score_scale
    )
    row_peak = jnp.max(scores, axis=-1, keepdims=True)
    log_total = row_peak + jnp.log(jnp.sum(jnp.exp(scores - row_peak), axis=-1, keepdims=True))
    probs_low = to_low(jnp.exp(scores - log_total))
    cross_mixed = to_low(
        jnp.einsum(
            "lhrt,lthc->lrhc", probs_low, values_c, preferred_element_type=jnp.float32
        ).reshape(lat_dev, tokens_dev, D)
    )
    after_cross = after_attn + matmul(cross_mixed, w_cross_out) + b_cross_out.astype(jnp.float32)
    normed_two, inverse_two = norm_parts(after_cross)
    hidden_two, x_attn, x_cross_q = lax.optimization_barrier(
        (
            to_low(normed_two * (1.0 + scale_two) + shift_two),
            *spread([attended, after_low]),
        )
    )
    inner_pre = matmul(hidden_two, w_in) + b_in.astype(jnp.float32)
    active = to_low(jax.nn.silu(inner_pre)).reshape(lat_dev, row_dev, col_dev, 2 * FF)
    padded = jnp.pad(with_halo(active, (("seq", 1),), 1), ((0, 0), (0, 0), (1, 1), (0, 0)))
    conv_out = (
        depth_conv(padded, w_depth, row_dev, col_dev, False) + b_depth.astype(jnp.float32)
    ).reshape(lat_dev, tokens_dev, 2 * FF)
    up_part = conv_out[..., :FF]
    gate_part = conv_out[..., FF:]
    gated_mix = to_low(up_part * jax.nn.silu(gate_part))
    branch_two = lax.optimization_barrier(
        matmul(gated_mix, w_point) + b_point.astype(jnp.float32)
    )
    output = (after_cross + gate_two * branch_two).astype(jnp.bfloat16).reshape(latents.shape)
    grad_out = cotangent.reshape(lat_dev, tokens_dev, D).astype(jnp.float32)
    grad_gate_two = jnp.sum(grad_out * branch_two, axis=1)
    grad_branch_two = to_low(grad_out * gate_two)
    grad_branch_two, x_cross_out, x_inner = lax.optimization_barrier(
        (grad_branch_two, *spread([cross_mixed, hidden_two]))
    )
    grad_gated = matmul_t(grad_branch_two, w_point)
    grad_up = grad_gated * jax.nn.silu(gate_part)
    grad_gate = grad_gated * up_part * silu_slope(gate_part)
    grad_conv = to_low(jnp.concatenate([grad_up, grad_gate], axis=-1)).reshape(
        lat_dev, row_dev, col_dev, 2 * FF
    )
    grad_b_depth = jnp.sum(grad_conv, axis=(0, 1, 2), dtype=jnp.float32)
    tap_grads = []
    for tap_row in range(3):
        for tap_col in range(3):
            tap_grads.append(
                jnp.einsum(
                    "lrcf,lrcf->f",
                    padded[:, tap_row : tap_row + row_dev, tap_col : tap_col + col_dev],
                    grad_conv,
                    preferred_element_type=jnp.float32,
                )
            )
    grad_w_depth = jnp.stack(tap_grads)
    grad_padded = jnp.pad(with_halo(grad_conv, (("seq", 1),), 1), ((0, 0), (0, 0), (1, 1), (0, 0)))
    grad_active = depth_conv(grad_padded, w_depth, row_dev, col_dev, True).reshape(
        lat_dev, tokens_dev, 2 * FF
    )
    grad_inner = to_low(grad_active * silu_slope(inner_pre))
    grad_inner, x_point = lax.optimization_barrier((grad_inner, *spread([gated_mix])))
    grad_hidden_two = matmul_t(grad_inner, w_in)
    grad_shift_two = jnp.sum(grad_hidden_two, axis=1)
    grad_scale_two = jnp.sum(grad_hidden_two * normed_two, axis=1)
    grad_second = grad_out + norm_back(grad_hidden_two * (1.0 + scale_two), normed_two, inverse_two)
    grad_cross_out = to_low(grad_second)
    grad_mixed = to_low(matmul_t(grad_cross_out, w_cross_out)).reshape(
        lat_dev, tokens_dev, CROSS_HEADS, cross_dim
    )
    scores_again = (
        jnp.einsum("lrhc,lthc->lhrt", query_c, keys_c, preferred_element_type=jnp.float32)
        * score_scale
    )
    probs = jnp.exp(scores_again - log_total)
    grad_probs = jnp.einsum(
        "lrhc,lthc->lhrt", grad_mixed, values_c, preferred_element_type=jnp.float32
    )
    grad_values_c = jnp.einsum(
        "lhrt,lrhc->lthc", to_low(probs), grad_mixed, preferred_element_type=jnp.float32
    )
    grad_scores = to_low(probs * (grad_probs - jnp.sum(probs * grad_probs, axis=-1, keepdims=True)))
    grad_query_c = to_low(
        jnp.einsum("lhrt,lthc->lrhc", grad_scores, keys_c, preferred_element_type=jnp.float32)
        * score_scale
    ).reshape(lat_dev, tokens_dev, D)
    grad_keys_c = (
        jnp.einsum("lhrt,lrhc->lthc", grad_scores, query_c, preferred_element_type=jnp.float32)
        * score_scale
    )
    grad_keyval_part = jnp.concatenate(
        [grad_keys_c.reshape(lat_dev, text_len, D), grad_values_c.reshape(lat_dev, text_len, D)],
        axis=-1,
    )
    grad_keyval_part = grad_keyval_part.reshape(lat_dev, text_len, segs, 2 * D // segs)
    grad_keyval = to_low(
        lax.psum_scatter(
            grad_keyval_part.astype(jnp.bfloat16), "seq", scatter_dimension=2, tiled=True
        ).astype(jnp.float32)
    ).reshape(lat_dev, text_len, 2 * D // segs)
    grad_w_cross_kv = outer_sum(text, grad_keyval)
    grad_first = grad_second + matmul_t(grad_query_c, w_cross_q)
    grad_gate_one = jnp.sum(grad_first * branch_one, axis=1)
    grad_branch_one = to_low(grad_first * gate_one)
    grad_branch_one, y_inner, y_point = lax.optimization_barrier(
        (grad_branch_one, *collect([grad_inner, grad_branch_two]))
    )
    grad_attended = matmul_t(grad_branch_one, w_attn_out).reshape(
        lat_dev, tokens_dev, heads_lin, 32
    )
    grad_numer = grad_attended / denominator[..., None]
    grad_denom = -jnp.sum(grad_attended * attn_val, axis=-1) / denominator
    grad_query = (
        jnp.einsum("lrhe,lhde->lrhd", grad_numer, kv_state, precision=precise)
        + grad_denom[..., None] * key_sum[:, None]
    )
    state_grad_part = jnp.einsum("lrhd,lrhe->lhde", query_f, grad_numer, precision=precise)
    sum_grad_part = jnp.einsum("lrhd,lrh->lhd", query_f, grad_denom, precision=precise)
    state_grad, sum_grad = state_sum(state_grad_part, sum_grad_part, jnp.bfloat16, 3)
    keys_f = keys_lin.astype(jnp.float32)
    values_f = values_lin.astype(jnp.float32)
    grad_keys = (
        jnp.einsum("lrhe,lhde->lrhd", values_f, state_grad, precision=precise) + sum_grad[:, None]
    )
    grad_values = jnp.einsum("lrhd,lhde->lrhe", keys_f, state_grad, precision=precise)
    grad_projected = to_low(
        jnp.concatenate(
            [
                grad_query.reshape(lat_dev, tokens_dev, D) * (query_pre > 0.0),
                grad_keys.reshape(lat_dev, tokens_dev, D) * (key_pre > 0.0),
                grad_values.reshape(lat_dev, tokens_dev, D),
            ],
            axis=-1,
        )
    )
    grad_projected, y_cross_out, y_cross_q, y_attn = lax.optimization_barrier(
        (grad_projected, *collect([grad_cross_out, grad_query_c, grad_branch_one]))
    )
    grad_hidden_one = matmul_t(grad_projected, w_qkv)
    grad_input = grad_first + norm_back(
        grad_hidden_one * (1.0 + scale_one), normed_one, inverse_one
    )
    grad_table = jnp.sum(
        jnp.stack(
            [
                jnp.sum(grad_hidden_one, axis=1),
                jnp.sum(grad_hidden_one * normed_one, axis=1),
                grad_gate_one,
                grad_shift_two,
                grad_scale_two,
                grad_gate_two,
            ],
            axis=1,
        ),
        axis=0,
    )
    grad_table = lax.optimization_barrier(grad_table)
    col_d = D // segs
    col_ff = 2 * FF // segs
    small_parts = jnp.concatenate(
        [
            grad_table.reshape(6, segs, col_d).transpose(1, 0, 2).reshape(segs, -1),
            grad_w_depth.reshape(9, segs, col_ff).transpose(1, 0, 2).reshape(segs, -1),
            grad_b_depth.reshape(segs, col_ff),
        ],
        axis=1,
    ).astype(jnp.bfloat16)
    small_parts = small_parts.reshape(segs, -1, LANE)
    small_mine = (
        lax.psum_scatter(small_parts, "seq", scatter_dimension=0, tiled=True)
        .astype(jnp.float32)
        .reshape(-1)
    )
    table_q = small_mine[: 6 * col_d].reshape(6, col_d)
    depth_q = small_mine[6 * col_d : 6 * col_d + 9 * col_ff].reshape(9, col_ff)
    depth_bias_q = small_mine[6 * col_d + 9 * col_ff :].reshape(1, col_ff)

    (y_qkv,) = collect([grad_projected])
    grad_w_qkv = outer_sum(x_qkv, y_qkv)
    grad_w_attn_out = outer_sum(x_attn, y_attn)
    grad_w_cross_q = outer_sum(x_cross_q, y_cross_q)
    grad_w_cross_out = outer_sum(x_cross_out, y_cross_out)
    grad_w_in = outer_sum(x_inner, y_inner)
    grad_w_point = outer_sum(x_point, y_point)
    grad_b_attn_out = jnp.sum(y_attn, axis=0, dtype=jnp.float32)
    grad_b_cross_out = jnp.sum(y_cross_out, axis=0, dtype=jnp.float32)
    grad_b_in = jnp.sum(y_inner, axis=0, dtype=jnp.float32)
    grad_b_point = jnp.sum(y_point, axis=0, dtype=jnp.float32)
    bias_part = jnp.concatenate(
        [grad_b_attn_out, grad_b_cross_out, grad_b_in, depth_bias_q.ravel(), grad_b_point]
    )
    len_bias = bias_part.size
    bias_rows = -(-bias_part.size // (8 * LANE)) * 8
    bias_part = jnp.pad(bias_part, (0, bias_rows * LANE - bias_part.size)).reshape(-1, LANE)
    quarter_grad = write_flat(
        segs,
        [
            table_q,
            grad_w_qkv,
            grad_w_attn_out,
            grad_b_attn_out,
            grad_w_cross_q,
            grad_w_cross_kv,
            grad_w_cross_out,
            grad_b_cross_out,
            grad_w_in,
            grad_b_in,
            depth_q,
            depth_bias_q,
            grad_w_point,
            grad_b_point,
        ],
    )
    if count_dp == 8 and quarter_grad.shape[0] % (8 * 560) == 0:
        grad_shard = reduce_shard(quarter_grad)
    else:
        grad_shard = lax.psum_scatter(
            quarter_grad.reshape(count_dp, -1, LANE), "dp", scatter_dimension=0, tiled=True
        )
        grad_shard = grad_shard.reshape(-1, LANE).astype(jnp.float32)
    factor, bias_grads = scale_of(grad_shard, bias_part)
    flat_outs = adam(
        factor,
        grad_shard,
        params_rows,
        moment_one.reshape(-1, LANE),
        moment_two.reshape(-1, LANE),
    )
    gradient, moment_one_new, moment_two_new, update = [
        value.reshape(params.shape) for value in flat_outs
    ]
    return (
        output,
        grad_input.reshape(latents.shape),
        gradient,
        moment_one_new,
        moment_two_new,
        update,
        bias_grads.reshape(1, -1)[:, :len_bias],
    )


def solution(mesh):
    return jax.shard_map(
        shards,
        mesh=mesh,
        in_specs=(
            P("dp", "seq", None, None),
            P("dp", None, None),
            P("dp", None),
            P("dp", "seq", None, None),
            P("seq", "dp"),
            P("seq", "dp"),
            P("seq", "dp"),
        ),
        out_specs=(
            P("dp", "seq", None, None),
            P("dp", "seq", None, None),
            P("seq", "dp"),
            P("seq", "dp"),
            P("seq", "dp"),
            P("seq", "dp"),
            P("seq", None),
        ),
        check_vma=False,
    )
```
